32 devices in a mesh: tm: 8 (over z, y), head: 4 (over x, core).
Axes of the slice: x: 2, y: 2, z: 4, core: 2. Of those that a mesh axis runs over, the one named last changes fastest.
Arguments:
- inputs: bfloat16 [1024, 4, 1024], P('tm'), may hold values from -6 to 6
- qkv_master: float32 [2, 1024, 3, 1024], P(None, 'tm', None, 'head'), may hold values from -0.1875 to 0.1875
- out_master: float32 [2, 1024, 1024], P(None, 'head', 'tm'), may hold values from -2.5 to 2.5
- up_master: float32 [2, 1024, 4096], P(None, 'tm', 'head'), may hold values from -0.1875 to 0.1875
- down_master: float32 [2, 4096, 1024], P(None, 'head', 'tm'), may hold values from -0.09375 to 0.09375
- norm_gain: float32 [2, 2, 1024], P(None, None, 'tm'), may hold values from 0.5 to 1.5
- norm_bias: float32 [2, 2, 1024], P(None, None, 'tm'), may hold values from -3 to 3
- frame_ids: int32 [1024, 4], P('tm'), may hold values from 0 to 4, as said below
- patch_pos: int32 [2, 1024, 4], P(None, 'tm'), may hold values from 0 to 23
- cotangent: bfloat16 [1024, 4, 1024], P('tm'), may hold values from -6 to 6
Outputs:
- outputs: bfloat16 [1024, 4, 1024], P('tm')
- input_grad: float32 [1024, 4, 1024], P('tm')
- qkv_grad: float32 [2, 1024, 3, 1024], P(None, 'tm', None, 'head')
- out_grad: float32 [2, 1024, 1024], P(None, 'head', 'tm')
- up_grad: float32 [2, 1024, 4096], P(None, 'tm', 'head')
- down_grad: float32 [2, 4096, 1024], P(None, 'head', 'tm')
- gain_grad: float32 [2, 2, 1024], P(None, None, 'tm')
- bias_grad: float32 [2, 2, 1024], P(None, None, 'tm')
The draws below stay inside these ranges and needn't reach their ends.
Inputs may be any that keep to these rules, and one draw needn't show every extreme that they name: `frame_ids`: in each sequence the frame id of position t is (t + c) // L, where L is 258 or 578 for the whole sequence and 0 <= c < L; sequences of one resolution stand side by side, both resolutions occur, and some sequence of the lower resolution has c = 257.
All inputs are finite; a program needn't handle non-finite values.
Results may differ from the reference program's by a relative error of at most 0.025.
Values may be sent and summed in bfloat16 or wider, within the bound.
No kernel may reach another device: no remote copies, remote signals or barrier semaphores. Data moves between devices by JAX's collectives and lax.ppermute only.
A program may use at most 256 MiB of HBM per device.

```python
import math
import jax
import jax.numpy as jnp
from jax import lax

D = 1024
HEADS = 16
HEAD_DIM = 64
FF = 4096
LAYERS = 2
MICRO = 4
FRAME_SMALL = 258
FRAME_LARGE = 578
TOKENS = 1024


def draw_frame_ids(key, part):
    coin = jax.random.randint(jax.random.fold_in(key, 11), (), 0, 2)
    sequence = jnp.arange(MICRO, dtype=jnp.int32)
    first_half = sequence < MICRO // 2
    is_small = jnp.where(coin == 0, first_half, jnp.logical_not(first_half))
    frame_len = jnp.where(is_small, FRAME_SMALL, FRAME_LARGE).astype(jnp.int32)
    offsets = jax.random.randint(jax.random.fold_in(key, 12), (MICRO,), 0, FRAME_LARGE) % frame_len
    first_small = jnp.where(coin == 0, 0, MICRO // 2).astype(jnp.int32)
    offsets = jnp.where(sequence == first_small, FRAME_SMALL - 1, offsets).astype(jnp.int32)
    places = jnp.arange(TOKENS, dtype=jnp.int32)[:, None]
    frame_table = (places + offsets[None, :]) // frame_len[None, :]
    return frame_table.astype(jnp.int32)


def set_ends(values, own_key, low, top_value):
    longest = values.shape.index(max(values.shape))
    spots = []
    for shift in (0, 1):
        where = [jax.random.randint(jax.random.fold_in(own_key, axis), (), 0, length) for axis, length in enumerate(values.shape)]
        where[longest] = (where[longest] + shift) % values.shape[longest]
        spots.append(tuple(where))
    return values.at[spots[0]].set(low).at[spots[1]].set(top_value)


def steps_of(own_key, extent, shards, smallest, largest):
    def one(dim, parts):
        heights = jax.random.uniform(jax.random.fold_in(jax.random.fold_in(own_key, 6), dim), (parts,), jnp.float32, smallest / len(shards), largest / len(shards))
        return jnp.repeat(jnp.exp(heights), extent[dim] // parts).reshape((-1,) + (1,) * (len(extent) - dim - 1))

    loudness = one(*shards[0])
    for cut in shards[1:]:
        loudness = loudness * one(*cut)
    return loudness


def scatter_about(own_key, dims, scale, bound, pieces=(), kind=jnp.bfloat16):
    values = jax.random.normal(own_key, dims, jnp.float32) * scale
    if len(pieces) > 0:
        values = steps_of(own_key, dims, pieces, -0.22, 0.18) * values
    return jnp.clip(values, min=-bound, max=bound).astype(kind)


def setup_inputs(seed: int = 0) -> dict:
    key_list = jax.random.split(jax.random.key(seed), 11)
    inputs = scatter_about(key_list[0], (TOKENS, MICRO, D), 1.0, 6.0, ((0, 8),))
    qkv_master = scatter_about(key_list[1], (LAYERS, D, 3, D), D ** -0.5, 0.1875, ((1, 8), (3, 4)), jnp.float32)
    out_master = scatter_about(key_list[2], (LAYERS, D, D), (D * 4 // TOKENS + 1) ** -0.5, 2.5, ((1, 4), (2, 8)), jnp.float32)
    up_master = scatter_about(key_list[3], (LAYERS, D, FF), D ** -0.5, 0.1875, ((1, 8), (2, 4)), jnp.float32)
    down_master = scatter_about(key_list[4], (LAYERS, FF, D), FF ** -0.5, 0.09375, ((1, 4), (2, 8)), jnp.float32)
    norm_gain = jnp.clip(1.0 + 0.1 * jax.random.normal(key_list[5], (LAYERS, 2, D), jnp.float32), 0.5, 1.5)
    norm_bias = scatter_about(key_list[6], (LAYERS, 2, D), 0.3, 3.0, ((2, 8),), jnp.float32)
    frame_ids = draw_frame_ids(jax.random.fold_in(key_list[10], 71), 0)
    patch_pos = set_ends(jax.random.randint(key_list[8], (2, TOKENS, MICRO), 0, 24), jax.random.fold_in(key_list[8], 1), 0, 23).astype(jnp.int32)
    cotangent = scatter_about(key_list[9], (TOKENS, MICRO, D), 1.0, 6.0, ((0, 8),))
    return dict(inputs=inputs, qkv_master=qkv_master, out_master=out_master, up_master=up_master, down_master=down_master, norm_gain=norm_gain, norm_bias=norm_bias, frame_ids=frame_ids, patch_pos=patch_pos, cotangent=cotangent)


@jax.custom_vjp
def low(v):
    return lax.optimization_barrier(v.astype(jnp.bfloat16)).astype(jnp.float32)

@jax.custom_vjp
def low_back(v):
    return v

def low_keep(v):
    return (low(v), None)

def low_pass(kept, grad):
    return (grad,)

def back_keep(v):
    return (v, None)

def back_low(kept, grad):
    return (low(grad),)
low.defvjp(low_keep, low_pass)
low_back.defvjp(back_keep, back_low)
highest = lax.Precision.HIGHEST
NEG_BIG = -1e+30

def tables(frame_ids, patch_pos, half_width):
    inverse = 10000.0 ** (-jnp.arange(half_width, dtype=jnp.float32) / half_width)
    coordinates = jnp.stack([frame_ids.astype(jnp.float32), patch_pos[0].astype(jnp.float32), patch_pos[1].astype(jnp.float32)], axis=-1)
    angles = coordinates[..., None] * inverse
    return (jnp.cos(angles), jnp.sin(angles))

def rotate(values, cosine, sine_table):
    half_width = values.shape[-1] // 6
    leading = values.shape[:-1]
    turned = values[..., :6 * half_width].reshape(leading + (3, 2, half_width))
    first_half = turned[..., 0, :]
    second_half = turned[..., 1, :]
    cos_part = cosine[:, :, None]
    sin_part = sine_table[:, :, None]
    new_first = first_half * cos_part - second_half * sin_part
    new_second = first_half * sin_part + second_half * cos_part
    joined = jnp.stack([new_first, new_second], axis=-2).reshape(leading + (6 * half_width,))
    return jnp.concatenate([joined, values[..., 6 * half_width:]], axis=-1)

def layer_norm(hidden, gain_row, bias_row):
    centered = hidden - lax.optimization_barrier(jnp.mean(hidden, axis=-1, keepdims=True))
    inverse_root = lax.rsqrt(lax.optimization_barrier(jnp.mean(centered * centered, axis=-1, keepdims=True)) + 1e-06)
    return centered * inverse_root * low(gain_row) + low(bias_row)

def attention(queries, key_vecs, values, frame_ids):
    total_rows, micro_count, head_count, head_width = queries.shape
    block_rows = math.gcd(total_rows, 512)
    block_count = total_rows // block_rows
    query_blocks = queries.reshape(block_count, block_rows, micro_count, head_count, head_width)
    frame_blocks = frame_ids.reshape(block_count, block_rows, micro_count)
    key_frames = frame_ids.T

    def one_block(pair_in):
        query_block, query_frames = pair_in
        scores = low_back(jnp.einsum('qbhd,kbhd->bhqk', query_block, key_vecs, precision=highest) * head_width ** (-0.5))
        allowed = key_frames[:, None, :] <= query_frames.T[:, :, None]
        scores = jnp.where(allowed[:, None], scores, NEG_BIG)
        row_max = lax.optimization_barrier(jnp.max(scores, axis=-1, keepdims=True))
        raised = jnp.exp(scores - row_max)
        weights = low(raised / lax.optimization_barrier(jnp.sum(raised, axis=-1, keepdims=True)))
        return jnp.einsum('bhqk,kbhd->qbhd', weights, values, precision=highest)
    result = lax.map(jax.checkpoint(one_block), (query_blocks, frame_blocks))
    return result.reshape(total_rows, micro_count, head_count, head_width)

def apply_block(hidden, weight_set, frame_ids, cosine, sine_table):
    qkv_w, out_w, up_w, down_w, gain_rows, bias_rows = weight_set
    total_rows, micro_count, model_width = hidden.shape
    normed = low(layer_norm(hidden, gain_rows[0], bias_rows[0]))
    projected = low_back(jnp.einsum('tbd,dkc->tbkc', normed, low(qkv_w), precision=highest))
    shaped = projected.reshape(total_rows, micro_count, 3, HEADS, HEAD_DIM)
    queries = low(rotate(shaped[:, :, 0], cosine, sine_table))
    key_vecs = low(rotate(shaped[:, :, 1], cosine, sine_table))
    values = low(shaped[:, :, 2])
    mixed_out = attention(queries, key_vecs, values, frame_ids).reshape(total_rows, micro_count, model_width)
    mixed_out = low(low_back(mixed_out))
    middle = hidden + low_back(jnp.einsum('tbc,cd->tbd', mixed_out, low(out_w), precision=highest))
    normed_two = low(layer_norm(middle, gain_rows[1], bias_rows[1]))
    upward = low_back(jnp.einsum('tbd,df->tbf', normed_two, low(up_w), precision=highest))
    activated = low(jax.nn.gelu(upward, approximate=False))
    return middle + low_back(jnp.einsum('tbf,fd->tbd', activated, low(down_w), precision=highest))

def reference(inputs, qkv_master, out_master, up_master, down_master, norm_gain, norm_bias, frame_ids, patch_pos, cotangent):
    cosine, sine_table = tables(frame_ids, patch_pos, HEAD_DIM // 6)

    def forward(hidden, qkv_all, out_all, up_all, down_all, gain_all, bias_all):
        for layer_index in range(LAYERS):
            weight_set = (qkv_all[layer_index], out_all[layer_index], up_all[layer_index], down_all[layer_index], gain_all[layer_index], bias_all[layer_index])
            hidden = apply_block(hidden, weight_set, frame_ids, cosine, sine_table)
        return hidden
    result, pullback = jax.vjp(forward, inputs.astype(jnp.float32), qkv_master, out_master, up_master, down_master, norm_gain, norm_bias)
    gradients = pullback(cotangent.astype(jnp.float32))
    return (result.astype(jnp.bfloat16), gradients[0], gradients[1], gradients[2], gradients[3], gradients[4], gradients[5], gradients[6])
```

```python
import functools

import jax
import jax.numpy as jnp
from jax import lax
from jax.experimental import pallas as pl
from jax.experimental.pallas import tpu as pltpu
from jax.sharding import PartitionSpec as P

HEAD_DIM = 64
PAIR = 2 * HEAD_DIM
GROUP = HEAD_DIM // 6
NEG_BIG = -1e30
F32 = jnp.float32
BF16 = jnp.bfloat16
NT = (((1,), (1,)), ((), ()))
TN = (((0,), (0,)), ((), ()))
NN = (((1,), (0,)), ((), ()))


def dot(left, right, dims):
    return lax.dot_general(left, right, dims, preferred_element_type=F32)


def rotary_tables(coordinates):
    lane = jnp.arange(PAIR, dtype=jnp.int32) % HEAD_DIM
    group = jnp.minimum(lane // (2 * GROUP), 2)
    place = lane % (2 * GROUP)
    turned = lane < 6 * GROUP
    first = turned & (place < GROUP)
    second = turned & (place >= GROUP)
    inverse = 10000.0 ** (-(place % GROUP).astype(F32) / GROUP)
    spread = jnp.where(
        group == 0,
        coordinates[:, 0:1],
        jnp.where(group == 1, coordinates[:, 1:2], coordinates[:, 2:3]),
    )
    angles = spread * inverse
    cosine = jnp.where(turned, jnp.cos(angles), 1.0)
    sine = jnp.sin(angles)
    return (cosine, jnp.where(first, -sine, 0.0), jnp.where(second, sine, 0.0))


def turn(values, cosine, sine_first, sine_second):
    ahead = pltpu.roll(values, PAIR - GROUP, 1)
    behind = pltpu.roll(values, GROUP, 1)
    return values * cosine + ahead * sine_first + behind * sine_second


def turn_back(values, cosine, sine_first, sine_second):
    ahead = pltpu.roll(values, PAIR - GROUP, 1)
    behind = pltpu.roll(values, GROUP, 1)
    return values * cosine - ahead * sine_first - behind * sine_second


def project_kernel(acts, weights, cosine, sine_first, sine_second, out):
    rows = out.shape[2]
    width = out.shape[1] * PAIR
    for step in range(acts.shape[0] // (2 * rows)):
        span = pl.ds(step * 2 * rows, 2 * rows)
        raw = dot(acts[span, :], weights[:, : 3 * width], NN)
        tables = (cosine[span, :], sine_first[span, :], sine_second[span, :])
        for pair in range(out.shape[1]):
            for part in range(3):
                start = part * width + pair * PAIR
                piece = raw[:, start : start + PAIR]
                if part < 2:
                    piece = turn(piece, *tables)
                piece = piece.astype(BF16)
                for half in range(2):
                    out[2 * step + half, pair, :, part * PAIR : (part + 1) * PAIR] = piece[
                        half * rows : (half + 1) * rows
                    ]


def lane_mask(shape, head):
    lane = lax.broadcasted_iota(jnp.int32, shape, 1)
    return (lane >= head * HEAD_DIM) & (lane < (head + 1) * HEAD_DIM)


def visible_bias(key_frames, query_frames, block):
    spread = jnp.concatenate([key_frames] * (block // key_frames.shape[1]), axis=1)
    return spread <= query_frames


def attend_kernel(block, start, qkv, key_frames, query_frames, out, out_t, lse):
    key_vecs = qkv[:, PAIR : 2 * PAIR]
    value_t = jnp.transpose(qkv[:, 2 * PAIR :].astype(F32)).astype(BF16)
    query_rows = out.shape[0]

    def one(step, carry):
        place = pl.multiple_of(step * block, block)
        source = pl.multiple_of(start[0] + step * block, block)
        queries = qkv[pl.ds(source, block), :PAIR] * jnp.asarray(HEAD_DIM**-0.5, BF16)
        seen = visible_bias(key_frames[...], query_frames[:, pl.ds(source, block)], block)
        pieces = []
        for head in range(2):
            mine = jnp.where(lane_mask(queries.shape, head), queries, jnp.zeros_like(queries))
            scores = jnp.where(seen, dot(key_vecs, mine, NT), NEG_BIG)
            top = jnp.max(scores, axis=0, keepdims=True)
            raised = jnp.exp(scores - top)
            total = jnp.sum(raised, axis=0, keepdims=True)
            summed = dot(
                value_t[head * HEAD_DIM : (head + 1) * HEAD_DIM], raised.astype(BF16), NN
            )
            pieces.append(summed / total)
            lse[head : head + 1, pl.ds(place, block)] = top + jnp.log(total)
        both = jnp.concatenate(pieces, axis=0)
        out_t[:, pl.ds(place, block)] = both
        out[pl.ds(place, block), :] = jnp.transpose(both).astype(BF16)
        return carry

    lax.fori_loop(0, query_rows // block, one, 0)


def attend_back_kernel(
    block,
    start,
    qkv,
    grad_out,
    out_t,
    lse,
    key_frames,
    query_frames,
    cosine,
    sine_first,
    sine_second,
    result,
    key_sum,
    value_sum,
):
    key_vecs = qkv[:, PAIR : 2 * PAIR]
    value_vecs = qkv[:, 2 * PAIR :]
    key_t = jnp.transpose(key_vecs.astype(F32)).astype(BF16)
    query_rows = grad_out.shape[0]
    key_sum[...] = jnp.zeros_like(key_sum)
    value_sum[...] = jnp.zeros_like(value_sum)
    if query_rows != qkv.shape[0]:
        result[:, :PAIR] = jnp.zeros((qkv.shape[0], PAIR), BF16)

    def one(step, carry):
        place = pl.multiple_of(step * block, block)
        source = pl.multiple_of(start[0] + step * block, block)
        queries = qkv[pl.ds(source, block), :PAIR] * jnp.asarray(HEAD_DIM**-0.5, BF16)
        upstream = grad_out[pl.ds(place, block), :]
        seen = visible_bias(key_frames[...], query_frames[:, pl.ds(source, block)], block)
        both = out_t[:, pl.ds(place, block)] * jnp.transpose(upstream.astype(F32))
        pieces = []
        for head in range(2):
            keep = lane_mask(queries.shape, head)
            mine = jnp.where(keep, queries, jnp.zeros_like(queries))
            above = jnp.where(keep, upstream, jnp.zeros_like(upstream))
            rows = slice(head * HEAD_DIM, (head + 1) * HEAD_DIM)
            delta = jnp.sum(both[rows], axis=0, keepdims=True)
            log_total = lse[head : head + 1, pl.ds(place, block)]
            weights = jnp.where(seen, jnp.exp(dot(key_vecs, mine, NT) - log_total), 0.0)
            slope = (weights * (dot(value_vecs, above, NT) - delta)).astype(BF16)
            value_sum[...] += dot(weights.astype(BF16), above, NN)
            key_sum[...] += dot(slope, mine, NN)
            pieces.append(dot(key_t[rows], slope, NN))
        query_grad = jnp.transpose(jnp.concatenate(pieces, axis=0)) * HEAD_DIM**-0.5
        span = pl.ds(source, block)
        result[span, :PAIR] = turn_back(
            query_grad, cosine[span, :], sine_first[span, :], sine_second[span, :]
        ).astype(BF16)
        return carry

    lax.fori_loop(0, query_rows // block, one, 0)
    result[:, PAIR : 2 * PAIR] = turn_back(
        key_sum[...], cosine[...], sine_first[...], sine_second[...]
    ).astype(BF16)
    result[:, 2 * PAIR :] = value_sum[...].astype(BF16)


def whole():
    return pl.BlockSpec(memory_space=pltpu.VMEM)


def scalars():
    return pl.BlockSpec(memory_space=pltpu.SMEM)


PARAMS = pltpu.CompilerParams(vmem_limit_bytes=56 * 1024 * 1024)


def project(acts, weights, tables, rows):
    pairs = 2
    return pl.pallas_call(
        project_kernel,
        out_shape=jax.ShapeDtypeStruct((acts.shape[0] // rows, pairs, rows, 3 * PAIR), BF16),
        in_specs=[whole()] * 5,
        out_specs=whole(),
        compiler_params=PARAMS,
        name="project",
    )(acts, weights, *tables)


def attend(start, qkv, key_frames, query_frames, query_rows):
    return pl.pallas_call(
        functools.partial(attend_kernel, 256),
        out_shape=(
            jax.ShapeDtypeStruct((query_rows, PAIR), BF16),
            jax.ShapeDtypeStruct((PAIR, query_rows), F32),
            jax.ShapeDtypeStruct((2, query_rows), F32),
        ),
        in_specs=[scalars()] + [whole()] * 3,
        out_specs=(whole(),) * 3,
        compiler_params=PARAMS,
        name="attend",
    )(start, qkv, key_frames, query_frames)


def attend_back(start, qkv, grad_out, out_t, lse, key_frames, query_frames, tables):
    return pl.pallas_call(
        functools.partial(attend_back_kernel, 256),
        out_shape=jax.ShapeDtypeStruct(qkv.shape, BF16),
        in_specs=[scalars()] + [whole()] * 9,
        out_specs=whole(),
        scratch_shapes=[pltpu.VMEM((qkv.shape[0], PAIR), F32)] * 2,
        compiler_params=PARAMS,
        name="attend_back",
    )(start, qkv, grad_out, out_t, lse, key_frames, query_frames, *tables)


def normalize(hidden):
    centered = hidden - jnp.mean(hidden, axis=-1, keepdims=True)
    inverse_root = lax.rsqrt(jnp.mean(centered * centered, axis=-1, keepdims=True) + 1e-06)
    return (centered * inverse_root, inverse_root)


def norm_back(upstream, normed, inverse_root, gain_row):
    scaled = upstream * gain_row
    return inverse_root * (
        scaled
        - jnp.mean(scaled, axis=-1, keepdims=True)
        - normed * jnp.mean(scaled * normed, axis=-1, keepdims=True)
    )


def gelu_pair(upward):
    bell = 0.5 * (1.0 + lax.erf(upward * 0.7071067811865476))
    slope = bell + upward * jnp.exp(-0.5 * upward * upward) * 0.3989422804014327
    return ((upward * bell).astype(BF16), slope)


def body(
    inputs,
    qkv_master,
    out_master,
    up_master,
    down_master,
    norm_gain,
    norm_bias,
    frame_ids,
    patch_pos,
    cotangent,
):
    rows, micro, width = inputs.shape
    tm_size = lax.axis_size("tm")
    head_size = lax.axis_size("head")
    here = lax.axis_index("tm")
    layers = qkv_master.shape[0]
    columns = qkv_master.shape[3]
    hidden_units = up_master.shape[2]
    slices = width // tm_size
    half = micro // 2
    half_rows = half * rows
    odd = lax.axis_index("head") % 2
    pairs = columns // PAIR
    units = micro * pairs
    repeats = tm_size // units
    tokens = rows * tm_size
    query_rows = tokens // repeats

    def swap(values, bit):
        return lax.ppermute(values, "head", [(i, i ^ bit) for i in range(head_size)])

    def both_halves(mine):
        return jnp.concatenate([mine, swap(mine, 1)], axis=0)

    def sum_heads(theirs, mine):
        total = (mine + swap(theirs.astype(BF16), 1).astype(F32)).astype(BF16)
        bit = 2
        while True:
            total = lax.optimization_barrier(total)
            total = total.astype(F32) + swap(total, bit).astype(F32)
            bit *= 2
            if bit >= head_size:
                return total
            total = total.astype(BF16)

    def spread(values):
        return lax.all_to_all(values, "tm", 0, 0, tiled=True)

    ordered = (jnp.arange(micro) + half * odd) % micro
    whole_numbers = jnp.concatenate([frame_ids[None], patch_pos], axis=0).astype(F32)
    whole_numbers = jnp.take(jnp.transpose(whole_numbers, (2, 0, 1)), ordered, axis=0)
    vectors = jnp.concatenate([norm_gain, norm_bias], axis=0).astype(BF16).astype(F32)
    parcel = jnp.concatenate(
        [
            jnp.broadcast_to(vectors.reshape(1, -1), (tm_size, vectors.size)),
            jnp.repeat(whole_numbers.reshape(micro, 3 * rows), tm_size // micro, axis=0),
        ],
        axis=1,
    )
    parcel = spread(parcel)
    vectors = parcel[:, : vectors.size].reshape(tm_size, 2, layers, 2, slices)
    vectors = jnp.transpose(vectors, (1, 2, 3, 0, 4)).reshape(2, layers, 2, width)
    gains, biases = vectors[0], vectors[1]
    places = parcel[:, -3 * rows :].reshape(tm_size, 3, rows)
    places = jnp.transpose(places, (1, 0, 2)).reshape(3, tokens)
    query_frames = places[0:1]
    key_frames = jnp.broadcast_to(places[0][:, None], (tokens, 128))
    sequence_tables = rotary_tables(places.T)
    row_tables = rotary_tables(jnp.transpose(whole_numbers, (0, 2, 1)).reshape(micro * rows, 3))
    start = ((here % repeats) * query_rows).reshape(1)

    def gather(shard):
        return lax.all_gather(shard, "tm", axis=0, tiled=True)

    weights = []
    for layer in range(layers):
        attention_shard = jnp.concatenate(
            [
                qkv_master[layer].astype(BF16).reshape(slices, 3 * columns),
                out_master[layer].astype(BF16).T,
            ],
            axis=1,
        )
        dense_shard = jnp.concatenate(
            [up_master[layer].astype(BF16), down_master[layer].astype(BF16).T], axis=1
        )
        weights.append((gather(attention_shard), gather(dense_shard)))

    def own_rows(values):
        mine = lax.dynamic_slice_in_dim(values, half * odd, half, 1)
        return jnp.transpose(mine, (1, 0, 2)).reshape(half_rows, width).astype(F32)

    def to_units(values):
        return jnp.repeat(values, repeats, axis=0) if repeats > 1 else values

    def from_units(values):
        if repeats == 1:
            return values
        grouped = values.reshape((units, repeats) + values.shape[1:]).astype(F32)
        return jnp.sum(grouped, axis=1).astype(BF16)

    hidden = own_rows(inputs)
    stored = []
    for layer in range(layers):
        attention_w, dense_w = weights[layer]
        out_w = attention_w[:, 3 * columns :]
        up_w = dense_w[:, :hidden_units]
        down_w = dense_w[:, hidden_units:]
        normed_one, root_one = normalize(hidden)
        first_in = both_halves(
            (normed_one * gains[layer, 0] + biases[layer, 0]).astype(BF16)
        )
        packed = project(first_in, attention_w, row_tables, rows)
        packed = to_units(packed.reshape(units, rows, 3 * PAIR))
        qkv = spread(packed).reshape(tokens, 3 * PAIR)
        mixed, mixed_t, lse = attend(start, qkv, key_frames, query_frames, query_rows)
        if repeats > 1:
            mixed = lax.dynamic_update_slice_in_dim(
                jnp.zeros((tokens, PAIR), BF16), mixed, start[0], 0
            )
        mixed = from_units(spread(mixed.reshape(tm_size, rows, PAIR)))
        mixed = jnp.transpose(mixed.reshape(micro, pairs, rows, PAIR), (0, 2, 1, 3)).reshape(
            micro * rows, columns
        )
        middle = hidden + sum_heads(
            dot(mixed[half_rows:], out_w, NT), dot(mixed[:half_rows], out_w, NT)
        )
        normed_two, root_two = normalize(middle)
        second_in = both_halves(
            (normed_two * gains[layer, 1] + biases[layer, 1]).astype(BF16)
        )
        activated, slope = gelu_pair(dot(second_in, up_w, NN))
        hidden = middle + sum_heads(
            dot(activated[half_rows:], down_w, NT), dot(activated[:half_rows], down_w, NT)
        )
        stored.append(
            (
                normed_one,
                root_one,
                first_in,
                qkv,
                mixed,
                mixed_t,
                lse,
                normed_two,
                root_two,
                second_in,
                activated,
                slope,
            )
        )

    def all_rows(mine):
        ours = both_halves(mine).reshape(micro, rows, width)
        return jnp.roll(ours, half * odd, axis=0)

    outputs = jnp.transpose(all_rows(hidden.astype(BF16)), (1, 0, 2))
    upstream = own_rows(cotangent)
    qkv_grads, out_grads, up_grads, down_grads, gain_sums, bias_sums = [], [], [], [], [], []
    for layer in reversed(range(layers)):
        attention_w, dense_w = weights[layer]
        qkv_w = attention_w[:, : 3 * columns]
        out_w = attention_w[:, 3 * columns :]
        up_w = dense_w[:, :hidden_units]
        down_w = dense_w[:, hidden_units:]
        (
            normed_one,
            root_one,
            first_in,
            qkv,
            mixed,
            mixed_t,
            lse,
            normed_two,
            root_two,
            second_in,
            activated,
            slope,
        ) = stored[layer]
        grad_mlp = both_halves(upstream.astype(BF16))
        up_in_grad = (dot(grad_mlp, down_w, NN) * slope).astype(BF16)
        second_grad = sum_heads(
            dot(up_in_grad[half_rows:], up_w, NT), dot(up_in_grad[:half_rows], up_w, NT)
        )
        dense_grad = jnp.concatenate(
            [
                dot(second_in, up_in_grad, TN).astype(BF16),
                dot(grad_mlp, activated, TN).astype(BF16),
            ],
            axis=1,
        )
        dense_grad = lax.psum_scatter(dense_grad, "tm", scatter_dimension=0, tiled=True)
        gain_two = jnp.sum(second_grad * normed_two, axis=0)
        bias_two = jnp.sum(second_grad, axis=0)
        upstream = upstream + norm_back(second_grad, normed_two, root_two, gains[layer, 1])
        grad_attn = both_halves(upstream.astype(BF16))
        grad_mixed = dot(grad_attn, out_w, NN).astype(BF16)
        grad_mixed = jnp.transpose(
            grad_mixed.reshape(micro, rows, pairs, PAIR), (0, 2, 1, 3)
        ).reshape(units, rows, PAIR)
        grad_mixed = spread(to_units(grad_mixed)).reshape(tokens, PAIR)
        if repeats > 1:
            grad_mixed = lax.dynamic_slice_in_dim(grad_mixed, start[0], query_rows, 0)
        packed_grad = attend_back(
            start, qkv, grad_mixed, mixed_t, lse, key_frames, query_frames, sequence_tables
        )
        packed_grad = from_units(spread(packed_grad.reshape(tm_size, rows, 3 * PAIR)))
        combined = jnp.transpose(
            packed_grad.reshape(micro, pairs, rows, 3, PAIR), (0, 2, 3, 1, 4)
        ).reshape(micro * rows, 3 * columns)
        first_grad = sum_heads(
            dot(combined[half_rows:], qkv_w, NT), dot(combined[:half_rows], qkv_w, NT)
        )
        attention_grad = jnp.concatenate(
            [
                dot(first_in, combined, TN).astype(BF16),
                dot(grad_attn, mixed, TN).astype(BF16),
            ],
            axis=1,
        )
        attention_grad = lax.psum_scatter(attention_grad, "tm", scatter_dimension=0, tiled=True)
        gain_one = jnp.sum(first_grad * normed_one, axis=0)
        bias_one = jnp.sum(first_grad, axis=0)
        upstream = upstream + norm_back(first_grad, normed_one, root_one, gains[layer, 0])
        qkv_grads.append(
            attention_grad[:, : 3 * columns].astype(F32).reshape(slices, 3, columns)
        )
        out_grads.append(attention_grad[:, 3 * columns :].astype(F32).T)
        up_grads.append(dense_grad[:, :hidden_units].astype(F32))
        down_grads.append(dense_grad[:, hidden_units:].astype(F32).T)
        gain_sums.append(jnp.stack([gain_one, gain_two]))
        bias_sums.append(jnp.stack([bias_one, bias_two]))
    small = jnp.stack([jnp.stack(gain_sums[::-1]), jnp.stack(bias_sums[::-1])])
    small = small + swap(small, 1)
    small = small.reshape(4 * layers, tm_size, slices).transpose(1, 0, 2)
    small = jnp.sum(spread(small), axis=0).reshape(2, layers, 2, slices)
    return (
        outputs,
        jnp.transpose(all_rows(upstream), (1, 0, 2)),
        jnp.stack(qkv_grads[::-1]),
        jnp.stack(out_grads[::-1]),
        jnp.stack(up_grads[::-1]),
        jnp.stack(down_grads[::-1]),
        small[0],
        small[1],
    )


def solution(mesh):
    placed = (
        P("tm", None, None),
        P(None, "tm", None, "head"),
        P(None, "head", "tm"),
        P(None, "tm", "head"),
        P(None, "head", "tm"),
        P(None, None, "tm"),
        P(None, None, "tm"),
        P("tm", None),
        P(None, "tm", None),
        P("tm", None, None),
    )
    return jax.shard_map(
        body,
        mesh=mesh,
        in_specs=placed,
        out_specs=(
            P("tm", None, None),
            P("tm", None, None),
            P(None, "tm", None, "head"),
            P(None, "head", "tm"),
            P(None, "tm", "head"),
            P(None, "head", "tm"),
            P(None, None, "tm"),
            P(None, None, "tm"),
        ),
        check_vma=False,
    )
```

```python
import functools

import jax
import jax.numpy as jnp
from jax import lax
from jax.experimental import pallas as pl
from jax.experimental.pallas import tpu as pltpu
from jax.sharding import PartitionSpec as P

HEAD_DIM = 64
PAIR = 2 * HEAD_DIM
GROUP = HEAD_DIM // 6
NEG_BIG = -1e30
F32 = jnp.float32
BF16 = jnp.bfloat16
NT = (((1,), (1,)), ((), ()))
TN = (((0,), (0,)), ((), ()))
NN = (((1,), (0,)), ((), ()))


def dot(left, right, dims):
    return lax.dot_general(left, right, dims, preferred_element_type=F32)


def rotary_tables(coordinates):
    lane = jnp.arange(PAIR, dtype=jnp.int32) % HEAD_DIM
    group = jnp.minimum(lane // (2 * GROUP), 2)
    place = lane % (2 * GROUP)
    turned = lane < 6 * GROUP
    first = turned & (place < GROUP)
    second = turned & (place >= GROUP)
    inverse = 10000.0 ** (-(place % GROUP).astype(F32) / GROUP)
    spread = jnp.where(
        group == 0,
        coordinates[:, 0:1],
        jnp.where(group == 1, coordinates[:, 1:2], coordinates[:, 2:3]),
    )
    angles = spread * inverse
    cosine = jnp.where(turned, jnp.cos(angles), 1.0)
    sine = jnp.sin(angles)
    return (cosine, jnp.where(first, -sine, 0.0), jnp.where(second, sine, 0.0))


def turn(values, cosine, sine_first, sine_second):
    ahead = pltpu.roll(values, PAIR - GROUP, 1)
    behind = pltpu.roll(values, GROUP, 1)
    return values * cosine + ahead * sine_first + behind * sine_second


def turn_back(values, cosine, sine_first, sine_second):
    ahead = pltpu.roll(values, PAIR - GROUP, 1)
    behind = pltpu.roll(values, GROUP, 1)
    return values * cosine - ahead * sine_first - behind * sine_second


def project_kernel(own, peer, left, right, cosine, sine_first, sine_second, out):
    rows = out.shape[2]
    width = out.shape[1] * PAIR
    middle = left.shape[0]
    for step, acts in enumerate((own, peer)):
        span = pl.ds(step * 2 * rows, 2 * rows)
        raw = dot(acts[:, :middle], left[:, : 3 * width], NN)
        raw += dot(acts[:, middle:], right[:, : 3 * width], NN)
        tables = (cosine[span, :], sine_first[span, :], sine_second[span, :])
        for pair in range(out.shape[1]):
            for part in range(3):
                start = part * width + pair * PAIR
                piece = raw[:, start : start + PAIR]
                if part < 2:
                    piece = turn(piece, *tables)
                piece = piece.astype(BF16)
                for half in range(2):
                    out[2 * step + half, pair, :, part * PAIR : (part + 1) * PAIR] = piece[
                        half * rows : (half + 1) * rows
                    ]


def unit_rows(tiles, micros, pairs, lanes):
    return jnp.concatenate(
        [
            jnp.concatenate([tiles[micro * pairs + pair, :, lanes] for pair in range(pairs)], axis=1)
            for micro in micros
        ],
        axis=0,
    )


def mix_kernel(pairs, mixed, left, right, theirs, mine):
    width = pairs * PAIR
    micro = mixed.shape[0] // pairs
    middle = left.shape[0]
    skip = left.shape[1] - width
    for micros, out in ((range(micro // 2, micro), theirs), (range(micro // 2), mine)):
        rows = unit_rows(mixed, micros, pairs, slice(0, PAIR))
        out[:, :middle] = dot(rows, left[:, skip:], NT).astype(out.dtype)
        out[:, middle:] = dot(rows, right[:, skip:], NT).astype(out.dtype)


def unmix_kernel(own, peer, left, right, out):
    rows = out.shape[2]
    width = out.shape[1] * PAIR
    middle = left.shape[0]
    skip = left.shape[1] - width
    for step, acts in enumerate((own, peer)):
        raw = dot(acts[:, :middle], left[:, skip:], NN) + dot(acts[:, middle:], right[:, skip:], NN)
        raw = raw.astype(BF16)
        for pair in range(out.shape[1]):
            for half in range(2):
                out[2 * step + half, pair] = raw[
                    half * rows : (half + 1) * rows, pair * PAIR : (pair + 1) * PAIR
                ]


def unproject_kernel(pairs, packed, left, right, theirs, mine):
    width = pairs * PAIR
    micro = packed.shape[0] // pairs
    middle = left.shape[0]
    for micros, out in ((range(micro // 2, micro), theirs), (range(micro // 2), mine)):
        for weights, place in ((left, slice(0, middle)), (right, slice(middle, 2 * middle))):
            total = 0.0
            for part in range(3):
                rows = unit_rows(packed, micros, pairs, slice(part * PAIR, (part + 1) * PAIR))
                total += dot(rows, weights[:, part * width : (part + 1) * width], NT)
            out[:, place] = total.astype(out.dtype)


def up_kernel(own, peer, left, right, activated, slope):
    middle = left.shape[0]
    half = own.shape[0]
    for step, acts in enumerate((own, peer)):
        upward = dot(acts[:, :middle], left[...], NN) + dot(acts[:, middle:], right[...], NN)
        bell = 0.5 * (1.0 + lax.erf(upward * 0.7071067811865476))
        span = slice(step * half, (step + 1) * half)
        activated[span, :] = (upward * bell).astype(BF16)
        slope[span, :] = bell + upward * jnp.exp(-0.5 * upward * upward) * 0.3989422804014327


def down_kernel(activated, left, right, theirs, mine):
    half = mine.shape[0]
    middle = left.shape[0]
    for span, out in ((slice(half, 2 * half), theirs), (slice(0, half), mine)):
        out[:, :middle] = dot(activated[span, :], left[...], NT).astype(out.dtype)
        out[:, middle:] = dot(activated[span, :], right[...], NT).astype(out.dtype)


def dense_back_kernel(own, peer, up_left, up_right, down_left, down_right, slope, inner, theirs, mine):
    half = mine.shape[0]
    middle = up_left.shape[0]
    for acts, span, out in (
        (peer, slice(half, 2 * half), theirs),
        (own, slice(0, half), mine),
    ):
        raw = dot(acts[:, :middle], down_left[...], NN)
        raw += dot(acts[:, middle:], down_right[...], NN)
        grad = (raw * slope[span, :]).astype(BF16)
        inner[span, :] = grad
        out[:, :middle] = dot(grad, up_left[...], NT).astype(out.dtype)
        out[:, middle:] = dot(grad, up_right[...], NT).astype(out.dtype)


def dense_products(own, peer, other):
    rows = jnp.concatenate([own[...], peer[...]], axis=0)
    for start in range(0, other.shape[1], 256):
        yield start, dot(rows, other[:, start : start + 256], TN)


def attention_products(pairs, first_own, first_peer, packed, grad_own, grad_peer, mixed):
    first = jnp.concatenate([first_own[...], first_peer[...]], axis=0)
    grad = jnp.concatenate([grad_own[...], grad_peer[...]], axis=0)
    width = pairs * PAIR
    micros = range(packed.shape[0] // pairs)
    for part in range(3):
        rows = unit_rows(packed, micros, pairs, slice(part * PAIR, (part + 1) * PAIR))
        yield part * width, dot(first, rows, TN)
    yield 3 * width, dot(grad, unit_rows(mixed, micros, pairs, slice(0, PAIR)), TN)


def far_kernel(products, *refs):
    out = refs[-1]
    for start, value in products(*refs[:-1]):
        out[:, start : start + value.shape[1]] = value.astype(BF16)


def near_kernel(products, *refs):
    arrived, keep, send = refs[-3:]
    half = keep.shape[0]
    for start, value in products(*refs[:-3]):
        span = slice(start, start + value.shape[1])
        value = value + arrived[:, span].astype(F32)
        keep[:, span] = value[:half]
        send[:, span] = value[half:].astype(BF16)


def lane_mask(shape, head):
    lane = lax.broadcasted_iota(jnp.int32, shape, 1)
    return (lane >= head * HEAD_DIM) & (lane < (head + 1) * HEAD_DIM)


def visible_bias(key_frames, query_frames, block):
    spread = jnp.concatenate([key_frames] * (block // key_frames.shape[1]), axis=1)
    return spread <= query_frames


def attend_kernel(block, start, qkv, key_frames, query_frames, out, out_t, lse):
    key_vecs = qkv[:, PAIR : 2 * PAIR]
    value_t = jnp.transpose(qkv[:, 2 * PAIR :].astype(F32)).astype(BF16)
    query_rows = out.shape[0]

    def one(step, carry):
        place = pl.multiple_of(step * block, block)
        source = pl.multiple_of(start[0] + step * block, block)
        queries = qkv[pl.ds(source, block), :PAIR] * jnp.asarray(HEAD_DIM**-0.5, BF16)
        seen = visible_bias(key_frames[...], query_frames[:, pl.ds(source, block)], block)
        pieces = []
        for head in range(2):
            mine = jnp.where(lane_mask(queries.shape, head), queries, jnp.zeros_like(queries))
            scores = jnp.where(seen, dot(key_vecs, mine, NT), NEG_BIG)
            top = jnp.max(scores, axis=0, keepdims=True)
            raised = jnp.exp(scores - top)
            total = jnp.sum(raised, axis=0, keepdims=True)
            summed = dot(
                value_t[head * HEAD_DIM : (head + 1) * HEAD_DIM], raised.astype(BF16), NN
            )
            pieces.append(summed / total)
            lse[head : head + 1, pl.ds(place, block)] = top + jnp.log(total)
        both = jnp.concatenate(pieces, axis=0)
        out_t[:, pl.ds(place, block)] = both
        out[pl.ds(place, block), :] = jnp.transpose(both).astype(BF16)
        return carry

    lax.fori_loop(0, query_rows // block, one, 0)


def attend_back_kernel(
    block,
    start,
    qkv,
    grad_out,
    out_t,
    lse,
    key_frames,
    query_frames,
    cosine,
    sine_first,
    sine_second,
    result,
    key_sum,
    value_sum,
):
    key_vecs = qkv[:, PAIR : 2 * PAIR]
    value_vecs = qkv[:, 2 * PAIR :]
    key_t = jnp.transpose(key_vecs.astype(F32)).astype(BF16)
    query_rows = grad_out.shape[0]
    key_sum[...] = jnp.zeros_like(key_sum)
    value_sum[...] = jnp.zeros_like(value_sum)
    if query_rows != qkv.shape[0]:
        result[:, :PAIR] = jnp.zeros((qkv.shape[0], PAIR), BF16)

    def one(step, carry):
        place = pl.multiple_of(step * block, block)
        source = pl.multiple_of(start[0] + step * block, block)
        queries = qkv[pl.ds(source, block), :PAIR] * jnp.asarray(HEAD_DIM**-0.5, BF16)
        upstream = grad_out[pl.ds(place, block), :]
        seen = visible_bias(key_frames[...], query_frames[:, pl.ds(source, block)], block)
        both = out_t[:, pl.ds(place, block)] * jnp.transpose(upstream.astype(F32))
        pieces = []
        for head in range(2):
            keep = lane_mask(queries.shape, head)
            mine = jnp.where(keep, queries, jnp.zeros_like(queries))
            above = jnp.where(keep, upstream, jnp.zeros_like(upstream))
            rows = slice(head * HEAD_DIM, (head + 1) * HEAD_DIM)
            delta = jnp.sum(both[rows], axis=0, keepdims=True)
            log_total = lse[head : head + 1, pl.ds(place, block)]
            weights = jnp.where(seen, jnp.exp(dot(key_vecs, mine, NT) - log_total), 0.0)
            slope = (weights * (dot(value_vecs, above, NT) - delta)).astype(BF16)
            value_sum[...] += dot(weights.astype(BF16), above, NN)
            key_sum[...] += dot(slope, mine, NN)
            pieces.append(dot(key_t[rows], slope, NN))
        query_grad = jnp.transpose(jnp.concatenate(pieces, axis=0)) * HEAD_DIM**-0.5
        span = pl.ds(source, block)
        result[span, :PAIR] = turn_back(
            query_grad, cosine[span, :], sine_first[span, :], sine_second[span, :]
        ).astype(BF16)
        return carry

    lax.fori_loop(0, query_rows // block, one, 0)
    result[:, PAIR : 2 * PAIR] = turn_back(
        key_sum[...], cosine[...], sine_first[...], sine_second[...]
    ).astype(BF16)
    result[:, 2 * PAIR :] = value_sum[...].astype(BF16)


def whole():
    return pl.BlockSpec(memory_space=pltpu.VMEM)


def scalars():
    return pl.BlockSpec(memory_space=pltpu.SMEM)


PARAMS = pltpu.CompilerParams(vmem_limit_bytes=24 * 1024 * 1024)


def call(kernel, outs, name, *operands, specs=None):
    shapes = [pltpu.VMEM(shape, kind) for shape, kind in outs]
    operands = [pltpu.with_memory_space_constraint(operand, pltpu.VMEM) for operand in operands]
    single = len(shapes) == 1
    return pl.pallas_call(
        kernel,
        out_shape=shapes[0] if single else shapes,
        in_specs=specs or [whole()] * len(operands),
        out_specs=whole() if single else [whole()] * len(shapes),
        compiler_params=PARAMS,
        name=name,
        grid=(1,) if specs else (),
    )(*operands)


def columns_of(array, count, index):
    return pl.BlockSpec((array.shape[0], count), lambda i: (0, index))


def up_project(own, peer, left, right, units):
    rows = 2 * own.shape[0]
    block = 256
    fixed = pl.BlockSpec(own.shape, lambda j: (0, 0))
    weight = pl.BlockSpec((left.shape[0], block), lambda j: (0, j))
    result = pl.BlockSpec((rows, block), lambda j: (0, j))
    return pl.pallas_call(
        up_kernel,
        grid=(units // block,),
        out_shape=(
            jax.ShapeDtypeStruct((rows, units), BF16),
            jax.ShapeDtypeStruct((rows, units), F32),
        ),
        in_specs=[fixed, fixed, weight, weight],
        out_specs=(result, result),
        compiler_params=PARAMS,
        name="up_project",
    )(own, peer, left, right)


def attend(start, qkv, key_frames, query_frames, query_rows):
    return pl.pallas_call(
        functools.partial(attend_kernel, 256),
        out_shape=(
            jax.ShapeDtypeStruct((query_rows, PAIR), BF16),
            jax.ShapeDtypeStruct((PAIR, query_rows), F32),
            jax.ShapeDtypeStruct((2, query_rows), F32),
        ),
        in_specs=[scalars()] + [whole()] * 3,
        out_specs=(whole(),) * 3,
        compiler_params=PARAMS,
        name="attend",
    )(start, qkv, key_frames, query_frames)


def attend_back(start, qkv, grad_out, out_t, lse, key_frames, query_frames, tables):
    return pl.pallas_call(
        functools.partial(attend_back_kernel, 256),
        out_shape=jax.ShapeDtypeStruct(qkv.shape, BF16),
        in_specs=[scalars()] + [whole()] * 9,
        out_specs=whole(),
        scratch_shapes=[pltpu.VMEM((qkv.shape[0], PAIR), F32)] * 2,
        compiler_params=PARAMS,
        name="attend_back",
    )(start, qkv, grad_out, out_t, lse, key_frames, query_frames, *tables)


def normalize(hidden):
    centered = hidden - jnp.mean(hidden, axis=-1, keepdims=True)
    inverse_root = lax.rsqrt(jnp.mean(centered * centered, axis=-1, keepdims=True) + 1e-06)
    return (centered * inverse_root, inverse_root)


def norm_back(upstream, normed, inverse_root, gain_row):
    scaled = upstream * gain_row
    return inverse_root * (
        scaled
        - jnp.mean(scaled, axis=-1, keepdims=True)
        - normed * jnp.mean(scaled * normed, axis=-1, keepdims=True)
    )


def body(
    inputs,
    qkv_master,
    out_master,
    up_master,
    down_master,
    norm_gain,
    norm_bias,
    frame_ids,
    patch_pos,
    cotangent,
):
    rows, micro, width = inputs.shape
    tm_size = lax.axis_size("tm")
    head_size = lax.axis_size("head")
    here = lax.axis_index("tm")
    layers = qkv_master.shape[0]
    columns = qkv_master.shape[3]
    hidden_units = up_master.shape[2]
    slices = width // tm_size
    middle_width = width // 2
    half = micro // 2
    half_rows = half * rows
    odd = lax.axis_index("head") % 2
    pairs = columns // PAIR
    units = micro * pairs
    repeats = tm_size // units
    tokens = rows * tm_size
    query_rows = tokens // repeats

    bits = []
    order = [0]
    bit = tm_size // 2
    while bit:
        bits.append(bit)
        order = order + [place | bit for place in order]
        bit //= 2
    feature = jnp.arange(width, dtype=jnp.int32)
    origin = (here ^ jnp.asarray(order, jnp.int32)[:, None]) * slices + jnp.arange(
        slices, dtype=jnp.int32
    )
    shuffle = (feature[:, None] == origin.reshape(1, width)).astype(BF16)

    def sync(*values):
        return lax.optimization_barrier(values)

    def hop(values, bit):
        return lax.ppermute(values, "tm", [(i, i ^ bit) for i in range(tm_size)])

    def swap(values, bit):
        return lax.ppermute(values, "head", [(i, i ^ bit) for i in range(head_size)])

    def sum_heads(theirs, mine):
        total = (mine + swap(theirs, 1).astype(F32)).astype(BF16)
        bit = 2
        while True:
            total = lax.optimization_barrier(total)
            total = total.astype(F32) + swap(total, bit).astype(F32)
            bit *= 2
            if bit >= head_size:
                return total
            total = total.astype(BF16)

    def spread(values):
        return lax.all_to_all(values, "tm", 0, 0, tiled=True)

    def gather_now(shard):
        pieces = [shard]
        for bit in bits[:-1]:
            pieces = pieces + [hop(piece, bit) for piece in pieces]
        others = [hop(piece, bits[-1]) for piece in pieces]
        return (jnp.concatenate(pieces, axis=0), jnp.concatenate(others, axis=0))

    def grow(held, stage):
        count = len(bits) - 1
        for bit in bits[stage : count if stage else 1]:
            held = jnp.concatenate([held, hop(held, bit)], axis=0)
        return held

    def finish(held):
        return (held, hop(held, bits[-1]))

    def fold(keep, send, stage):
        later = bits[-2::-1]
        for bit in later[stage:1] if stage == 0 else later[stage:]:
            total = keep + hop(send, bit).astype(F32)
            if bit == bits[0]:
                return total
            cut = total.shape[0] // 2
            keep, send = total[:cut], total[cut:].astype(BF16)
        return keep, send

    ordered = (jnp.arange(micro) + half * odd) % micro
    whole_numbers = jnp.concatenate([frame_ids[None], patch_pos], axis=0).astype(F32)
    whole_numbers = jnp.take(jnp.transpose(whole_numbers, (2, 0, 1)), ordered, axis=0)
    vectors = jnp.concatenate([norm_gain, norm_bias], axis=0).astype(BF16).astype(F32)
    parcel = jnp.concatenate(
        [
            jnp.broadcast_to(vectors.reshape(1, -1), (tm_size, vectors.size)),
            jnp.repeat(whole_numbers.reshape(micro, 3 * rows), tm_size // micro, axis=0),
        ],
        axis=1,
    )
    parcel = spread(parcel)
    vectors = parcel[:, : vectors.size].reshape(tm_size, 4 * layers, slices)
    vectors = jnp.transpose(vectors, (1, 0, 2)).reshape(4 * layers, width).astype(BF16)
    vectors = dot(vectors, shuffle, NN).reshape(2, layers, 2, width)
    gains, biases = vectors[0], vectors[1]
    places = parcel[:, -3 * rows :].reshape(tm_size, 3, rows)
    places = jnp.transpose(places, (1, 0, 2)).reshape(3, tokens)
    query_frames = places[0:1]
    key_frames = jnp.broadcast_to(places[0][:, None], (tokens, 128))
    sequence_tables = rotary_tables(places.T)
    row_tables = rotary_tables(jnp.transpose(whole_numbers, (0, 2, 1)).reshape(micro * rows, 3))
    start = ((here % repeats) * query_rows).reshape(1)

    attention_shards = [
        jnp.concatenate(
            [
                qkv_master[layer].astype(BF16).reshape(slices, 3 * columns),
                out_master[layer].astype(BF16).T,
            ],
            axis=1,
        )
        for layer in range(layers)
    ]
    up_held = [up_master[layer].astype(BF16) for layer in range(layers)]
    down_held = [down_master[layer].astype(BF16).T for layer in range(layers)]
    attention_held = attention_shards

    def own_rows(values):
        mine = lax.dynamic_slice_in_dim(values, half * odd, half, 1)
        mine = jnp.transpose(mine, (1, 0, 2)).reshape(half_rows, width)
        return dot(mine, shuffle, NN)

    def to_units(values):
        return jnp.repeat(values, repeats, axis=0) if repeats > 1 else values

    def from_units(values):
        if repeats == 1:
            return values
        grouped = values.reshape((units, repeats) + values.shape[1:]).astype(F32)
        return jnp.sum(grouped, axis=1).astype(BF16)

    sums = [((half_rows, width), BF16), ((half_rows, width), F32)]
    hidden = own_rows(inputs)
    upstream = own_rows(cotangent)
    attention_w = gather_now(attention_shards[0])
    up_held[0] = grow(up_held[0], 0)
    stored = []
    weights = []
    for layer in range(layers):
        more = layer + 1 < layers
        normed_one, root_one = normalize(hidden)
        first_own = (normed_one * gains[layer, 0] + biases[layer, 0]).astype(BF16)
        first_in = (first_own, swap(first_own, 1))
        first_in, attention_w, up, down = sync(
            first_in, attention_w, up_held[layer], down_held[layer]
        )
        packed = call(
            project_kernel,
            [((micro, pairs, rows, 3 * PAIR), BF16)],
            "project",
            *first_in,
            *attention_w,
            *row_tables,
        )
        packed = to_units(packed.reshape(units, rows, 3 * PAIR))
        qkv = spread(packed).reshape(tokens, 3 * PAIR)
        up = grow(up, 1)
        down = grow(down, 0)
        if more:
            qkv, up, down, attention_held[layer + 1] = sync(
                qkv, up, down, attention_held[layer + 1]
            )
        else:
            qkv, up, down = sync(qkv, up, down)
        mixed, mixed_t, lse = attend(start, qkv, key_frames, query_frames, query_rows)
        if repeats > 1:
            mixed = lax.dynamic_update_slice_in_dim(
                jnp.zeros((tokens, PAIR), BF16), mixed, start[0], 0
            )
        mixed = from_units(spread(mixed.reshape(tm_size, rows, PAIR)))
        up_w = finish(up)
        down = grow(down, 1)
        if more:
            attention_next = grow(attention_held[layer + 1], 0)
            mixed, up_w, down, attention_next = sync(mixed, up_w, down, attention_next)
        else:
            mixed, up_w, down = sync(mixed, up_w, down)
        middle = hidden + sum_heads(
            *call(functools.partial(mix_kernel, pairs), sums, "mix", mixed, *attention_w)
        )
        normed_two, root_two = normalize(middle)
        second_own = (normed_two * gains[layer, 1] + biases[layer, 1]).astype(BF16)
        second_in = (second_own, swap(second_own, 1))
        down_w = finish(down)
        if more:
            attention_next = grow(attention_next, 1)
            second_in, attention_next, up_held[layer + 1] = sync(
                second_in, attention_next, up_held[layer + 1]
            )
        activated, slope = up_project(*second_in, *up_w, hidden_units)
        hidden = middle + sum_heads(
            *call(down_kernel, sums, "down_project", activated, *down_w)
        )
        stored.append(
            (
                normed_one,
                root_one,
                first_in,
                qkv,
                mixed,
                mixed_t,
                lse,
                normed_two,
                root_two,
                second_in,
                activated,
                slope,
            )
        )
        weights.append((attention_w, up_w, down_w))
        if more:
            attention_w = finish(attention_next)
            up_held[layer + 1] = grow(up_held[layer + 1], 0)

    def all_rows(mine):
        ours = jnp.concatenate([mine, swap(mine, 1)], axis=0).reshape(micro, rows, width)
        return jnp.transpose(jnp.roll(ours, half * odd, axis=0), (1, 0, 2))

    outputs = all_rows(dot(hidden.astype(BF16), shuffle, NT).astype(BF16))
    qkv_grads, out_grads, up_grads, down_grads, gain_sums, bias_sums = [], [], [], [], [], []

    def products(kernel, sources, span, name):
        def side(index):
            return [
                whole() if place % 3 == 2 else columns_of(operand, middle_width, index)
                for place, operand in enumerate(sources)
            ]

        def far():
            return call(
                functools.partial(far_kernel, kernel),
                [((middle_width, span), BF16)],
                name + "_far",
                *sources,
                specs=side(1),
            )

        def near(arrived):
            kept = (middle_width // 2, span)
            return call(
                functools.partial(near_kernel, kernel),
                [(kept, F32), (kept, BF16)],
                name + "_near",
                *sources,
                arrived,
                specs=side(0) + [whole()],
            )

        return far, near

    late = None
    for layer in reversed(range(layers)):
        attention_w, up_w, down_w = weights[layer]
        (
            normed_one,
            root_one,
            first_in,
            qkv,
            mixed,
            mixed_t,
            lse,
            normed_two,
            root_two,
            second_in,
            activated,
            slope,
        ) = stored[layer]
        grad_own = upstream.astype(BF16)
        grad_mlp = (grad_own, swap(grad_own, 1))
        if late is None:
            grad_mlp = sync(grad_mlp)[0]
        else:
            grad_mlp, late_arrived = sync(grad_mlp, late_arrived)
            late_sum = late(late_arrived)
            late_sum = fold(*late_sum, 0)
        down_far, down_near = products(
            dense_products, (*grad_mlp, activated), hidden_units, "down_grad"
        )
        down_arrived = hop(down_far(), bits[-1])
        inner, theirs, mine = call(
            dense_back_kernel,
            [((micro * rows, hidden_units), BF16)] + sums,
            "dense_back",
            *grad_mlp,
            *up_w,
            *down_w,
            slope,
        )
        second_grad = sum_heads(theirs, mine)
        gain_two = jnp.sum(second_grad * normed_two, axis=0)
        bias_two = jnp.sum(second_grad, axis=0)
        upstream = upstream + norm_back(second_grad, normed_two, root_two, gains[layer, 1])
        grad_own = upstream.astype(BF16)
        grad_attn = (grad_own, swap(grad_own, 1))
        if late is None:
            grad_attn, down_arrived = sync(grad_attn, down_arrived)
        else:
            grad_attn, down_arrived, late_sum = sync(grad_attn, down_arrived, late_sum)
            late_sum = fold(*late_sum, 1)
        up_far, up_near = products(dense_products, (*second_in, inner), hidden_units, "up_grad")
        up_arrived = hop(up_far(), bits[-1])
        down_sum = fold(*down_near(down_arrived), 0)
        grad_mixed = call(
            unmix_kernel,
            [((micro, pairs, rows, PAIR), BF16)],
            "unmix",
            *grad_attn,
            *attention_w,
        )
        grad_mixed = to_units(grad_mixed.reshape(units, rows, PAIR))
        grad_mixed = spread(grad_mixed).reshape(tokens, PAIR)
        if repeats > 1:
            grad_mixed = lax.dynamic_slice_in_dim(grad_mixed, start[0], query_rows, 0)
        packed_grad = attend_back(
            start, qkv, grad_mixed, mixed_t, lse, key_frames, query_frames, sequence_tables
        )
        if late is None:
            packed_grad, up_arrived, down_sum = sync(packed_grad, up_arrived, down_sum)
        else:
            packed_grad, up_arrived, down_sum, late_sum = sync(
                packed_grad, up_arrived, down_sum, late_sum
            )
            qkv_grads.append(late_sum[:, : 3 * columns].reshape(slices, 3, columns))
            out_grads.append(late_sum[:, 3 * columns :].T)
        packed_grad = from_units(spread(packed_grad.reshape(tm_size, rows, 3 * PAIR)))
        down_sum = fold(*down_sum, 1)
        up_sum = fold(*up_near(up_arrived), 0)
        packed_grad, up_sum, down_sum = sync(packed_grad, up_sum, down_sum)
        far, late = products(
            functools.partial(attention_products, pairs),
            (*first_in, packed_grad, *grad_attn, mixed),
            4 * columns,
            "attention_grad",
        )
        late_arrived = hop(far(), bits[-1])
        up_sum = fold(*up_sum, 1)
        first_grad = sum_heads(
            *call(
                functools.partial(unproject_kernel, pairs),
                sums,
                "unproject",
                packed_grad,
                *attention_w,
            )
        )
        gain_one = jnp.sum(first_grad * normed_one, axis=0)
        bias_one = jnp.sum(first_grad, axis=0)
        upstream = upstream + norm_back(first_grad, normed_one, root_one, gains[layer, 0])
        up_grads.append(up_sum)
        down_grads.append(down_sum.T)
        gain_sums.append(jnp.stack([gain_one, gain_two]))
        bias_sums.append(jnp.stack([bias_one, bias_two]))
    late_sum = fold(*fold(*late(late_arrived), 0), 1)
    qkv_grads.append(late_sum[:, : 3 * columns].reshape(slices, 3, columns))
    out_grads.append(late_sum[:, 3 * columns :].T)
    small = jnp.stack([jnp.stack(gain_sums[::-1]), jnp.stack(bias_sums[::-1])])
    small = (small + swap(small, 1)).reshape(4 * layers, width)
    exact = lax.Precision.HIGHEST
    small = lax.dot_general(small, shuffle.astype(F32), NT, precision=exact)
    small = small.reshape(4 * layers, tm_size, slices).transpose(1, 0, 2)
    small = jnp.sum(spread(small), axis=0).reshape(2, layers, 2, slices)
    input_grad = lax.dot_general(upstream, shuffle.astype(F32), NT, precision=exact)
    return (
        outputs,
        all_rows(input_grad),
        jnp.stack(qkv_grads[::-1]),
        jnp.stack(out_grads[::-1]),
        jnp.stack(up_grads[::-1]),
        jnp.stack(down_grads[::-1]),
        small[0],
        small[1],
    )


def solution(mesh):
    placed = (
        P("tm", None, None),
        P(None, "tm", None, "head"),
        P(None, "head", "tm"),
        P(None, "tm", "head"),
        P(None, "head", "tm"),
        P(None, None, "tm"),
        P(None, None, "tm"),
        P("tm", None),
        P(None, "tm", None),
        P("tm", None, None),
    )
    return jax.shard_map(
        body,
        mesh=mesh,
        in_specs=placed,
        out_specs=(
            P("tm", None, None),
            P("tm", None, None),
            P(None, "tm", None, "head"),
            P(None, "head", "tm"),
            P(None, "tm", "head"),
            P(None, "head", "tm"),
            P(None, None, "tm"),
            P(None, None, "tm"),
        ),
        check_vma=False,
    )
```

```python
import functools

import jax
import jax.numpy as jnp
from jax import lax
from jax.experimental import pallas as pl
from jax.experimental.pallas import tpu as pltpu
from jax.sharding import PartitionSpec as P

HEAD_DIM = 64
PAIR = 2 * HEAD_DIM
GROUP = HEAD_DIM // 6
NEG_BIG = -1e30
F32 = jnp.float32
BF16 = jnp.bfloat16
NT = (((1,), (1,)), ((), ()))
TN = (((0,), (0,)), ((), ()))
NN = (((1,), (0,)), ((), ()))


def dot(left, right, dims):
    return lax.dot_general(left, right, dims, preferred_element_type=F32)


def rotary_tables(coordinates):
    lane = jnp.arange(PAIR, dtype=jnp.int32) % HEAD_DIM
    group = jnp.minimum(lane // (2 * GROUP), 2)
    place = lane % (2 * GROUP)
    turned = lane < 6 * GROUP
    first = turned & (place < GROUP)
    second = turned & (place >= GROUP)
    inverse = 10000.0 ** (-(place % GROUP).astype(F32) / GROUP)
    spread = jnp.where(
        group == 0,
        coordinates[:, 0:1],
        jnp.where(group == 1, coordinates[:, 1:2], coordinates[:, 2:3]),
    )
    angles = spread * inverse
    cosine = jnp.where(turned, jnp.cos(angles), 1.0)
    sine = jnp.sin(angles)
    return (cosine, jnp.where(first, -sine, 0.0), jnp.where(second, sine, 0.0))


def turn(values, cosine, sine_first, sine_second):
    ahead = pltpu.roll(values, PAIR - GROUP, 1)
    behind = pltpu.roll(values, GROUP, 1)
    return values * cosine + ahead * sine_first + behind * sine_second


def turn_back(values, cosine, sine_first, sine_second):
    ahead = pltpu.roll(values, PAIR - GROUP, 1)
    behind = pltpu.roll(values, GROUP, 1)
    return values * cosine - ahead * sine_first - behind * sine_second


def project_kernel(own, peer, left, right, cosine, sine_first, sine_second, out):
    rows = out.shape[2]
    width = out.shape[1] * PAIR
    middle = left.shape[0]
    for step, acts in enumerate((own, peer)):
        span = pl.ds(step * 2 * rows, 2 * rows)
        raw = dot(acts[:, :middle], left[:, : 3 * width], NN)
        raw += dot(acts[:, middle:], right[:, : 3 * width], NN)
        tables = (cosine[span, :], sine_first[span, :], sine_second[span, :])
        for pair in range(out.shape[1]):
            for part in range(3):
                start = part * width + pair * PAIR
                piece = raw[:, start : start + PAIR]
                if part < 2:
                    piece = turn(piece, *tables)
                piece = piece.astype(BF16)
                for half in range(2):
                    out[2 * step + half, pair, :, part * PAIR : (part + 1) * PAIR] = piece[
                        half * rows : (half + 1) * rows
                    ]


def unit_rows(tiles, micros, pairs, lanes):
    return jnp.concatenate(
        [
            jnp.concatenate([tiles[micro * pairs + pair, :, lanes] for pair in range(pairs)], axis=1)
            for micro in micros
        ],
        axis=0,
    )


def mix_kernel(pairs, mixed, left, right, theirs, mine):
    width = pairs * PAIR
    micro = mixed.shape[0] // pairs
    middle = left.shape[0]
    skip = left.shape[1] - width
    for micros, out in ((range(micro // 2, micro), theirs), (range(micro // 2), mine)):
        rows = unit_rows(mixed, micros, pairs, slice(0, PAIR))
        out[:, :middle] = dot(rows, left[:, skip:], NT).astype(out.dtype)
        out[:, middle:] = dot(rows, right[:, skip:], NT).astype(out.dtype)


def unmix_kernel(own, peer, left, right, out):
    rows = out.shape[2]
    width = out.shape[1] * PAIR
    middle = left.shape[0]
    skip = left.shape[1] - width
    for step, acts in enumerate((own, peer)):
        raw = dot(acts[:, :middle], left[:, skip:], NN) + dot(acts[:, middle:], right[:, skip:], NN)
        raw = raw.astype(BF16)
        for pair in range(out.shape[1]):
            for half in range(2):
                out[2 * step + half, pair] = raw[
                    half * rows : (half + 1) * rows, pair * PAIR : (pair + 1) * PAIR
                ]


def unproject_kernel(pairs, packed, left, right, theirs, mine):
    width = pairs * PAIR
    micro = packed.shape[0] // pairs
    middle = left.shape[0]
    for micros, out in ((range(micro // 2, micro), theirs), (range(micro // 2), mine)):
        for weights, place in ((left, slice(0, middle)), (right, slice(middle, 2 * middle))):
            total = 0.0
            for part in range(3):
                rows = unit_rows(packed, micros, pairs, slice(part * PAIR, (part + 1) * PAIR))
                total += dot(rows, weights[:, part * width : (part + 1) * width], NT)
            out[:, place] = total.astype(out.dtype)


def up_kernel(own, peer, left, right, activated, slope):
    middle = left.shape[0]
    half = own.shape[0]
    for start in range(0, activated.shape[1], 256):
        block = slice(start, start + 256)
        for step, acts in enumerate((own, peer)):
            upward = dot(acts[:, :middle], left[:, block], NN)
            upward += dot(acts[:, middle:], right[:, block], NN)
            bell = 0.5 * (1.0 + lax.erf(upward * 0.7071067811865476))
            span = slice(step * half, (step + 1) * half)
            activated[span, block] = (upward * bell).astype(BF16)
            slope[span, block] = (
                bell + upward * jnp.exp(-0.5 * upward * upward) * 0.3989422804014327
            )


def down_kernel(activated, left, right, theirs, mine):
    half = mine.shape[0]
    middle = left.shape[0]
    for span, out in ((slice(half, 2 * half), theirs), (slice(0, half), mine)):
        out[:, :middle] = dot(activated[span, :], left[...], NT).astype(out.dtype)
        out[:, middle:] = dot(activated[span, :], right[...], NT).astype(out.dtype)


def dense_back_kernel(own, peer, up_left, up_right, down_left, down_right, slope, inner, theirs, mine):
    half = mine.shape[0]
    middle = up_left.shape[0]
    for acts, span, out in (
        (peer, slice(half, 2 * half), theirs),
        (own, slice(0, half), mine),
    ):
        raw = dot(acts[:, :middle], down_left[...], NN)
        raw += dot(acts[:, middle:], down_right[...], NN)
        grad = (raw * slope[span, :]).astype(BF16)
        inner[span, :] = grad
        out[:, :middle] = dot(grad, up_left[...], NT).astype(out.dtype)
        out[:, middle:] = dot(grad, up_right[...], NT).astype(out.dtype)


def side_of(own, peer, side):
    middle = own.shape[1] // 2
    span = slice(side * middle, (side + 1) * middle)
    return jnp.concatenate([own[:, span], peer[:, span]], axis=0)


def product_blocks(left, right, start):
    for place in range(0, right.shape[1], 256):
        yield start + place, dot(left, right[:, place : place + 256], TN)


def down_products(side, own, peer, activated):
    yield from product_blocks(side_of(own, peer, side), activated, 0)


def up_products(side, own, peer, inner):
    yield from product_blocks(side_of(own, peer, side), inner, 0)


def dense_products(side, first_own, first_peer, inner, grad_own, grad_peer, activated):
    yield from product_blocks(side_of(first_own, first_peer, side), inner, 0)
    yield from product_blocks(side_of(grad_own, grad_peer, side), activated, inner.shape[1])


def projection_products(pairs, parts, side, first_own, first_peer, packed):
    first = side_of(first_own, first_peer, side)
    micros = range(packed.shape[0] // pairs)
    for place, part in enumerate(parts):
        rows = unit_rows(packed, micros, pairs, slice(part * PAIR, (part + 1) * PAIR))
        yield place * pairs * PAIR, dot(first, rows, TN)


def mix_products(pairs, side, grad_own, grad_peer, mixed):
    micros = range(mixed.shape[0] // pairs)
    grad = side_of(grad_own, grad_peer, side)
    yield 0, dot(grad, unit_rows(mixed, micros, pairs, slice(0, PAIR)), TN)


def attention_products(pairs, side, first_own, first_peer, packed, grad_own, grad_peer, mixed):
    yield from projection_products(pairs, range(3), side, first_own, first_peer, packed)
    for start, value in mix_products(pairs, side, grad_own, grad_peer, mixed):
        yield 3 * pairs * PAIR + start, value


def far_kernel(products, *refs):
    out = refs[-1]
    for start, value in products(1, *refs[:-1]):
        out[:, start : start + value.shape[1]] = value.astype(BF16)


def near_kernel(products, arrivals, *refs):
    keep, send = refs[-2:]
    half = keep.shape[0]
    arrived = refs[-2 - arrivals : -2]
    width = arrived[0].shape[1]
    for start, value in products(0, *refs[: -2 - arrivals]):
        come = arrived[start // width]
        place = start % width
        value = value + come[:, place : place + value.shape[1]].astype(F32)
        keep[:, start : start + value.shape[1]] = value[:half]
        send[:, start : start + value.shape[1]] = value[half:].astype(BF16)


def lane_mask(shape, head):
    lane = lax.broadcasted_iota(jnp.int32, shape, 1)
    return (lane >= head * HEAD_DIM) & (lane < (head + 1) * HEAD_DIM)


def visible_bias(key_frames, query_frames, block):
    spread = jnp.concatenate([key_frames] * (block // key_frames.shape[1]), axis=1)
    return spread <= query_frames


def attend_kernel(block, start, qkv, key_frames, query_frames, out, out_t, lse):
    key_vecs = qkv[:, PAIR : 2 * PAIR]
    value_t = jnp.transpose(qkv[:, 2 * PAIR :].astype(F32)).astype(BF16)
    query_rows = out.shape[0]

    def one(step, carry):
        place = pl.multiple_of(step * block, block)
        source = pl.multiple_of(start[0] + step * block, block)
        queries = qkv[pl.ds(source, block), :PAIR] * jnp.asarray(HEAD_DIM**-0.5, BF16)
        seen = visible_bias(key_frames[...], query_frames[:, pl.ds(source, block)], block)
        pieces = []
        for head in range(2):
            mine = jnp.where(lane_mask(queries.shape, head), queries, jnp.zeros_like(queries))
            scores = jnp.where(seen, dot(key_vecs, mine, NT), NEG_BIG)
            top = jnp.max(scores, axis=0, keepdims=True)
            raised = jnp.exp(scores - top)
            total = jnp.sum(raised, axis=0, keepdims=True)
            summed = dot(
                value_t[head * HEAD_DIM : (head + 1) * HEAD_DIM], raised.astype(BF16), NN
            )
            pieces.append(summed / total)
            lse[head : head + 1, pl.ds(place, block)] = top + jnp.log(total)
        both = jnp.concatenate(pieces, axis=0)
        out_t[:, pl.ds(place, block)] = both
        out[pl.ds(place, block), :] = jnp.transpose(both).astype(BF16)
        return carry

    lax.fori_loop(0, query_rows // block, one, 0)


def attend_back_kernel(
    block,
    start,
    qkv,
    grad_out,
    out_t,
    lse,
    key_frames,
    query_frames,
    cosine,
    sine_first,
    sine_second,
    result,
    key_sum,
    value_sum,
):
    key_vecs = qkv[:, PAIR : 2 * PAIR]
    value_vecs = qkv[:, 2 * PAIR :]
    key_t = jnp.transpose(key_vecs.astype(F32)).astype(BF16)
    query_rows = grad_out.shape[0]
    key_sum[...] = jnp.zeros_like(key_sum)
    value_sum[...] = jnp.zeros_like(value_sum)
    if query_rows != qkv.shape[0]:
        result[:, :PAIR] = jnp.zeros((qkv.shape[0], PAIR), BF16)

    def one(step, carry):
        place = pl.multiple_of(step * block, block)
        source = pl.multiple_of(start[0] + step * block, block)
        queries = qkv[pl.ds(source, block), :PAIR] * jnp.asarray(HEAD_DIM**-0.5, BF16)
        upstream = grad_out[pl.ds(place, block), :]
        seen = visible_bias(key_frames[...], query_frames[:, pl.ds(source, block)], block)
        both = out_t[:, pl.ds(place, block)] * jnp.transpose(upstream.astype(F32))
        pieces = []
        for head in range(2):
            keep = lane_mask(queries.shape, head)
            mine = jnp.where(keep, queries, jnp.zeros_like(queries))
            above = jnp.where(keep, upstream, jnp.zeros_like(upstream))
            rows = slice(head * HEAD_DIM, (head + 1) * HEAD_DIM)
            delta = jnp.sum(both[rows], axis=0, keepdims=True)
            log_total = lse[head : head + 1, pl.ds(place, block)]
            weights = jnp.where(seen, jnp.exp(dot(key_vecs, mine, NT) - log_total), 0.0)
            slope = (weights * (dot(value_vecs, above, NT) - delta)).astype(BF16)
            value_sum[...] += dot(weights.astype(BF16), above, NN)
            key_sum[...] += dot(slope, mine, NN)
            pieces.append(dot(key_t[rows], slope, NN))
        query_grad = jnp.transpose(jnp.concatenate(pieces, axis=0)) * HEAD_DIM**-0.5
        span = pl.ds(source, block)
        result[span, :PAIR] = turn_back(
            query_grad, cosine[span, :], sine_first[span, :], sine_second[span, :]
        ).astype(BF16)
        return carry

    lax.fori_loop(0, query_rows // block, one, 0)
    result[:, PAIR : 2 * PAIR] = turn_back(
        key_sum[...], cosine[...], sine_first[...], sine_second[...]
    ).astype(BF16)
    result[:, 2 * PAIR :] = value_sum[...].astype(BF16)


def whole():
    return pl.BlockSpec(memory_space=pltpu.VMEM)


def scalars():
    return pl.BlockSpec(memory_space=pltpu.SMEM)


def on_chip(operands):
    return [pltpu.with_memory_space_constraint(operand, pltpu.VMEM) for operand in operands]


def call(kernel, outs, name, *operands, numbers=(), scratch=(), scale=1, local=True):
    shapes = [(pltpu.VMEM if local else jax.ShapeDtypeStruct)(shape, kind) for shape, kind in outs]
    single = len(shapes) == 1
    return pl.pallas_call(
        kernel,
        out_shape=shapes[0] if single else shapes,
        in_specs=[scalars()] * len(numbers) + [whole()] * len(operands),
        out_specs=whole() if single else [whole()] * len(shapes),
        scratch_shapes=scratch,
        compiler_params=pltpu.CompilerParams(vmem_limit_bytes=scale * 10 * 1024 * 1024),
        name=name,
    )(*numbers, *(on_chip(operands) if local else operands))


def call_window(kernel, outs, name, operands, weights, width, index):
    shapes = [jax.ShapeDtypeStruct(shape, kind) for shape, kind in outs]

    def full(shape):
        return pl.BlockSpec(shape, lambda i: (0,) * len(shape))

    single = len(shapes) == 1
    specs = [full(shape) for shape, kind in outs]
    return pl.pallas_call(
        kernel,
        grid=(1,),
        out_shape=shapes[0] if single else shapes,
        in_specs=[full(operand.shape) for operand in operands]
        + [pl.BlockSpec((part.shape[0], width), lambda i: (0, index)) for part in weights],
        out_specs=specs[0] if single else specs,
        compiler_params=pltpu.CompilerParams(vmem_limit_bytes=10 * 1024 * 1024),
        name=name,
    )(*operands, *weights)


def attend(start, qkv, key_frames, query_frames, query_rows):
    return call(
        functools.partial(attend_kernel, 256),
        [((query_rows, PAIR), BF16), ((PAIR, query_rows), F32), ((2, query_rows), F32)],
        "attend",
        qkv,
        key_frames,
        query_frames,
        numbers=(start,),
        scale=max(2, 2 * qkv.shape[0] // 1024),
        local=False,
    )


def attend_back(start, qkv, grad_out, out_t, lse, key_frames, query_frames, tables):
    return call(
        functools.partial(attend_back_kernel, 256),
        [(qkv.shape, BF16)],
        "attend_back",
        qkv,
        grad_out,
        out_t,
        lse,
        key_frames,
        query_frames,
        *tables,
        numbers=(start,),
        scratch=[pltpu.VMEM((qkv.shape[0], PAIR), F32)] * 2,
        scale=max(2, 2 * qkv.shape[0] // 1024),
        local=False,
    )


def restore_kernel(places, values, out):
    size = values.shape[1] // places.shape[0]
    for block in range(places.shape[0]):
        place = pl.multiple_of(places[block], size)
        out[:, pl.ds(place, size)] = values[:, block * size : (block + 1) * size]


def restore(places, shuffle, values):
    if values.shape[1] // places.shape[0] % 128 == 0:
        return call(restore_kernel, [(values.shape, values.dtype)], "restore", values, numbers=(places,))
    exact = lax.Precision.HIGHEST
    return lax.dot_general(
        values.astype(F32), shuffle.astype(F32), NT, precision=exact
    ).astype(values.dtype)


def normalize(hidden):
    centered = hidden - jnp.mean(hidden, axis=-1, keepdims=True)
    inverse_root = lax.rsqrt(jnp.mean(centered * centered, axis=-1, keepdims=True) + 1e-06)
    return (centered * inverse_root, inverse_root)


def norm_back(upstream, normed, inverse_root, gain_row):
    scaled = upstream * gain_row
    return inverse_root * (
        scaled
        - jnp.mean(scaled, axis=-1, keepdims=True)
        - normed * jnp.mean(scaled * normed, axis=-1, keepdims=True)
    )


def body(
    inputs,
    qkv_master,
    out_master,
    up_master,
    down_master,
    norm_gain,
    norm_bias,
    frame_ids,
    patch_pos,
    cotangent,
):
    rows, micro, width = inputs.shape
    tm_size = lax.axis_size("tm")
    head_size = lax.axis_size("head")
    here = lax.axis_index("tm")
    layers = qkv_master.shape[0]
    columns = qkv_master.shape[3]
    hidden_units = up_master.shape[2]
    slices = width // tm_size
    middle_width = width // 2
    half = micro // 2
    half_rows = half * rows
    odd = lax.axis_index("head") % 2
    pairs = columns // PAIR
    units = micro * pairs
    repeats = tm_size // units
    tokens = rows * tm_size
    query_rows = tokens // repeats

    bits = []
    order = [0]
    bit = tm_size // 2
    while bit:
        bits.append(bit)
        order = order + [place | bit for place in order]
        bit //= 2
    last = bits[-1]

    def sync(*values):
        return lax.optimization_barrier(values)

    def hop(values, bit):
        return lax.ppermute(values, "tm", [(i, i ^ bit) for i in range(tm_size)])

    def swap(values, bit):
        return lax.ppermute(values, "head", [(i, i ^ bit) for i in range(head_size)])

    def sum_heads(theirs, mine):
        total = (mine + swap(theirs, 1).astype(F32)).astype(BF16)
        bit = 2
        while True:
            total = lax.optimization_barrier(total)
            total = total.astype(F32) + swap(total, bit).astype(F32)
            bit *= 2
            if bit >= head_size:
                return total
            total = total.astype(BF16)

    def spread(values):
        return lax.all_to_all(values, "tm", 0, 0, tiled=True)

    def grow(held, some):
        for bit in some:
            held = jnp.concatenate([held, hop(held, bit)], axis=0)
        return held

    def reach(held, some):
        pieces = [held]
        for bit in some:
            so_far = jnp.concatenate(pieces, axis=0) if len(pieces) > 1 else held
            pieces.append(hop(so_far, bit))
        return pieces

    def stack(pieces):
        return jnp.concatenate(pieces, axis=0)

    def fold(parts, some):
        keep, send = parts
        for bit in some:
            total = keep + hop(send, bit).astype(F32)
            if bit == bits[0]:
                return total
            cut = total.shape[0] // 2
            keep, send = total[:cut], total[cut:].astype(BF16)
        return keep, send

    def own_rows(values, shuffle):
        mine = lax.dynamic_slice_in_dim(values, half * odd, half, 1)
        mine = jnp.transpose(mine, (1, 0, 2)).reshape(half_rows, width)
        return dot(mine, shuffle, NN)

    def to_units(values):
        return jnp.repeat(values, repeats, axis=0) if repeats > 1 else values

    def from_units(values):
        if repeats == 1:
            return values
        grouped = values.reshape((units, repeats) + values.shape[1:]).astype(F32)
        return jnp.sum(grouped, axis=1).astype(BF16)

    attention_held = [
        jnp.concatenate(
            [
                qkv_master[layer].astype(BF16).reshape(slices, 3 * columns),
                out_master[layer].astype(BF16).T,
            ],
            axis=1,
        )
        for layer in range(layers)
    ]
    up_held = [up_master[layer].astype(BF16) for layer in range(layers)]
    down_held = [down_master[layer].astype(BF16).T for layer in range(layers)]

    pieces = {0: attention_held[0]}
    for bit in bits:
        pieces[bit] = hop(pieces[0], bit)

    ordered = (jnp.arange(micro) + half * odd) % micro
    whole_numbers = jnp.concatenate([frame_ids[None], patch_pos], axis=0).astype(F32)
    whole_numbers = jnp.take(jnp.transpose(whole_numbers, (2, 0, 1)), ordered, axis=0)
    vectors = jnp.concatenate([norm_gain, norm_bias], axis=0).astype(BF16).astype(F32)
    parcel = jnp.concatenate(
        [
            jnp.broadcast_to(vectors.reshape(1, -1), (tm_size, vectors.size)),
            jnp.repeat(whole_numbers.reshape(micro, 3 * rows), tm_size // micro, axis=0),
        ],
        axis=1,
    )
    parcel = spread(parcel)

    early = [pieces.pop(bit) for bit in bits[:-1]]
    early, inputs, whole_numbers, up, here = sync(
        early, inputs, whole_numbers, up_held[0], here
    )
    pieces.update(zip(bits[:-1], early))
    for bit in bits:
        for place in [place for place in order if place and place & (bit - 1) == 0]:
            if place & bit and place not in pieces:
                pieces[place] = hop(pieces[place ^ bit], bit)
    up = grow(up, bits[:1])
    down = down_held[0]
    feature = jnp.arange(width, dtype=jnp.int32)
    origin = (here ^ jnp.asarray(order, jnp.int32)[:, None]) * slices + jnp.arange(
        slices, dtype=jnp.int32
    )
    shuffle = (feature[:, None] == origin.reshape(1, width)).astype(BF16)
    vectors = parcel[:, : vectors.size].reshape(tm_size, 4 * layers, slices)
    vectors = jnp.transpose(vectors, (1, 0, 2)).reshape(4 * layers, width).astype(BF16)
    vectors = dot(vectors, shuffle, NN).reshape(2, layers, 2, width)
    gains, biases = vectors[0], vectors[1]
    places = parcel[:, -3 * rows :].reshape(tm_size, 3, rows)
    places = jnp.transpose(places, (1, 0, 2)).reshape(3, tokens)
    query_frames = places[0:1]
    key_frames = jnp.broadcast_to(places[0][:, None], (tokens, 128))
    row_tables = rotary_tables(jnp.transpose(whole_numbers, (0, 2, 1)).reshape(micro * rows, 3))
    start = ((here % repeats) * query_rows).reshape(1)
    offsets = origin[:, 0]

    sums = [((half_rows, width), BF16), ((half_rows, width), F32)]
    hidden = own_rows(inputs, shuffle)
    attention_w = tuple(
        jnp.concatenate([pieces[place] for place in places_of], axis=0)
        for places_of in (order[: tm_size // 2], order[tm_size // 2 :])
    )
    stored = []
    weights = []
    for layer in range(layers):
        more = layer + 1 < layers
        normed_one, root_one = normalize(hidden)
        first_own = (normed_one * gains[layer, 0] + biases[layer, 0]).astype(BF16)
        first_in = (first_own, swap(first_own, 1))
        if layer == 0:
            first_in, attention_w, down = sync(first_in, attention_w, down)
        else:
            first_in, attention_w, up, down = sync(first_in, attention_w, up, down)
        packed = call(
            project_kernel,
            [((micro, pairs, rows, 3 * PAIR), BF16)],
            "project",
            *first_in,
            *attention_w,
            *row_tables,
        )
        packed = to_units(packed.reshape(units, rows, 3 * PAIR))
        qkv = spread(packed).reshape(tokens, 3 * PAIR)
        if layer == 0:
            up = reach(up, bits[1:-1])
        up_far = [hop(up[0], last)]
        down = grow(down, bits[:1])
        if layer == 0:
            sequence_tables = rotary_tables(places.T)
            qkv, up, up_far, down, sequence_tables = sync(
                qkv, up, up_far, down, sequence_tables
            )
        else:
            qkv, up, up_far, down = sync(qkv, up, up_far, down)
        up_far = up_far + [hop(piece, last) for piece in up[1:]]
        down = reach(down, bits[1:-1])
        mixed, mixed_t, lse = attend(start, qkv, key_frames, query_frames, query_rows)
        if repeats > 1:
            mixed = lax.dynamic_update_slice_in_dim(
                jnp.zeros((tokens, PAIR), BF16), mixed, start[0], 0
            )
        mixed = from_units(spread(mixed.reshape(tm_size, rows, PAIR)))
        if more:
            mixed, up_far, down, coming, next_up, next_down = sync(
                mixed,
                up_far,
                down,
                attention_held[layer + 1],
                up_held[layer + 1],
                down_held[layer + 1],
            )
        else:
            mixed, up_far, down = sync(mixed, up_far, down)
        middle = hidden + sum_heads(
            *call_window(
                functools.partial(mix_kernel, pairs),
                sums,
                "mix",
                (mixed,),
                attention_w,
                columns,
                3,
            )
        )
        normed_two, root_two = normalize(middle)
        second_own = (normed_two * gains[layer, 1] + biases[layer, 1]).astype(BF16)
        second_in = (second_own, swap(second_own, 1))
        down_far = [hop(piece, last) for piece in down]
        up_w = (stack(up), stack(up_far))
        if more:
            coming = reach(grow(coming, bits[:1]), bits[1:-1])
            second_in, up_w, coming, next_up = sync(second_in, up_w, coming, next_up)
            coming_far = [hop(piece, last) for piece in coming]
            next_up = reach(grow(next_up, bits[:1]), bits[1:-1])
        else:
            second_in, up_w = sync(second_in, up_w)
        activated, slope = call(
            up_kernel,
            [((micro * rows, hidden_units), BF16), ((micro * rows, hidden_units), F32)],
            "up_project",
            *second_in,
            *up_w,
        )
        down_w = (stack(down), stack(down_far))
        activated, down_w = sync(activated, down_w)
        if more:
            hidden = middle + sum_heads(
                *call(down_kernel, sums, "down_project", activated, *down_w)
            )
        stored.append(
            (
                normed_one,
                root_one,
                first_in,
                qkv,
                mixed,
                mixed_t,
                lse,
                normed_two,
                root_two,
                second_in,
                activated,
                slope,
            )
        )
        weights.append((attention_w, up_w, down_w))
        if more:
            attention_w = (stack(coming), stack(coming_far))
            up, down = next_up, next_down

    def all_rows(mine):
        ours = jnp.concatenate([mine, swap(mine, 1)], axis=0).reshape(micro, rows, width)
        return jnp.transpose(jnp.roll(ours, half * odd, axis=0), (1, 0, 2))

    def finish(middle, activated, down_w):
        hidden = middle + sum_heads(
            *call(down_kernel, sums, "down_project", activated, *down_w)
        )
        return all_rows(restore(offsets, shuffle, hidden.astype(BF16)))

    upstream = own_rows(cotangent, shuffle)

    def far(kernel, span, name, *sources):
        return call(
            functools.partial(far_kernel, kernel), [((middle_width, span), BF16)], name, *sources
        )

    def near(kernel, span, name, arrivals, *sources):
        kept = (middle_width // 2, span)
        return call(
            functools.partial(near_kernel, kernel, len(arrivals)),
            [(kept, F32), (kept, BF16)],
            name,
            *sources,
            *arrivals,
        )

    gain_sums, bias_sums = [], []
    up_grads, down_grads, qkv_grads, out_grads = [], [], [], []
    middle_bits, first_bit = bits[-2:0:-1], bits[:1]
    mix_pairs = functools.partial(mix_products, pairs)
    late = None
    for layer in reversed(range(layers)):
        attention_w, up_w, down_w = weights[layer]
        (
            normed_one,
            root_one,
            first_in,
            qkv,
            mixed,
            mixed_t,
            lse,
            normed_two,
            root_two,
            second_in,
            activated,
            slope,
        ) = stored[layer]
        ending = layer == 0
        grad_own = upstream.astype(BF16)
        grad_mlp = (grad_own, swap(grad_own, 1))
        if late:
            grad_mlp, late_down = sync(grad_mlp, late_down)
        inner, theirs, mine = call(
            dense_back_kernel,
            [((micro * rows, hidden_units), BF16)] + sums,
            "dense_back",
            *grad_mlp,
            *up_w,
            *down_w,
            slope,
        )
        down_far = far(down_products, hidden_units, "down_far", *grad_mlp, activated)
        theirs, mine, inner, down_far = sync(theirs, mine, inner, down_far)
        if late:
            theirs, late_far, late_up = sync(theirs, late_far, late_up)
            late_up = fold(late_up, first_bit)
        down_far = hop(down_far, last)
        second_grad = sum_heads(theirs, mine)
        if late:
            late_sum = near(by_pairs, 4 * columns, "attention_near", (late_far,), *late)
            late_sum = fold(late_sum, middle_bits)
        up_far = far(up_products, hidden_units, "up_far", *second_in, inner)
        gain_two = jnp.sum(second_grad * normed_two, axis=0)
        bias_two = jnp.sum(second_grad, axis=0)
        upstream = upstream + norm_back(second_grad, normed_two, root_two, gains[layer, 1])
        grad_own = upstream.astype(BF16)
        grad_attn = (grad_own, swap(grad_own, 1))
        if late:
            grad_attn, up_far, down_far, late_up, late_sum = sync(
                grad_attn, up_far, down_far, late_up, late_sum
            )
            down_grads.append(late_down)
            up_grads.append(late_up)
        else:
            grad_attn, up_far, down_far = sync(grad_attn, up_far, down_far)
        grad_mixed = call_window(
            unmix_kernel,
            [((micro, pairs, rows, PAIR), BF16)],
            "unmix",
            grad_attn,
            attention_w,
            columns,
            3,
        )
        grad_mixed = to_units(grad_mixed.reshape(units, rows, PAIR))
        grad_mixed = spread(grad_mixed).reshape(tokens, PAIR)
        if repeats > 1:
            grad_mixed = lax.dynamic_slice_in_dim(grad_mixed, start[0], query_rows, 0)
        down_sum = near(
            down_products, hidden_units, "down_near", (down_far,), *grad_mlp, activated
        )
        up_far, down_sum = sync(up_far, down_sum)
        up_far = hop(up_far, last)
        grad_mixed, down_sum = sync(grad_mixed, down_sum)
        down_sum = fold(down_sum, middle_bits)
        if late:
            grad_mixed, late_sum = sync(grad_mixed, late_sum)
            late_sum = fold(late_sum, first_bit)
        if ending:
            out_far = far(mix_pairs, columns, "out_far", *grad_attn, mixed)
            out_far = hop(out_far, last)
        packed_grad = attend_back(
            start, qkv, grad_mixed, mixed_t, lse, key_frames, query_frames, sequence_tables
        )
        if late:
            packed_grad, late_sum = sync(packed_grad, late_sum)
            qkv_grads.append(late_sum[:, : 3 * columns].reshape(slices, 3, columns))
            out_grads.append(late_sum[:, 3 * columns :])
        packed_grad, up_far, down_sum = sync(packed_grad, up_far, down_sum)
        if layer + 1 == layers:
            packed_grad, middle, last_in = sync(packed_grad, middle, activated)
            outputs = finish(middle, last_in, down_w)
        down_sum = fold(down_sum, first_bit)
        up_sum = near(up_products, hidden_units, "up_near", (up_far,), *second_in, inner)
        if ending:
            packed_grad, out_far = sync(packed_grad, out_far)
            out_sum = near(mix_pairs, columns, "out_near", (out_far,), *grad_attn, mixed)
            out_sum = fold(out_sum, middle_bits)
        packed_grad = from_units(spread(packed_grad.reshape(tm_size, rows, 3 * PAIR)))
        packed_grad, up_sum = sync(packed_grad, up_sum)
        up_sum = fold(up_sum, middle_bits)
        by_pairs = functools.partial(attention_products, pairs)
        if ending:
            packed_grad, out_sum = sync(packed_grad, out_sum)
            groups = []
            for parts in ((0, 1), (2,)):
                products = functools.partial(projection_products, pairs, parts)
                span = len(parts) * columns
                arrived = far(products, span, "qkv_far", *first_in, packed_grad)
                groups.append((products, span, hop(arrived, last)))
        else:
            late = (*first_in, packed_grad, *grad_attn, mixed)
            late_far = hop(far(by_pairs, 4 * columns, "attention_far", *late), last)
            late_down = down_sum
            late_up = up_sum
        theirs, mine = call(
            functools.partial(unproject_kernel, pairs),
            sums,
            "unproject",
            packed_grad,
            *attention_w,
        )
        if ending:
            theirs, mine, up_sum, out_sum = sync(theirs, mine, up_sum, out_sum)
        first_grad = sum_heads(theirs, mine)
        gain_one = jnp.sum(first_grad * normed_one, axis=0)
        bias_one = jnp.sum(first_grad, axis=0)
        upstream = upstream + norm_back(first_grad, normed_one, root_one, gains[layer, 0])
        if ending:
            up_grads.append(fold(up_sum, first_bit))
            out_grads.append(fold(out_sum, first_bit))
            down_grads.append(down_sum)
            qkv_sums = []
            for products, span, arrived in groups:
                part = near(products, span, "qkv_near", (arrived,), *first_in, packed_grad)
                qkv_sums.append(fold(fold(part, middle_bits), first_bit))
            qkv_sums = [part.reshape(slices, -1, columns) for part in qkv_sums]
            qkv_grads.append(jnp.concatenate(qkv_sums, axis=1))
        gain_sums.append(jnp.stack([gain_one, gain_two]))
        bias_sums.append(jnp.stack([bias_one, bias_two]))
    small = jnp.stack([jnp.stack(gain_sums[::-1]), jnp.stack(bias_sums[::-1])])
    small = (small + swap(small, 1)).reshape(4 * layers, width)
    small = restore(offsets, shuffle, small)
    small = small.reshape(4 * layers, tm_size, slices).transpose(1, 0, 2)
    small = jnp.sum(spread(small), axis=0).reshape(2, layers, 2, slices)
    input_grad = restore(offsets, shuffle, upstream)
    return (
        outputs,
        all_rows(input_grad),
        jnp.stack(qkv_grads[::-1]),
        jnp.stack([grad.T for grad in out_grads[::-1]]),
        jnp.stack(up_grads[::-1]),
        jnp.stack([grad.T for grad in down_grads[::-1]]),
        small[0],
        small[1],
    )


def solution(mesh):
    placed = (
        P("tm", None, None),
        P(None, "tm", None, "head"),
        P(None, "head", "tm"),
        P(None, "tm", "head"),
        P(None, "head", "tm"),
        P(None, None, "tm"),
        P(None, None, "tm"),
        P("tm", None),
        P(None, "tm", None),
        P("tm", None, None),
    )
    return jax.shard_map(
        body,
        mesh=mesh,
        in_specs=placed,
        out_specs=(
            P("tm", None, None),
            P("tm", None, None),
            P(None, "tm", None, "head"),
            P(None, "head", "tm"),
            P(None, "tm", "head"),
            P(None, "head", "tm"),
            P(None, None, "tm"),
            P(None, None, "tm"),
        ),
        check_vma=False,
    )
```

```python
import functools

import jax
import jax.numpy as jnp
from jax import lax
from jax.experimental import pallas as pl
from jax.experimental.pallas import tpu as pltpu
from jax.sharding import PartitionSpec as P

HEAD_DIM = 64
PAIR = 2 * HEAD_DIM
GROUP = HEAD_DIM // 6
NEG_BIG = -1e30
F32 = jnp.float32
BF16 = jnp.bfloat16
NT = (((1,), (1,)), ((), ()))
TN = (((0,), (0,)), ((), ()))
NN = (((1,), (0,)), ((), ()))


def dot(left, right, dims):
    return lax.dot_general(left, right, dims, preferred_element_type=F32)


def rotary_tables(coordinates):
    lane = jnp.arange(PAIR, dtype=jnp.int32) % HEAD_DIM
    group = jnp.minimum(lane // (2 * GROUP), 2)
    place = lane % (2 * GROUP)
    turned = lane < 6 * GROUP
    first = turned & (place < GROUP)
    second = turned & (place >= GROUP)
    inverse = 10000.0 ** (-(place % GROUP).astype(F32) / GROUP)
    spread = jnp.where(
        group == 0,
        coordinates[:, 0:1],
        jnp.where(group == 1, coordinates[:, 1:2], coordinates[:, 2:3]),
    )
    angles = spread * inverse
    cosine = jnp.where(turned, jnp.cos(angles), 1.0)
    sine = jnp.sin(angles)
    return (cosine, jnp.where(first, -sine, 0.0), jnp.where(second, sine, 0.0))


def turn(values, cosine, sine_first, sine_second):
    ahead = pltpu.roll(values, PAIR - GROUP, 1)
    behind = pltpu.roll(values, GROUP, 1)
    return values * cosine + ahead * sine_first + behind * sine_second


def turn_back(values, cosine, sine_first, sine_second):
    ahead = pltpu.roll(values, PAIR - GROUP, 1)
    behind = pltpu.roll(values, GROUP, 1)
    return values * cosine - ahead * sine_first - behind * sine_second


def project_kernel(own, peer, left, right, cosine, sine_first, sine_second, out):
    rows = out.shape[2]
    width = out.shape[1] * PAIR
    middle = left.shape[0]
    for step, acts in enumerate((own, peer)):
        span = pl.ds(step * 2 * rows, 2 * rows)
        raw = dot(acts[:, :middle], left[:, : 3 * width], NN)
        raw += dot(acts[:, middle:], right[:, : 3 * width], NN)
        tables = (cosine[span, :], sine_first[span, :], sine_second[span, :])
        for pair in range(out.shape[1]):
            for part in range(3):
                start = part * width + pair * PAIR
                piece = raw[:, start : start + PAIR]
                if part < 2:
                    piece = turn(piece, *tables)
                piece = piece.astype(BF16)
                for half in range(2):
                    out[2 * step + half, pair, :, part * PAIR : (part + 1) * PAIR] = piece[
                        half * rows : (half + 1) * rows
                    ]


def unit_rows(tiles, micros, pairs, lanes):
    return jnp.concatenate(
        [
            jnp.concatenate([tiles[micro * pairs + pair, :, lanes] for pair in range(pairs)], axis=1)
            for micro in micros
        ],
        axis=0,
    )


def mix_kernel(pairs, mixed, left, right, theirs, mine):
    width = pairs * PAIR
    micro = mixed.shape[0] // pairs
    middle = left.shape[0]
    skip = left.shape[1] - width
    for micros, out in ((range(micro // 2, micro), theirs), (range(micro // 2), mine)):
        rows = unit_rows(mixed, micros, pairs, slice(0, PAIR))
        out[:, :middle] = dot(rows, left[:, skip:], NT).astype(out.dtype)
        out[:, middle:] = dot(rows, right[:, skip:], NT).astype(out.dtype)


def unmix_kernel(own, peer, left, right, out):
    rows = out.shape[2]
    width = out.shape[1] * PAIR
    middle = left.shape[0]
    skip = left.shape[1] - width
    for step, acts in enumerate((own, peer)):
        raw = dot(acts[:, :middle], left[:, skip:], NN) + dot(acts[:, middle:], right[:, skip:], NN)
        raw = raw.astype(BF16)
        for pair in range(out.shape[1]):
            for half in range(2):
                out[2 * step + half, pair] = raw[
                    half * rows : (half + 1) * rows, pair * PAIR : (pair + 1) * PAIR
                ]


def unproject_kernel(pairs, packed, left, right, theirs, mine):
    width = pairs * PAIR
    micro = packed.shape[0] // pairs
    middle = left.shape[0]
    for micros, out in ((range(micro // 2, micro), theirs), (range(micro // 2), mine)):
        for weights, place in ((left, slice(0, middle)), (right, slice(middle, 2 * middle))):
            total = 0.0
            for part in range(3):
                rows = unit_rows(packed, micros, pairs, slice(part * PAIR, (part + 1) * PAIR))
                total += dot(rows, weights[:, part * width : (part + 1) * width], NT)
            out[:, place] = total.astype(out.dtype)


def up_kernel(own, peer, left, right, activated, slope):
    middle = left.shape[0]
    half = own.shape[0]
    for start in range(0, activated.shape[1], 256):
        block = slice(start, start + 256)
        for step, acts in enumerate((own, peer)):
            upward = dot(acts[:, :middle], left[:, block], NN)
            upward += dot(acts[:, middle:], right[:, block], NN)
            bell = 0.5 * (1.0 + lax.erf(upward * 0.7071067811865476))
            span = slice(step * half, (step + 1) * half)
            activated[span, block] = (upward * bell).astype(BF16)
            slope[span, block] = (
                bell + upward * jnp.exp(-0.5 * upward * upward) * 0.3989422804014327
            )


def down_kernel(activated, left, right, theirs, mine):
    half = mine.shape[0]
    middle = left.shape[1]
    for span, out in ((slice(half, 2 * half), theirs), (slice(0, half), mine)):
        out[:, :middle] = dot(activated[span, :], left[...], NN).astype(out.dtype)
        out[:, middle:] = dot(activated[span, :], right[...], NN).astype(out.dtype)


def dense_back_kernel(own, peer, up_left, up_right, down_left, down_right, slope, inner, theirs, mine):
    half = mine.shape[0]
    middle = up_left.shape[0]
    for acts, span, out in (
        (peer, slice(half, 2 * half), theirs),
        (own, slice(0, half), mine),
    ):
        raw = dot(acts[:, :middle], down_left[...], NT)
        raw += dot(acts[:, middle:], down_right[...], NT)
        grad = (raw * slope[span, :]).astype(BF16)
        inner[span, :] = grad
        out[:, :middle] = dot(grad, up_left[...], NT).astype(out.dtype)
        out[:, middle:] = dot(grad, up_right[...], NT).astype(out.dtype)


def pair_kernel(mine, come, total):
    total[...] = (mine[...] + come[...].astype(F32)).astype(BF16)


def normalized(hidden, gain, bias):
    centered = hidden - jnp.mean(hidden, axis=-1, keepdims=True)
    root = lax.rsqrt(jnp.mean(centered * centered, axis=-1, keepdims=True) + 1e-06)
    normed = centered * root
    return normed, root, (normed * gain + bias).astype(BF16)


def first_norm_kernel(gain, bias, hidden, vectors, normed, root, out):
    normed[...], scale, out[...] = normalized(
        hidden[...], vectors[gain : gain + 1, :], vectors[bias : bias + 1, :]
    )
    root[...] = jnp.broadcast_to(scale, root.shape)


def norm_kernel(gain, bias, hidden, total, come, vectors, result, normed, root, out):
    value = hidden[...] + (total[...].astype(F32) + come[...].astype(F32))
    result[...] = value
    normed[...], scale, out[...] = normalized(
        value, vectors[gain : gain + 1, :], vectors[bias : bias + 1, :]
    )
    root[...] = jnp.broadcast_to(scale, root.shape)


def norm_back_kernel(gain, total, come, normed, root, vectors, upstream, result, out, sums):
    grad = total[...].astype(F32) + come[...].astype(F32)
    known = normed[...]
    sums[0:1, :] = jnp.sum(grad * known, axis=0, keepdims=True)
    sums[1:2, :] = jnp.sum(grad, axis=0, keepdims=True)
    scaled = grad * vectors[gain : gain + 1, :]
    value = upstream[...] + root[:, 0:1] * (
        scaled
        - jnp.mean(scaled, axis=-1, keepdims=True)
        - known * jnp.mean(scaled * known, axis=-1, keepdims=True)
    )
    result[...] = value
    out[...] = value.astype(BF16)


def quarter_of(own, peer, quarter):
    size = own.shape[1] // 4
    span = slice(quarter * size, (quarter + 1) * size)
    return jnp.concatenate([own[:, span], peer[:, span]], axis=0)


def up_products(quarter, own, peer, inner):
    rows = quarter_of(own, peer, quarter)
    for start in range(0, inner.shape[1], 256):
        span = slice(start, start + 256)
        yield (slice(None), span), dot(rows, inner[:, span], TN)


def down_products(quarter, own, peer, activated):
    rows = quarter_of(own, peer, quarter)
    for start in range(0, activated.shape[1], 256):
        span = slice(start, start + 256)
        yield (span, slice(None)), dot(activated[:, span], rows, TN)


def projection_products(pairs, parts, quarter, own, peer, packed):
    rows = quarter_of(own, peer, quarter)
    micros = range(packed.shape[0] // pairs)
    for place, part in enumerate(parts):
        other = unit_rows(packed, micros, pairs, slice(part * PAIR, (part + 1) * PAIR))
        span = slice(place * pairs * PAIR, (place + 1) * pairs * PAIR)
        yield (slice(None), span), dot(rows, other, TN)


def mix_products(pairs, start, quarter, own, peer, mixed):
    rows = quarter_of(own, peer, quarter)
    micros = range(mixed.shape[0] // pairs)
    other = unit_rows(mixed, micros, pairs, slice(0, PAIR))
    yield (slice(None), slice(start, start + pairs * PAIR)), dot(rows, other, TN)


def attention_products(pairs, quarter, own, peer, packed, grad_own, grad_peer, mixed):
    yield from projection_products(pairs, range(3), quarter, own, peer, packed)
    yield from mix_products(pairs, 3 * pairs * PAIR, quarter, grad_own, grad_peer, mixed)


def far_kernel(products, *refs):
    for quarter, out in ((2, refs[-2]), (3, refs[-1])):
        for place, value in products(quarter, *refs[:-2]):
            out[place] = value.astype(BF16)


def send_kernel(products, *refs):
    arrived, out = refs[-2:]
    for place, value in products(1, *refs[:-2]):
        out[place] = (value + arrived[place].astype(F32)).astype(BF16)


def keep_kernel(products, axis, *refs):
    arrived, folded, keep, send = refs[-4:]
    half = keep.shape[axis]
    for place, value in products(0, *refs[:-4]):
        value = value + arrived[place].astype(F32) + folded[place].astype(F32)
        if axis:
            keep[place] = value[:, :half]
            send[place] = value[:, half:].astype(BF16)
        else:
            keep[place] = value[:half]
            send[place] = value[half:].astype(BF16)


def lane_mask(shape, head):
    lane = lax.broadcasted_iota(jnp.int32, shape, 1)
    return (lane >= head * HEAD_DIM) & (lane < (head + 1) * HEAD_DIM)


def visible_bias(key_frames, query_frames, block):
    spread = jnp.concatenate([key_frames] * (block // key_frames.shape[1]), axis=1)
    return spread <= query_frames


def attend_kernel(block, start, qkv, key_frames, query_frames, out, out_t, lse):
    key_vecs = qkv[:, PAIR : 2 * PAIR]
    value_t = jnp.transpose(qkv[:, 2 * PAIR :].astype(F32)).astype(BF16)
    query_rows = out.shape[0]

    def one(step, carry):
        place = pl.multiple_of(step * block, block)
        source = pl.multiple_of(start[0] + step * block, block)
        queries = qkv[pl.ds(source, block), :PAIR] * jnp.asarray(HEAD_DIM**-0.5, BF16)
        seen = visible_bias(key_frames[...], query_frames[:, pl.ds(source, block)], block)
        pieces = []
        for head in range(2):
            mine = jnp.where(lane_mask(queries.shape, head), queries, jnp.zeros_like(queries))
            scores = jnp.where(seen, dot(key_vecs, mine, NT), NEG_BIG)
            top = jnp.max(scores, axis=0, keepdims=True)
            raised = jnp.exp(scores - top)
            total = jnp.sum(raised, axis=0, keepdims=True)
            summed = dot(
                value_t[head * HEAD_DIM : (head + 1) * HEAD_DIM], raised.astype(BF16), NN
            )
            pieces.append(summed / total)
            lse[head : head + 1, pl.ds(place, block)] = top + jnp.log(total)
        both = jnp.concatenate(pieces, axis=0)
        out_t[:, pl.ds(place, block)] = both
        out[pl.ds(place, block), :] = jnp.transpose(both).astype(BF16)
        return carry

    lax.fori_loop(0, query_rows // block, one, 0)


def attend_back_kernel(
    block,
    start,
    qkv,
    grad_out,
    out_t,
    lse,
    key_frames,
    query_frames,
    cosine,
    sine_first,
    sine_second,
    result,
    key_sum,
    value_sum,
):
    key_vecs = qkv[:, PAIR : 2 * PAIR]
    value_vecs = qkv[:, 2 * PAIR :]
    key_t = jnp.transpose(key_vecs.astype(F32)).astype(BF16)
    query_rows = grad_out.shape[0]
    key_sum[...] = jnp.zeros_like(key_sum)
    value_sum[...] = jnp.zeros_like(value_sum)
    if query_rows != qkv.shape[0]:
        result[:, :PAIR] = jnp.zeros((qkv.shape[0], PAIR), BF16)

    def one(step, carry):
        place = pl.multiple_of(step * block, block)
        source = pl.multiple_of(start[0] + step * block, block)
        queries = qkv[pl.ds(source, block), :PAIR] * jnp.asarray(HEAD_DIM**-0.5, BF16)
        upstream = grad_out[pl.ds(place, block), :]
        seen = visible_bias(key_frames[...], query_frames[:, pl.ds(source, block)], block)
        both = out_t[:, pl.ds(place, block)] * jnp.transpose(upstream.astype(F32))
        pieces = []
        for head in range(2):
            keep = lane_mask(queries.shape, head)
            mine = jnp.where(keep, queries, jnp.zeros_like(queries))
            above = jnp.where(keep, upstream, jnp.zeros_like(upstream))
            rows = slice(head * HEAD_DIM, (head + 1) * HEAD_DIM)
            delta = jnp.sum(both[rows], axis=0, keepdims=True)
            log_total = lse[head : head + 1, pl.ds(place, block)]
            weights = jnp.where(seen, jnp.exp(dot(key_vecs, mine, NT) - log_total), 0.0)
            slope = (weights * (dot(value_vecs, above, NT) - delta)).astype(BF16)
            value_sum[...] += dot(weights.astype(BF16), above, NN)
            key_sum[...] += dot(slope, mine, NN)
            pieces.append(dot(key_t[rows], slope, NN))
        query_grad = jnp.transpose(jnp.concatenate(pieces, axis=0)) * HEAD_DIM**-0.5
        span = pl.ds(source, block)
        result[span, :PAIR] = turn_back(
            query_grad, cosine[span, :], sine_first[span, :], sine_second[span, :]
        ).astype(BF16)
        return carry

    lax.fori_loop(0, query_rows // block, one, 0)
    result[:, PAIR : 2 * PAIR] = turn_back(
        key_sum[...], cosine[...], sine_first[...], sine_second[...]
    ).astype(BF16)
    result[:, 2 * PAIR :] = value_sum[...].astype(BF16)


def whole():
    return pl.BlockSpec(memory_space=pltpu.VMEM)


def scalars():
    return pl.BlockSpec(memory_space=pltpu.SMEM)


def call(kernel, outs, name, *operands, numbers=(), scratch=(), scale=1, away=False):
    shapes = [(jax.ShapeDtypeStruct if away else pltpu.VMEM)(shape, kind) for shape, kind in outs]
    memory = pltpu.HBM if away else pltpu.VMEM
    operands = [pltpu.with_memory_space_constraint(operand, memory) for operand in operands]
    single = len(shapes) == 1
    return pl.pallas_call(
        kernel,
        out_shape=shapes[0] if single else shapes,
        in_specs=[scalars()] * len(numbers) + [whole()] * len(operands),
        out_specs=whole() if single else [whole()] * len(shapes),
        scratch_shapes=scratch,
        compiler_params=pltpu.CompilerParams(vmem_limit_bytes=scale * 10 * 1024 * 1024),
        name=name,
    )(*numbers, *operands)


def call_window(kernel, outs, name, operands, weights, width, index):
    shapes = [jax.ShapeDtypeStruct(shape, kind) for shape, kind in outs]

    def full(shape):
        return pl.BlockSpec(shape, lambda i: (0,) * len(shape))

    single = len(shapes) == 1
    specs = [full(shape) for shape, kind in outs]
    return pl.pallas_call(
        kernel,
        grid=(1,),
        out_shape=shapes[0] if single else shapes,
        in_specs=[full(operand.shape) for operand in operands]
        + [pl.BlockSpec((part.shape[0], width), lambda i: (0, index)) for part in weights],
        out_specs=specs[0] if single else specs,
        compiler_params=pltpu.CompilerParams(vmem_limit_bytes=10 * 1024 * 1024),
        name=name,
    )(*operands, *weights)


def attend(start, qkv, key_frames, query_frames, query_rows):
    return call(
        functools.partial(attend_kernel, 256),
        [((query_rows, PAIR), BF16), ((PAIR, query_rows), F32), ((2, query_rows), F32)],
        "attend",
        qkv,
        key_frames,
        query_frames,
        numbers=(start,),
        scale=max(2, 2 * qkv.shape[0] // 1024),
        away=True,
    )


def attend_back(start, qkv, grad_out, out_t, lse, key_frames, query_frames, tables):
    return call(
        functools.partial(attend_back_kernel, 256),
        [(qkv.shape, BF16)],
        "attend_back",
        qkv,
        grad_out,
        out_t,
        lse,
        key_frames,
        query_frames,
        *tables,
        numbers=(start,),
        scratch=[pltpu.VMEM((qkv.shape[0], PAIR), F32)] * 2,
        scale=max(2, 2 * qkv.shape[0] // 1024),
        away=True,
    )


def restore_kernel(places, values, out):
    size = values.shape[1] // places.shape[0]
    for block in range(places.shape[0]):
        place = pl.multiple_of(places[block], size)
        out[:, pl.ds(place, size)] = values[:, block * size : (block + 1) * size]


def restore(places, shuffle, values):
    if values.shape[1] // places.shape[0] % 128 == 0:
        return call(restore_kernel, [(values.shape, values.dtype)], "restore", values, numbers=(places,))
    exact = lax.Precision.HIGHEST
    return lax.dot_general(
        values.astype(F32), shuffle.astype(F32), NT, precision=exact
    ).astype(values.dtype)


def body(
    inputs,
    qkv_master,
    out_master,
    up_master,
    down_master,
    norm_gain,
    norm_bias,
    frame_ids,
    patch_pos,
    cotangent,
):
    rows, micro, width = inputs.shape
    tm_size = lax.axis_size("tm")
    head_size = lax.axis_size("head")
    here = lax.axis_index("tm")
    layers = qkv_master.shape[0]
    columns = qkv_master.shape[3]
    hidden_units = up_master.shape[2]
    slices = width // tm_size
    half = micro // 2
    half_rows = half * rows
    odd = lax.axis_index("head") % 2
    pairs = columns // PAIR
    units = micro * pairs
    repeats = tm_size // units
    tokens = rows * tm_size
    query_rows = tokens // repeats

    bits = []
    order = [0]
    bit = tm_size // 2
    while bit:
        bits.append(bit)
        order = order + [place | bit for place in order]
        bit //= 2
    last = bits[-1]

    def sync(*values):
        return lax.optimization_barrier(values)

    def tie(value, *others):
        return sync(value, others)[0]

    def hop(values, bit):
        return lax.ppermute(values, "tm", [(i, i ^ bit) for i in range(tm_size)])

    def swap(values, bit):
        return lax.ppermute(values, "head", [(i, i ^ bit) for i in range(head_size)])

    half_shape = (half_rows, width)
    sums = [(half_shape, BF16), (half_shape, F32)]

    def sum_heads(theirs, mine):
        total = call(pair_kernel, [(half_shape, BF16)], "pair", mine, swap(theirs, 1))
        bit = 2
        while 2 * bit < head_size:
            total = sync((total.astype(F32) + swap(total, bit).astype(F32)).astype(BF16))[0]
            bit *= 2
        return total, swap(total, bit)

    def exchange(values):
        return lax.all_to_all(values, "tm", 0, 0, tiled=True)

    def grow(held, axis=0):
        return jnp.concatenate([held, hop(held, bits[0])], axis=axis)

    def reach(held, axis=0):
        pieces = [held]
        for bit in bits[1:-1]:
            so_far = jnp.concatenate(pieces, axis=axis) if len(pieces) > 1 else held
            pieces.append(hop(so_far, bit))
        return pieces

    def stack(pieces, axis=0):
        return jnp.concatenate(pieces, axis=axis)

    def fold(parts, axis=0):
        keep, send = parts
        for bit in bits[-3::-1]:
            total = keep + hop(send, bit).astype(F32)
            if bit == bits[0]:
                return total
            keep, send = jnp.split(total, 2, axis=axis)
            send = send.astype(BF16)

    def own_rows(values, shuffle):
        mine = lax.dynamic_slice_in_dim(values, half * odd, half, 1)
        mine = jnp.transpose(mine, (1, 0, 2)).reshape(half_rows, width)
        return dot(mine, shuffle, NN)

    def to_units(values):
        return jnp.repeat(values, repeats, axis=0) if repeats > 1 else values

    def from_units(values):
        if repeats == 1:
            return values
        grouped = values.reshape((units, repeats) + values.shape[1:]).astype(F32)
        return jnp.sum(grouped, axis=1).astype(BF16)

    def attention_shard(qkv_part, out_part):
        return jnp.concatenate(
            [qkv_part.astype(BF16).reshape(slices, 3 * columns), out_part.astype(BF16).T], axis=1
        )

    pieces = {0: attention_shard(qkv_master[0], out_master[0])}
    for bit in bits:
        pieces[bit] = hop(pieces[0], bit)

    ordered = (jnp.arange(micro) + half * odd) % micro
    whole_numbers = jnp.concatenate([frame_ids[None], patch_pos], axis=0).astype(F32)
    whole_numbers = jnp.take(jnp.transpose(whole_numbers, (2, 0, 1)), ordered, axis=0)
    vectors = jnp.concatenate([norm_gain, norm_bias], axis=0).astype(BF16).astype(F32)
    parcel = jnp.concatenate(
        [
            jnp.broadcast_to(vectors.reshape(1, -1), (tm_size, vectors.size)),
            jnp.repeat(whole_numbers.reshape(micro, 3 * rows), tm_size // micro, axis=0),
        ],
        axis=1,
    )
    parcel = exchange(parcel)

    early = [pieces.pop(bit) for bit in bits[:-1]]
    masters = (qkv_master, out_master, up_master, down_master)
    early, inputs, whole_numbers, here, masters = sync(
        early, inputs, whole_numbers, here, masters
    )
    qkv_master, out_master, up_master, down_master = masters
    attention_held = [
        attention_shard(qkv_master[layer], out_master[layer]) for layer in range(layers)
    ]
    up_held = [up_master[layer].astype(BF16) for layer in range(layers)]
    down_held = [down_master[layer].astype(BF16) for layer in range(layers)]
    up, down = up_held[0], down_held[0]
    pieces.update(zip(bits[:-1], early))
    for bit in bits:
        if bit == last:
            parcel, pieces[sum(bits[:-1])] = sync(parcel, pieces[sum(bits[:-1])])
        for place in [place for place in order if place and place & (bit - 1) == 0]:
            if place & bit and place not in pieces:
                pieces[place] = hop(pieces[place ^ bit], bit)
    up = grow(up)
    down = grow(down, 1)
    feature = jnp.arange(width, dtype=jnp.int32)
    origin = (here ^ jnp.asarray(order, jnp.int32)[:, None]) * slices + jnp.arange(
        slices, dtype=jnp.int32
    )
    offsets = origin[:, 0]
    shuffle = (feature[:, None] == origin.reshape(1, width)).astype(BF16)
    vectors = parcel[:, : vectors.size].reshape(tm_size, 4 * layers, slices)
    vectors = jnp.transpose(vectors, (1, 0, 2)).reshape(4 * layers, width).astype(BF16)
    vectors = dot(vectors, shuffle, NN)
    places = parcel[:, -3 * rows :].reshape(tm_size, 3, rows)
    places = jnp.transpose(places, (1, 0, 2)).reshape(3, tokens)
    query_frames = places[0:1]
    row_tables = rotary_tables(jnp.transpose(whole_numbers, (0, 2, 1)).reshape(micro * rows, 3))
    start = ((here % repeats) * query_rows).reshape(1)

    hidden = own_rows(inputs, shuffle)
    root_shape = (half_rows, 128)
    norm_outs = [(half_shape, F32), (root_shape, F32), (half_shape, BF16)]

    def row_of(layer, which):
        return 2 * layer + which, 2 * layers + 2 * layer + which

    def norm(layer, which, hidden, total, come):
        return call(
            functools.partial(norm_kernel, *row_of(layer, which)),
            [(half_shape, F32)] + norm_outs,
            "norm",
            hidden,
            total,
            come,
            vectors,
        )

    normed_one, root_one, first_own = call(
        functools.partial(first_norm_kernel, *row_of(0, 0)), norm_outs, "first_norm", hidden, vectors
    )
    key_frames = jnp.broadcast_to(places[0][:, None], (tokens, 128))
    first_own, pieces = sync(first_own, pieces)
    first_own, attention_held[1:], key_frames = sync(first_own, attention_held[1:], key_frames)
    attention_w = tuple(
        stack([pieces[place] for place in places_of])
        for places_of in (order[: tm_size // 2], order[tm_size // 2 :])
    )
    stored = []
    weights = []
    for layer in range(layers):
        more = layer + 1 < layers
        first_in = (first_own, swap(first_own, 1))
        first_in, attention_w, up, down = sync(first_in, attention_w, up, down)
        packed = call(
            project_kernel,
            [((micro, pairs, rows, 3 * PAIR), BF16)],
            "project",
            *first_in,
            *attention_w,
            *row_tables,
        )
        packed = to_units(packed.reshape(units, rows, 3 * PAIR))
        qkv = exchange(packed).reshape(tokens, 3 * PAIR)
        if layer == 0:
            up = reach(up)
            sequence_tables = rotary_tables(places.T)
            qkv, sequence_tables = sync(qkv, sequence_tables)
            down_far = [hop(down, last)]
        else:
            down_far = []
        up_far = [hop(up[0], last)]
        qkv, up_far, down, down_far = sync(qkv, up_far, down, down_far)
        down = reach(down, 1)
        if layer:
            up_far = up_far + [hop(piece, last) for piece in tie(up[1:], qkv)]
        if more:
            coming = grow(tie(attention_held[layer + 1], qkv))
        mixed, mixed_t, lse = attend(start, qkv, key_frames, query_frames, query_rows)
        if repeats > 1:
            mixed = lax.dynamic_update_slice_in_dim(
                jnp.zeros((tokens, PAIR), BF16), mixed, start[0], 0
            )
        mixed, up_far, up = sync(mixed, up_far, up)
        if more:
            mixed, coming = sync(mixed, coming)
        mixed = from_units(exchange(mixed.reshape(tm_size, rows, PAIR)))
        if layer:
            down_far = [hop(down[0], last)]
        else:
            up_far = up_far + [hop(piece, last) for piece in up[1:]]
        mixed, up_far, down_far, down = sync(mixed, up_far, down_far, down)
        theirs, mine = call_window(
            functools.partial(mix_kernel, pairs), sums, "mix", (mixed,), attention_w, columns, 3
        )
        total, come = sum_heads(theirs, mine)
        down_far = down_far + [hop(piece, last) for piece in down[1:]]
        up_w = (stack(up), stack(up_far))
        if more:
            coming, next_up = tie((coming, up_held[layer + 1]), mixed)
            coming_far = [hop(coming, last)]
            coming = reach(coming)
            next_up = grow(next_up)
            come = tie(come, coming, next_up)
        come = tie(come, up_w)
        middle, normed_two, root_two, second_own = norm(layer, 1, hidden, total, come)
        second_in = (second_own, swap(second_own, 1))
        activated, slope = call(
            up_kernel,
            [((micro * rows, hidden_units), BF16), ((micro * rows, hidden_units), F32)],
            "up_project",
            *second_in,
            *up_w,
        )
        down_w = (stack(down, 1), stack(down_far, 1))
        activated = tie(activated, down_w)
        if more:
            theirs, mine = call(down_kernel, sums, "down_project", activated, *down_w)
            theirs = tie(theirs, coming_far)
            total, come = sum_heads(theirs, mine)
            coming_far = coming_far + [hop(piece, last) for piece in coming[1:]]
            next_up, next_down = tie((next_up, down_held[layer + 1]), second_in)
            next_up = reach(next_up)
            next_down = grow(next_down, 1)
            attention_next = (stack(coming), stack(coming_far))
            come = tie(come, next_up, next_down, attention_next)
        stored.append(
            (
                normed_one,
                root_one,
                first_in,
                qkv,
                mixed,
                mixed_t,
                lse,
                normed_two,
                root_two,
                second_in,
                activated,
                slope,
            )
        )
        weights.append((attention_w, up_w, down_w))
        if more:
            hidden, normed_one, root_one, first_own = norm(layer + 1, 0, middle, total, come)
            attention_w = attention_next
            up, down = next_up, next_down

    def all_rows(mine, other):
        ours = jnp.concatenate([mine, other], axis=0).reshape(micro, rows, width)
        return jnp.transpose(jnp.roll(ours, half * odd, axis=0), (1, 0, 2))

    def final(middle, activated, down_w):
        total, come = sum_heads(*call(down_kernel, sums, "down_project", activated, *down_w))
        result = middle + (total.astype(F32) + come.astype(F32))
        result = restore(offsets, shuffle, result.astype(BF16))
        return all_rows(result, swap(result, 1))

    class Gradient:
        def __init__(self, products, span, axis, name, *sources):
            self.products, self.axis, self.name, self.sources = products, axis, name, sources
            self.shape = (span, width // 4) if axis else (width // 4, span)
            self.ends = (span, width // 8) if axis else (width // 8, span)
            self.far = None

        def start(self, away=False):
            self.far = call(
                functools.partial(far_kernel, self.products),
                [(self.shape, BF16)] * 2,
                self.name + "_far",
                *self.sources,
                away=away,
            )

        def hop_second(self):
            self.second = hop(self.far[1], last)

        def hop_first(self):
            self.first = hop(self.far[0], last)

        def send(self, away=False):
            self.sent = call(
                functools.partial(send_kernel, self.products),
                [(self.shape, BF16)],
                self.name + "_send",
                *self.sources,
                self.second,
                away=away,
            )

        def hop_sent(self):
            self.sent = hop(self.sent, bits[-2])

        def keep(self, away=False):
            self.kept = call(
                functools.partial(keep_kernel, self.products, self.axis),
                [(self.ends, F32), (self.ends, BF16)],
                self.name + "_keep",
                *self.sources,
                self.first,
                self.sent,
                away=away,
            )

        def hop_kept(self):
            self.kept = fold(self.kept, self.axis)

    upstream = own_rows(cotangent, shuffle)
    grad_own = upstream.astype(BF16)
    back_outs = [(half_shape, F32), (half_shape, BF16), ((2, width), F32)]

    def norm_back(layer, which, total, come, normed, root, upstream):
        return call(
            functools.partial(norm_back_kernel, row_of(layer, which)[0]),
            back_outs,
            "norm_back",
            total,
            come,
            normed,
            root,
            vectors,
            upstream,
        )

    vector_sums = {}
    up_grads, down_grads, qkv_grads, out_grads = [], [], [], []
    late_attention = late_up = None
    for layer in reversed(range(layers)):
        attention_w, up_w, down_w = weights[layer]
        (
            normed_one,
            root_one,
            first_in,
            qkv,
            mixed,
            mixed_t,
            lse,
            normed_two,
            root_two,
            second_in,
            activated,
            slope,
        ) = stored[layer]
        ending = layer == 0
        late = late_attention is not None
        grad_mlp = (grad_own, swap(grad_own, 1))
        if late:
            late_attention.hop_first()
        down = Gradient(down_products, hidden_units, 1, "down", *grad_mlp, activated)
        down.start()
        down.hop_second()
        grad_mlp = tie(grad_mlp, down.far)
        inner, theirs, mine = call(
            dense_back_kernel,
            [((micro * rows, hidden_units), BF16)] + sums,
            "dense_back",
            *grad_mlp,
            *up_w,
            *down_w,
            slope,
        )
        if late:
            theirs = tie(theirs, late_attention.first)
        total, come = sum_heads(theirs, mine)
        up = Gradient(up_products, hidden_units, 0, "up", *second_in, inner)
        up.start()
        come = tie(come, up.far, down.second)
        if late:
            late_attention.send()
            late_attention.hop_sent()
            late_up.keep()
            come = tie(come, late_up.kept)
            come = tie(come, late_attention.sent)
        upstream, grad_own, vector_sums[layer, 1] = norm_back(
            layer, 1, total, come, normed_two, root_two, upstream
        )
        grad_attn = (grad_own, swap(grad_own, 1))
        grad_mixed = call_window(
            unmix_kernel,
            [((micro, pairs, rows, PAIR), BF16)],
            "unmix",
            grad_attn,
            attention_w,
            columns,
            3,
        )
        down.second = tie(down.second, grad_mixed)
        grad_mixed = to_units(grad_mixed.reshape(units, rows, PAIR))
        grad_mixed = exchange(grad_mixed).reshape(tokens, PAIR)
        if repeats > 1:
            grad_mixed = lax.dynamic_slice_in_dim(grad_mixed, start[0], query_rows, 0)
        down.send(True)
        down.far = tie(down.far, down.second)
        down.hop_first()
        grad_mixed = tie(grad_mixed, down.sent, down.first)
        if ending:
            out = Gradient(
                functools.partial(mix_products, pairs, 0), columns, 0, "out", *grad_attn, mixed
            )
            out.start(True)
            grad_mixed = tie(grad_mixed, out.far)
        if late:
            late_attention.keep(True)
            grad_mixed = tie(grad_mixed, late_attention.kept)
            late_up.kept = tie(late_up.kept, down.sent)
            late_up.hop_kept()
            late_attention.kept = tie(late_attention.kept, grad_mixed)
            late_attention.hop_kept()
        down.sent, up.far = tie((down.sent, up.far), grad_mixed)
        down.hop_sent()
        up.hop_second()
        packed_grad = attend_back(
            start, qkv, grad_mixed, mixed_t, lse, key_frames, query_frames, sequence_tables
        )
        packed_grad = tie(packed_grad, down.sent, up.second)
        if late:
            packed_grad = tie(packed_grad, late_attention.kept, late_up.kept)
            up_grads.append(late_up.kept)
            attention_grad = late_attention.kept
            qkv_grads.append(attention_grad[:, : 3 * columns].reshape(slices, 3, columns))
            out_grads.append(attention_grad[:, 3 * columns :])
        if layer + 1 == layers:
            middle, last_in = tie((middle, activated), packed_grad)
            outputs = final(middle, last_in, down_w)
        down.first, up.second, up.far = tie((down.first, up.second, up.far), packed_grad)
        packed_grad = from_units(exchange(packed_grad.reshape(tm_size, rows, 3 * PAIR)))
        down.keep(True)
        up.send(True)
        up.hop_first()
        packed_grad = tie(packed_grad, down.kept, up.sent, up.first)
        if ending:
            out.far = tie(out.far, down.first)
            out.hop_second()
            out.hop_first()
            down.hop_kept()
            packed_grad = tie(packed_grad, out.first, out.second, outputs, down.kept)
        if not ending:
            down.kept = tie(down.kept, packed_grad)
        up.sent = tie(up.sent, packed_grad)
        if ending:
            products = functools.partial(projection_products, pairs, range(3))
            group = Gradient(products, 3 * columns, 0, "qkv", *first_in, packed_grad)
            group.start()
            group.hop_second()
            group.hop_first()
            packed_grad = tie(packed_grad, group.far)
        theirs, mine = call(
            functools.partial(unproject_kernel, pairs),
            sums,
            "unproject",
            packed_grad,
            *attention_w,
        )
        total, come = sum_heads(theirs, mine)
        if not ending:
            down.hop_kept()
        up.hop_sent()
        down_grads.append(down.kept)
        if ending:
            out.second = tie(out.second, theirs)
            out.send()
            out.hop_sent()
            come = tie(come, group.second, up.sent, out.sent)
            group.second, up.sent, out.sent = tie((group.second, up.sent, out.sent), come)
            group.send()
            up.keep()
            out.keep()
            come = tie(come, group.sent, up.kept, out.kept)
            group.hop_sent()
            up.hop_kept()
            out.hop_kept()
        else:
            late_attention = Gradient(
                functools.partial(attention_products, pairs),
                4 * columns,
                0,
                "attention",
                *first_in,
                packed_grad,
                *grad_attn,
                mixed,
            )
            late_attention.start()
            late_attention.hop_second()
            come = tie(come, down.kept, up.sent, late_attention.second)
        late_up = up
        upstream, grad_own, vector_sums[layer, 0] = norm_back(
            layer, 0, total, come, normed_one, root_one, upstream
        )
    restored = restore(offsets, shuffle, upstream)
    restored = (restored, swap(restored, 1))
    group.first = tie(group.first, restored, up.kept, out.kept)
    group.keep()
    restored, vector_sums, done = tie(
        (restored, vector_sums, (up_grads, down_grads, out_grads, qkv_grads, up.kept, out.kept)),
        group.kept,
    )
    up_grads, down_grads, out_grads, qkv_grads, up.kept, out.kept = done
    group.hop_kept()
    up_grads.append(up.kept)
    out_grads.append(out.kept)
    qkv_grads.append(group.kept.reshape(slices, 3, columns))
    names = [(layer, which) for layer in range(layers) for which in range(2)]
    small = jnp.concatenate(
        [vector_sums[name][kind : kind + 1] for kind in range(2) for name in names], axis=0
    )
    small = small + swap(small, 1)
    for bit in bits[::-1]:
        near, far = jnp.split(small, 2, axis=1)
        small = near + hop(far, bit)
    small = small.reshape(2, layers, 2, slices)
    return (
        outputs,
        all_rows(*restored),
        jnp.stack(qkv_grads[::-1]),
        jnp.stack([grad.T for grad in out_grads[::-1]]),
        jnp.stack(up_grads[::-1]),
        jnp.stack(down_grads[::-1]),
        small[0],
        small[1],
    )


def solution(mesh):
    placed = (
        P("tm", None, None),
        P(None, "tm", None, "head"),
        P(None, "head", "tm"),
        P(None, "tm", "head"),
        P(None, "head", "tm"),
        P(None, None, "tm"),
        P(None, None, "tm"),
        P("tm", None),
        P(None, "tm", None),
        P("tm", None, None),
    )
    return jax.shard_map(
        body,
        mesh=mesh,
        in_specs=placed,
        out_specs=(
            P("tm", None, None),
            P("tm", None, None),
            P(None, "tm", None, "head"),
            P(None, "head", "tm"),
            P(None, "tm", "head"),
            P(None, "head", "tm"),
            P(None, None, "tm"),
            P(None, None, "tm"),
        ),
        check_vma=False,
    )
```

```python
import functools

import jax
import jax.numpy as jnp
from jax import lax
from jax.experimental import pallas as pl
from jax.experimental.pallas import tpu as pltpu
from jax.sharding import PartitionSpec as P

HEAD_DIM = 64
PAIR = 2 * HEAD_DIM
GROUP = HEAD_DIM // 6
NEG_BIG = -1e30
F32 = jnp.float32
BF16 = jnp.bfloat16
NT = (((1,), (1,)), ((), ()))
TN = (((0,), (0,)), ((), ()))
NN = (((1,), (0,)), ((), ()))


def dot(left, right, dims):
    return lax.dot_general(left, right, dims, preferred_element_type=F32)


def rotary_tables(coordinates):
    lane = jnp.arange(PAIR, dtype=jnp.int32) % HEAD_DIM
    group = jnp.minimum(lane // (2 * GROUP), 2)
    place = lane % (2 * GROUP)
    turned = lane < 6 * GROUP
    first = turned & (place < GROUP)
    second = turned & (place >= GROUP)
    inverse = 10000.0 ** (-(place % GROUP).astype(F32) / GROUP)
    spread = jnp.where(
        group == 0,
        coordinates[:, 0:1],
        jnp.where(group == 1, coordinates[:, 1:2], coordinates[:, 2:3]),
    )
    angles = spread * inverse
    cosine = jnp.where(turned, jnp.cos(angles), 1.0)
    sine = jnp.sin(angles)
    return (cosine, jnp.where(first, -sine, 0.0), jnp.where(second, sine, 0.0))


def turn(values, cosine, sine_first, sine_second):
    ahead = pltpu.roll(values, PAIR - GROUP, 1)
    behind = pltpu.roll(values, GROUP, 1)
    return values * cosine + ahead * sine_first + behind * sine_second


def turn_back(values, cosine, sine_first, sine_second):
    ahead = pltpu.roll(values, PAIR - GROUP, 1)
    behind = pltpu.roll(values, GROUP, 1)
    return values * cosine - ahead * sine_first - behind * sine_second


def project_kernel(own, peer, left, right, cosine, sine_first, sine_second, out):
    rows = out.shape[2]
    width = out.shape[1] * PAIR
    middle = left.shape[0]
    for step, acts in enumerate((own, peer)):
        span = pl.ds(step * 2 * rows, 2 * rows)
        raw = dot(acts[:, :middle], left[:, : 3 * width], NN)
        raw += dot(acts[:, middle:], right[:, : 3 * width], NN)
        tables = (cosine[span, :], sine_first[span, :], sine_second[span, :])
        for pair in range(out.shape[1]):
            for part in range(3):
                start = part * width + pair * PAIR
                piece = raw[:, start : start + PAIR]
                if part < 2:
                    piece = turn(piece, *tables)
                piece = piece.astype(BF16)
                for half in range(2):
                    out[2 * step + half, pair, :, part * PAIR : (part + 1) * PAIR] = piece[
                        half * rows : (half + 1) * rows
                    ]


def unit_rows(tiles, micros, pairs, lanes):
    return jnp.concatenate(
        [
            jnp.concatenate([tiles[micro * pairs + pair, :, lanes] for pair in range(pairs)], axis=1)
            for micro in micros
        ],
        axis=0,
    )


def mix_kernel(pairs, mixed, left, right, theirs, mine):
    width = pairs * PAIR
    micro = mixed.shape[0] // pairs
    middle = left.shape[0]
    skip = left.shape[1] - width
    for micros, out in ((range(micro // 2, micro), theirs), (range(micro // 2), mine)):
        rows = unit_rows(mixed, micros, pairs, slice(0, PAIR))
        out[:, :middle] = dot(rows, left[:, skip:], NT).astype(out.dtype)
        out[:, middle:] = dot(rows, right[:, skip:], NT).astype(out.dtype)


def unmix_kernel(own, peer, left, right, out):
    rows = out.shape[2]
    width = out.shape[1] * PAIR
    middle = left.shape[0]
    skip = left.shape[1] - width
    for step, acts in enumerate((own, peer)):
        raw = dot(acts[:, :middle], left[:, skip:], NN) + dot(acts[:, middle:], right[:, skip:], NN)
        raw = raw.astype(BF16)
        for pair in range(out.shape[1]):
            for half in range(2):
                out[2 * step + half, pair] = raw[
                    half * rows : (half + 1) * rows, pair * PAIR : (pair + 1) * PAIR
                ]


def unproject_kernel(pairs, packed, left, right, theirs, mine):
    width = pairs * PAIR
    micro = packed.shape[0] // pairs
    middle = left.shape[0]
    for micros, out in ((range(micro // 2, micro), theirs), (range(micro // 2), mine)):
        for weights, place in ((left, slice(0, middle)), (right, slice(middle, 2 * middle))):
            total = 0.0
            for part in range(3):
                rows = unit_rows(packed, micros, pairs, slice(part * PAIR, (part + 1) * PAIR))
                total += dot(rows, weights[:, part * width : (part + 1) * width], NT)
            out[:, place] = total.astype(out.dtype)


def up_kernel(own, peer, left, right, activated, slope):
    middle = left.shape[0]
    half = own.shape[0]
    for start in range(0, activated.shape[1], 256):
        block = slice(start, start + 256)
        for step, acts in enumerate((own, peer)):
            upward = dot(acts[:, :middle], left[:, block], NN)
            upward += dot(acts[:, middle:], right[:, block], NN)
            bell = 0.5 * (1.0 + lax.erf(upward * 0.7071067811865476))
            span = slice(step * half, (step + 1) * half)
            activated[span, block] = (upward * bell).astype(BF16)
            slope[span, block] = (
                bell + upward * jnp.exp(-0.5 * upward * upward) * 0.3989422804014327
            )


def down_kernel(activated, left, right, theirs, mine):
    half = mine.shape[0]
    middle = left.shape[1]
    for span, out in ((slice(half, 2 * half), theirs), (slice(0, half), mine)):
        out[:, :middle] = dot(activated[span, :], left[...], NN).astype(out.dtype)
        out[:, middle:] = dot(activated[span, :], right[...], NN).astype(out.dtype)


def dense_back_kernel(own, peer, up_left, up_right, down_left, down_right, slope, inner, theirs, mine):
    half = mine.shape[0]
    middle = up_left.shape[0]
    for acts, span, out in (
        (peer, slice(half, 2 * half), theirs),
        (own, slice(0, half), mine),
    ):
        raw = dot(acts[:, :middle], down_left[...], NT)
        raw += dot(acts[:, middle:], down_right[...], NT)
        grad = (raw * slope[span, :]).astype(BF16)
        inner[span, :] = grad
        out[:, :middle] = dot(grad, up_left[...], NT).astype(out.dtype)
        out[:, middle:] = dot(grad, up_right[...], NT).astype(out.dtype)


def pair_kernel(mine, come, total):
    total[...] = (mine[...] + come[...].astype(F32)).astype(BF16)


def normalized(hidden, gain, bias):
    centered = hidden - jnp.mean(hidden, axis=-1, keepdims=True)
    root = lax.rsqrt(jnp.mean(centered * centered, axis=-1, keepdims=True) + 1e-06)
    normed = centered * root
    return normed, root, (normed * gain + bias).astype(BF16)


def first_norm_kernel(gain, bias, hidden, vectors, normed, root, out):
    normed[...], scale, out[...] = normalized(
        hidden[...], vectors[gain : gain + 1, :], vectors[bias : bias + 1, :]
    )
    root[...] = jnp.broadcast_to(scale, root.shape)


def norm_kernel(gain, bias, hidden, total, come, vectors, result, normed, root, out):
    value = hidden[...] + (total[...].astype(F32) + come[...].astype(F32))
    result[...] = value
    normed[...], scale, out[...] = normalized(
        value, vectors[gain : gain + 1, :], vectors[bias : bias + 1, :]
    )
    root[...] = jnp.broadcast_to(scale, root.shape)


def norm_back_kernel(gain, total, come, normed, root, vectors, upstream, result, out, sums):
    grad = total[...].astype(F32) + come[...].astype(F32)
    known = normed[...]
    sums[0:1, :] = jnp.sum(grad * known, axis=0, keepdims=True)
    sums[1:2, :] = jnp.sum(grad, axis=0, keepdims=True)
    scaled = grad * vectors[gain : gain + 1, :]
    value = upstream[...] + root[:, 0:1] * (
        scaled
        - jnp.mean(scaled, axis=-1, keepdims=True)
        - known * jnp.mean(scaled * known, axis=-1, keepdims=True)
    )
    result[...] = value
    out[...] = value.astype(BF16)


def quarter_of(own, peer, quarter):
    size = own.shape[1] // 4
    span = slice(quarter * size, (quarter + 1) * size)
    return jnp.concatenate([own[:, span], peer[:, span]], axis=0)


def up_products(quarter, own, peer, inner):
    rows = quarter_of(own, peer, quarter)
    for start in range(0, inner.shape[1], 256):
        span = slice(start, start + 256)
        yield (slice(None), span), dot(rows, inner[:, span], TN)


def down_products(quarter, own, peer, activated):
    rows = quarter_of(own, peer, quarter)
    for start in range(0, activated.shape[1], 256):
        span = slice(start, start + 256)
        yield (span, slice(None)), dot(activated[:, span], rows, TN)


def projection_products(pairs, parts, quarter, own, peer, packed):
    rows = quarter_of(own, peer, quarter)
    micros = range(packed.shape[0] // pairs)
    for place, part in enumerate(parts):
        other = unit_rows(packed, micros, pairs, slice(part * PAIR, (part + 1) * PAIR))
        span = slice(place * pairs * PAIR, (place + 1) * pairs * PAIR)
        yield (slice(None), span), dot(rows, other, TN)


def mix_products(pairs, start, quarter, own, peer, mixed):
    rows = quarter_of(own, peer, quarter)
    micros = range(mixed.shape[0] // pairs)
    other = unit_rows(mixed, micros, pairs, slice(0, PAIR))
    yield (slice(None), slice(start, start + pairs * PAIR)), dot(rows, other, TN)


def attention_products(pairs, quarter, own, peer, packed, grad_own, grad_peer, mixed):
    yield from projection_products(pairs, range(3), quarter, own, peer, packed)
    yield from mix_products(pairs, 3 * pairs * PAIR, quarter, grad_own, grad_peer, mixed)


def far_kernel(products, *refs):
    for quarter, out in ((2, refs[-2]), (3, refs[-1])):
        for place, value in products(quarter, *refs[:-2]):
            out[place] = value.astype(BF16)


def send_kernel(products, *refs):
    arrived, out = refs[-2:]
    for place, value in products(1, *refs[:-2]):
        out[place] = (value + arrived[place].astype(F32)).astype(BF16)


def keep_kernel(products, axis, *refs):
    arrived, folded, keep, send = refs[-4:]
    half = keep.shape[axis]
    for place, value in products(0, *refs[:-4]):
        value = value + arrived[place].astype(F32) + folded[place].astype(F32)
        if axis:
            keep[place] = value[:, :half]
            send[place] = value[:, half:].astype(BF16)
        else:
            keep[place] = value[:half]
            send[place] = value[half:].astype(BF16)


def lane_mask(shape, head):
    lane = lax.broadcasted_iota(jnp.int32, shape, 1)
    return (lane >= head * HEAD_DIM) & (lane < (head + 1) * HEAD_DIM)


def visible_bias(key_frames, query_frames, block):
    spread = jnp.concatenate([key_frames] * (block // key_frames.shape[1]), axis=1)
    return spread <= query_frames


def attend_kernel(block, start, qkv, key_frames, query_frames, out, out_t, lse):
    key_vecs = qkv[:, PAIR : 2 * PAIR]
    value_t = jnp.transpose(qkv[:, 2 * PAIR :].astype(F32)).astype(BF16)
    query_rows = out.shape[0]

    def one(step, carry):
        place = pl.multiple_of(step * block, block)
        source = pl.multiple_of(start[0] + step * block, block)
        queries = qkv[pl.ds(source, block), :PAIR] * jnp.asarray(HEAD_DIM**-0.5, BF16)
        seen = visible_bias(key_frames[...], query_frames[:, pl.ds(source, block)], block)
        pieces = []
        for head in range(2):
            mine = jnp.where(lane_mask(queries.shape, head), queries, jnp.zeros_like(queries))
            scores = jnp.where(seen, dot(key_vecs, mine, NT), NEG_BIG)
            top = jnp.max(scores, axis=0, keepdims=True)
            raised = jnp.exp(scores - top)
            total = jnp.sum(raised, axis=0, keepdims=True)
            summed = dot(
                value_t[head * HEAD_DIM : (head + 1) * HEAD_DIM], raised.astype(BF16), NN
            )
            pieces.append(summed / total)
            lse[head : head + 1, pl.ds(place, block)] = top + jnp.log(total)
        both = jnp.concatenate(pieces, axis=0)
        out_t[:, pl.ds(place, block)] = both
        out[pl.ds(place, block), :] = jnp.transpose(both).astype(BF16)
        return carry

    lax.fori_loop(0, query_rows // block, one, 0)


def attend_back_kernel(
    block,
    start,
    qkv,
    grad_out,
    out_t,
    lse,
    key_frames,
    query_frames,
    cosine,
    sine_first,
    sine_second,
    result,
    key_sum,
    value_sum,
):
    key_vecs = qkv[:, PAIR : 2 * PAIR]
    value_vecs = qkv[:, 2 * PAIR :]
    key_t = jnp.transpose(key_vecs.astype(F32)).astype(BF16)
    query_rows = grad_out.shape[0]
    key_sum[...] = jnp.zeros_like(key_sum)
    value_sum[...] = jnp.zeros_like(value_sum)
    if query_rows != qkv.shape[0]:
        result[:, :PAIR] = jnp.zeros((qkv.shape[0], PAIR), BF16)

    def one(step, carry):
        place = pl.multiple_of(step * block, block)
        source = pl.multiple_of(start[0] + step * block, block)
        queries = qkv[pl.ds(source, block), :PAIR] * jnp.asarray(HEAD_DIM**-0.5, BF16)
        upstream = grad_out[pl.ds(place, block), :]
        seen = visible_bias(key_frames[...], query_frames[:, pl.ds(source, block)], block)
        both = out_t[:, pl.ds(place, block)] * jnp.transpose(upstream.astype(F32))
        pieces = []
        for head in range(2):
            keep = lane_mask(queries.shape, head)
            mine = jnp.where(keep, queries, jnp.zeros_like(queries))
            above = jnp.where(keep, upstream, jnp.zeros_like(upstream))
            rows = slice(head * HEAD_DIM, (head + 1) * HEAD_DIM)
            delta = jnp.sum(both[rows], axis=0, keepdims=True)
            log_total = lse[head : head + 1, pl.ds(place, block)]
            weights = jnp.where(seen, jnp.exp(dot(key_vecs, mine, NT) - log_total), 0.0)
            slope = (weights * (dot(value_vecs, above, NT) - delta)).astype(BF16)
            value_sum[...] += dot(weights.astype(BF16), above, NN)
            key_sum[...] += dot(slope, mine, NN)
            pieces.append(dot(key_t[rows], slope, NN))
        query_grad = jnp.transpose(jnp.concatenate(pieces, axis=0)) * HEAD_DIM**-0.5
        span = pl.ds(source, block)
        result[span, :PAIR] = turn_back(
            query_grad, cosine[span, :], sine_first[span, :], sine_second[span, :]
        ).astype(BF16)
        return carry

    lax.fori_loop(0, query_rows // block, one, 0)
    result[:, PAIR : 2 * PAIR] = turn_back(
        key_sum[...], cosine[...], sine_first[...], sine_second[...]
    ).astype(BF16)
    result[:, 2 * PAIR :] = value_sum[...].astype(BF16)


def whole():
    return pl.BlockSpec(memory_space=pltpu.VMEM)


def scalars():
    return pl.BlockSpec(memory_space=pltpu.SMEM)


def call(kernel, outs, name, *operands, numbers=(), scratch=(), scale=1, away=False):
    shapes = [(jax.ShapeDtypeStruct if away else pltpu.VMEM)(shape, kind) for shape, kind in outs]
    memory = pltpu.HBM if away else pltpu.VMEM
    operands = [pltpu.with_memory_space_constraint(operand, memory) for operand in operands]
    single = len(shapes) == 1
    return pl.pallas_call(
        kernel,
        out_shape=shapes[0] if single else shapes,
        in_specs=[scalars()] * len(numbers) + [whole()] * len(operands),
        out_specs=whole() if single else [whole()] * len(shapes),
        scratch_shapes=scratch,
        compiler_params=pltpu.CompilerParams(vmem_limit_bytes=scale * 10 * 1024 * 1024),
        name=name,
    )(*numbers, *operands)


def strip_kernel(*refs):
    pieces, (left, right, extras, vectors) = refs[:-4], refs[-4:]
    count = len(pieces)
    size = left.shape[0] // (count // 2)
    for place, piece in enumerate(pieces):
        out = (left, right)[place // (count // 2)]
        first = place % (count // 2) * size
        out[first : first + size, :] = piece[:size, :]
        extras[place] = piece[size:, :]
        extra = piece[size:, :].astype(F32)
        for row in range(vectors.shape[0]):
            start = row * size
            lanes = start % extra.shape[1]
            line = start // extra.shape[1]
            vectors[row : row + 1, place * size : (place + 1) * size] = extra[
                line : line + 1, lanes : lanes + size
            ]


def shard_kernel(qkv, out, result):
    width = qkv.shape[3]
    for part in range(3):
        result[:, part * width : (part + 1) * width] = qkv[0, :, part, :].astype(BF16)
    result[:, 3 * width :] = jnp.transpose(out[0]).astype(BF16)


def shard(layer, qkv_all, out_all):
    rows, width = qkv_all.shape[1], qkv_all.shape[3]
    return pl.pallas_call(
        shard_kernel,
        grid=(1,),
        out_shape=jax.ShapeDtypeStruct((rows, 4 * width), BF16),
        in_specs=[
            pl.BlockSpec((1,) + qkv_all.shape[1:], lambda i: (layer, 0, 0, 0)),
            pl.BlockSpec((1,) + out_all.shape[1:], lambda i: (layer, 0, 0)),
        ],
        out_specs=pl.BlockSpec((rows, 4 * width), lambda i: (0, 0)),
        compiler_params=pltpu.CompilerParams(vmem_limit_bytes=10 * 1024 * 1024),
        name="shard",
    )(qkv_all, out_all)


def call_window(kernel, outs, name, operands, weights, width, index):
    shapes = [jax.ShapeDtypeStruct(shape, kind) for shape, kind in outs]

    def full(shape):
        return pl.BlockSpec(shape, lambda i: (0,) * len(shape))

    single = len(shapes) == 1
    specs = [full(shape) for shape, kind in outs]
    return pl.pallas_call(
        kernel,
        grid=(1,),
        out_shape=shapes[0] if single else shapes,
        in_specs=[full(operand.shape) for operand in operands]
        + [pl.BlockSpec((part.shape[0], width), lambda i: (0, index)) for part in weights],
        out_specs=specs[0] if single else specs,
        compiler_params=pltpu.CompilerParams(vmem_limit_bytes=10 * 1024 * 1024),
        name=name,
    )(*operands, *weights)


def attend(start, qkv, key_frames, query_frames, query_rows):
    return call(
        functools.partial(attend_kernel, 256),
        [((query_rows, PAIR), BF16), ((PAIR, query_rows), F32), ((2, query_rows), F32)],
        "attend",
        qkv,
        key_frames,
        query_frames,
        numbers=(start,),
        scale=max(2, 2 * qkv.shape[0] // 1024),
        away=True,
    )


def attend_back(start, qkv, grad_out, out_t, lse, key_frames, query_frames, tables):
    return call(
        functools.partial(attend_back_kernel, 256),
        [(qkv.shape, BF16)],
        "attend_back",
        qkv,
        grad_out,
        out_t,
        lse,
        key_frames,
        query_frames,
        *tables,
        numbers=(start,),
        scratch=[pltpu.VMEM((qkv.shape[0], PAIR), F32)] * 2,
        scale=max(2, 2 * qkv.shape[0] // 1024),
        away=True,
    )


def restore_kernel(places, values, out):
    size = values.shape[1] // places.shape[0]
    for block in range(places.shape[0]):
        place = pl.multiple_of(places[block], size)
        out[:, pl.ds(place, size)] = values[:, block * size : (block + 1) * size]


def restore(places, shuffle, values):
    if values.shape[1] // places.shape[0] % 128 == 0:
        return call(restore_kernel, [(values.shape, values.dtype)], "restore", values, numbers=(places,))
    exact = lax.Precision.HIGHEST
    return lax.dot_general(
        values.astype(F32), shuffle.astype(F32), NT, precision=exact
    ).astype(values.dtype)


def body(
    inputs,
    qkv_master,
    out_master,
    up_master,
    down_master,
    norm_gain,
    norm_bias,
    frame_ids,
    patch_pos,
    cotangent,
):
    rows, micro, width = inputs.shape
    tm_size = lax.axis_size("tm")
    head_size = lax.axis_size("head")
    here = lax.axis_index("tm")
    layers = qkv_master.shape[0]
    columns = qkv_master.shape[3]
    hidden_units = up_master.shape[2]
    slices = width // tm_size
    half = micro // 2
    half_rows = half * rows
    odd = lax.axis_index("head") % 2
    pairs = columns // PAIR
    units = micro * pairs
    repeats = tm_size // units
    tokens = rows * tm_size
    query_rows = tokens // repeats

    bits = []
    order = [0]
    bit = tm_size // 2
    while bit:
        bits.append(bit)
        order = order + [place | bit for place in order]
        bit //= 2
    last = bits[-1]

    def sync(*values):
        return lax.optimization_barrier(values)

    def tie(value, *others):
        return sync(value, others)[0]

    def hop(values, bit):
        return lax.ppermute(values, "tm", [(i, i ^ bit) for i in range(tm_size)])

    def swap(values, bit):
        return lax.ppermute(values, "head", [(i, i ^ bit) for i in range(head_size)])

    half_shape = (half_rows, width)
    sums = [(half_shape, BF16), (half_shape, F32)]

    def sum_heads(theirs, mine):
        total = call(pair_kernel, [(half_shape, BF16)], "pair", mine, swap(theirs, 1))
        bit = 2
        while 2 * bit < head_size:
            total = sync((total.astype(F32) + swap(total, bit).astype(F32)).astype(BF16))[0]
            bit *= 2
        return total, swap(total, bit)

    def exchange(values):
        return lax.all_to_all(values, "tm", 0, 0, tiled=True)

    def grow(held, axis=0):
        return jnp.concatenate([held, hop(held, bits[0])], axis=axis)

    def reach(held, axis=0):
        pieces = [held]
        for bit in bits[1:-1]:
            so_far = jnp.concatenate(pieces, axis=axis) if len(pieces) > 1 else held
            pieces.append(hop(so_far, bit))
        return pieces

    def stack(pieces, axis=0):
        return jnp.concatenate(pieces, axis=axis)

    def fold(parts, axis=0):
        keep, send = parts
        for bit in bits[-3::-1]:
            total = keep + hop(send, bit).astype(F32)
            if bit == bits[0]:
                return total
            keep, send = jnp.split(total, 2, axis=axis)
            send = send.astype(BF16)

    def own_rows(values, shuffle):
        mine = lax.dynamic_slice_in_dim(values, half * odd, half, 1)
        mine = jnp.transpose(mine, (1, 0, 2)).reshape(half_rows, width)
        return dot(mine, shuffle, NN)

    def to_units(values):
        return jnp.repeat(values, repeats, axis=0) if repeats > 1 else values

    def from_units(values):
        if repeats == 1:
            return values
        grouped = values.reshape((units, repeats) + values.shape[1:]).astype(F32)
        return jnp.sum(grouped, axis=1).astype(BF16)

    def attention_shard(layer, qkv_all, out_all):
        if slices % 128 == 0:
            return shard(layer, qkv_all, out_all)
        return jnp.concatenate(
            [
                qkv_all[layer].astype(BF16).reshape(slices, 3 * columns),
                out_all[layer].astype(BF16).T,
            ],
            axis=1,
        )

    ordered = (jnp.arange(micro) + half * odd) % micro
    whole_numbers = jnp.concatenate([frame_ids[None], patch_pos], axis=0).astype(F32)
    whole_numbers = jnp.take(jnp.transpose(whole_numbers, (2, 0, 1)), ordered, axis=0)
    vectors = jnp.concatenate([norm_gain, norm_bias], axis=0)
    extra = jnp.concatenate([vectors.reshape(-1), whole_numbers.reshape(-1)]).astype(BF16)
    extra = jnp.pad(extra, (0, 8 * 4 * columns - extra.size)).reshape(8, 4 * columns)

    pieces = {
        0: jnp.concatenate([attention_shard(0, qkv_master, out_master), extra], axis=0)
    }
    for bit in bits:
        pieces[bit] = hop(pieces[0], bit)

    early = [pieces.pop(bit) for bit in bits[:-1]]
    masters = (qkv_master, out_master, up_master, down_master)
    early, inputs, whole_numbers, here, masters = sync(
        early, inputs, whole_numbers, here, masters
    )
    qkv_master, out_master, up_master, down_master = masters
    attention_held = [None] + [
        attention_shard(layer, qkv_master, out_master) for layer in range(1, layers)
    ]
    up_held = [up_master[layer].astype(BF16) for layer in range(layers)]
    down_held = [down_master[layer].astype(BF16) for layer in range(layers)]
    up, down = up_held[0], down_held[0]
    pieces.update(zip(bits[:-1], early))
    for bit in bits:
        for place in [place for place in order if place and place & (bit - 1) == 0]:
            if place & bit and place not in pieces:
                pieces[place] = hop(pieces[place ^ bit], bit)
    up = grow(up)
    down = grow(down, 1)
    feature = jnp.arange(width, dtype=jnp.int32)
    origin = (here ^ jnp.asarray(order, jnp.int32)[:, None]) * slices + jnp.arange(
        slices, dtype=jnp.int32
    )
    offsets = origin[:, 0]
    shuffle = (feature[:, None] == origin.reshape(1, width)).astype(BF16)
    row_tables = rotary_tables(jnp.transpose(whole_numbers, (0, 2, 1)).reshape(micro * rows, 3))
    start = ((here % repeats) * query_rows).reshape(1)

    hidden = own_rows(inputs, shuffle)
    root_shape = (half_rows, 128)
    norm_outs = [(half_shape, F32), (root_shape, F32), (half_shape, BF16)]

    def row_of(layer, which):
        return 2 * layer + which, 2 * layers + 2 * layer + which

    def norm(layer, which, hidden, total, come):
        return call(
            functools.partial(norm_kernel, *row_of(layer, which)),
            [(half_shape, F32)] + norm_outs,
            "norm",
            hidden,
            total,
            come,
            vectors,
        )

    hidden, attention_held[1:], row_tables = sync(hidden, attention_held[1:], row_tables)
    hidden, pieces, up = sync(hidden, pieces, up)
    if slices % 128 == 0:
        left, right, extras, vectors = call(
            strip_kernel,
            [((width // 2, 4 * columns), BF16)] * 2
            + [((tm_size, 8, 4 * columns), BF16), ((4 * layers, width), F32)],
            "strip",
            *[pieces[place] for place in order],
        )
        attention_w = (left, right)
        extras = extras.reshape(tm_size, -1)
    else:
        extras = jnp.stack([pieces[place][slices:].reshape(-1) for place in order])
        vectors = extras[:, : vectors.size].reshape(tm_size, 4 * layers, slices).astype(F32)
        vectors = jnp.transpose(vectors, (1, 0, 2)).reshape(4 * layers, width)
        attention_w = tuple(
            stack([pieces[place][:slices] for place in places_of])
            for places_of in (order[: tm_size // 2], order[tm_size // 2 :])
        )
    numbers = extras[:, 4 * layers * slices : 4 * layers * slices + 3 * rows * micro]
    numbers = lax.dynamic_index_in_dim(
        numbers.reshape(tm_size, micro, 3 * rows), here // (tm_size // micro), 1, keepdims=False
    )
    devices = jnp.arange(tm_size, dtype=jnp.int32)
    origins = (devices[:, None] == (here ^ jnp.asarray(order, jnp.int32))[None, :]).astype(BF16)
    places = dot(origins, numbers, NN).reshape(tm_size, 3, rows)
    places = jnp.transpose(places, (1, 0, 2)).reshape(3, tokens)
    query_frames = places[0:1]
    normed_one, root_one, first_own = call(
        functools.partial(first_norm_kernel, *row_of(0, 0)), norm_outs, "first_norm", hidden, vectors
    )
    stored = []
    weights = []
    for layer in range(layers):
        more = layer + 1 < layers
        first_in = (first_own, swap(first_own, 1))
        first_in, attention_w = sync(first_in, attention_w)
        first_in, down = sync(first_in, down)
        up = tie(up, first_in)
        packed = call(
            project_kernel,
            [((micro, pairs, rows, 3 * PAIR), BF16)],
            "project",
            *first_in,
            *attention_w,
            *row_tables,
        )
        up, down = tie((up, down), packed)
        packed = to_units(packed.reshape(units, rows, 3 * PAIR))
        qkv = exchange(packed).reshape(tokens, 3 * PAIR)
        down_far = []
        if layer == 0:
            up = reach(up)
            sequence_tables = rotary_tables(places.T)
            key_frames = jnp.broadcast_to(places[0][:, None], (tokens, 128))
            qkv, sequence_tables, key_frames = sync(qkv, sequence_tables, key_frames)
        up_far = [hop(up[0], last)]
        qkv, up_far = sync(qkv, up_far)
        if layer == 0:
            down_far = [hop(down, last)]
        down = reach(down, 1)
        if layer:
            up_far = up_far + [hop(piece, last) for piece in tie(up[1:], qkv)]
        if more:
            coming = grow(tie(attention_held[layer + 1], packed))
        mixed, mixed_t, lse = attend(start, qkv, key_frames, query_frames, query_rows)
        if repeats > 1:
            mixed = lax.dynamic_update_slice_in_dim(
                jnp.zeros((tokens, PAIR), BF16), mixed, start[0], 0
            )
        mixed, up_far, up, down_far = sync(mixed, up_far, up, down_far)
        if more:
            mixed, coming = sync(mixed, coming)
        mixed = from_units(exchange(mixed.reshape(tm_size, rows, PAIR)))
        if layer:
            down_far = [hop(down[0], last)]
        else:
            up_far = up_far + [hop(piece, last) for piece in up[1:]]
        mixed, up_far, down_far, down = sync(mixed, up_far, down_far, down)
        theirs, mine = call_window(
            functools.partial(mix_kernel, pairs), sums, "mix", (mixed,), attention_w, columns, 3
        )
        total, come = sum_heads(theirs, mine)
        down_far = down_far + [hop(piece, last) for piece in down[1:]]
        up_w = (stack(up), stack(up_far))
        if more:
            coming, next_up = tie((coming, up_held[layer + 1]), mixed)
            coming_far = [hop(coming, last)]
            coming = reach(coming)
            next_up = grow(next_up)
            come = tie(come, coming, next_up)
        come = tie(come, up_w)
        middle, normed_two, root_two, second_own = norm(layer, 1, hidden, total, come)
        second_in = (second_own, swap(second_own, 1))
        activated, slope = call(
            up_kernel,
            [((micro * rows, hidden_units), BF16), ((micro * rows, hidden_units), F32)],
            "up_project",
            *second_in,
            *up_w,
        )
        down_w = (stack(down, 1), stack(down_far, 1))
        activated = tie(activated, down_w)
        if more:
            theirs, mine = call(down_kernel, sums, "down_project", activated, *down_w)
            total, come = sum_heads(theirs, mine)
            coming_far = coming_far + [hop(piece, last) for piece in coming[1:]]
            next_up, next_down = tie((next_up, down_held[layer + 1]), second_in)
            next_up = reach(next_up)
            next_down = grow(next_down, 1)
            attention_next = (stack(coming), stack(coming_far))
            come = tie(come, next_up, next_down, coming_far[0])
        stored.append(
            (
                normed_one,
                root_one,
                first_in,
                qkv,
                mixed,
                mixed_t,
                lse,
                normed_two,
                root_two,
                second_in,
                activated,
                slope,
            )
        )
        weights.append((attention_w, up_w, down_w))
        if more:
            hidden, normed_one, root_one, first_own = norm(layer + 1, 0, middle, total, come)
            attention_w = attention_next
            up, down = next_up, next_down

    def all_rows(mine, other):
        ours = jnp.concatenate([mine, other], axis=0).reshape(micro, rows, width)
        return jnp.transpose(jnp.roll(ours, half * odd, axis=0), (1, 0, 2))

    def final(middle, activated, down_w):
        total, come = sum_heads(*call(down_kernel, sums, "down_project", activated, *down_w))
        result = middle + (total.astype(F32) + come.astype(F32))
        result = restore(offsets, shuffle, result.astype(BF16))
        return all_rows(result, swap(result, 1))

    class Gradient:
        def __init__(self, products, span, axis, name, *sources):
            self.products, self.axis, self.name, self.sources = products, axis, name, sources
            self.shape = (span, width // 4) if axis else (width // 4, span)
            self.ends = (span, width // 8) if axis else (width // 8, span)
            self.far = None

        def start(self, away=False):
            self.far = call(
                functools.partial(far_kernel, self.products),
                [(self.shape, BF16)] * 2,
                self.name + "_far",
                *self.sources,
                away=away,
            )

        def hop_second(self):
            self.second = hop(self.far[1], last)

        def hop_first(self):
            self.first = hop(self.far[0], last)

        def send(self, away=False):
            self.sent = call(
                functools.partial(send_kernel, self.products),
                [(self.shape, BF16)],
                self.name + "_send",
                *self.sources,
                self.second,
                away=away,
            )

        def hop_sent(self):
            self.sent = hop(self.sent, bits[-2])

        def keep(self, away=False):
            self.kept = call(
                functools.partial(keep_kernel, self.products, self.axis),
                [(self.ends, F32), (self.ends, BF16)],
                self.name + "_keep",
                *self.sources,
                self.first,
                self.sent,
                away=away,
            )

        def hop_kept(self):
            self.kept = fold(self.kept, self.axis)

    upstream = own_rows(cotangent, shuffle)
    grad_own = upstream.astype(BF16)
    back_outs = [(half_shape, F32), (half_shape, BF16), ((2, width), F32)]

    def norm_back(layer, which, total, come, normed, root, upstream):
        return call(
            functools.partial(norm_back_kernel, row_of(layer, which)[0]),
            back_outs,
            "norm_back",
            total,
            come,
            normed,
            root,
            vectors,
            upstream,
        )

    vector_sums = {}
    up_grads, down_grads, qkv_grads, out_grads = [], [], [], []
    late_attention = late_up = None
    for layer in reversed(range(layers)):
        attention_w, up_w, down_w = weights[layer]
        (
            normed_one,
            root_one,
            first_in,
            qkv,
            mixed,
            mixed_t,
            lse,
            normed_two,
            root_two,
            second_in,
            activated,
            slope,
        ) = stored[layer]
        ending = layer == 0
        late = late_attention is not None
        grad_mlp = (grad_own, swap(grad_own, 1))
        if late:
            late_attention.hop_first()
        down = Gradient(down_products, hidden_units, 1, "down", *grad_mlp, activated)
        down.start()
        down.hop_second()
        grad_mlp = tie(grad_mlp, down.far)
        inner, theirs, mine = call(
            dense_back_kernel,
            [((micro * rows, hidden_units), BF16)] + sums,
            "dense_back",
            *grad_mlp,
            *up_w,
            *down_w,
            slope,
        )
        if late:
            theirs = tie(theirs, late_attention.first)
        total, come = sum_heads(theirs, mine)
        up = Gradient(up_products, hidden_units, 0, "up", *second_in, inner)
        up.start()
        come = tie(come, up.far, down.second)
        if late:
            late_attention.send()
            late_attention.hop_sent()
            late_up.keep()
            come = tie(come, late_up.kept)
            come = tie(come, late_attention.sent)
        upstream, grad_own, vector_sums[layer, 1] = norm_back(
            layer, 1, total, come, normed_two, root_two, upstream
        )
        grad_attn = (grad_own, swap(grad_own, 1))
        grad_mixed = call_window(
            unmix_kernel,
            [((micro, pairs, rows, PAIR), BF16)],
            "unmix",
            grad_attn,
            attention_w,
            columns,
            3,
        )
        down.second = tie(down.second, grad_mixed)
        grad_mixed = to_units(grad_mixed.reshape(units, rows, PAIR))
        grad_mixed = exchange(grad_mixed).reshape(tokens, PAIR)
        if repeats > 1:
            grad_mixed = lax.dynamic_slice_in_dim(grad_mixed, start[0], query_rows, 0)
        down.send(True)
        down.far = tie(down.far, down.second)
        down.hop_first()
        grad_mixed = tie(grad_mixed, down.sent, down.first)
        if ending:
            out = Gradient(
                functools.partial(mix_products, pairs, 0), columns, 0, "out", *grad_attn, mixed
            )
            out.start(True)
            grad_mixed = tie(grad_mixed, out.far)
        if late:
            late_attention.keep(True)
            grad_mixed = tie(grad_mixed, late_attention.kept)
            late_up.kept = tie(late_up.kept, down.sent)
            late_up.hop_kept()
            late_attention.kept = tie(late_attention.kept, grad_mixed)
            late_attention.hop_kept()
        down.sent, up.far = tie((down.sent, up.far), grad_mixed)
        down.hop_sent()
        up.hop_second()
        packed_grad = attend_back(
            start, qkv, grad_mixed, mixed_t, lse, key_frames, query_frames, sequence_tables
        )
        packed_grad = tie(packed_grad, down.sent, up.second)
        if late:
            packed_grad = tie(packed_grad, late_attention.kept, late_up.kept)
            up_grads.append(late_up.kept)
            attention_grad = late_attention.kept
            qkv_grads.append(attention_grad[:, : 3 * columns].reshape(slices, 3, columns))
            out_grads.append(attention_grad[:, 3 * columns :])
        if layer + 1 == layers:
            middle, last_in = tie((middle, activated), packed_grad)
            outputs = final(middle, last_in, down_w)
        down.first, up.second, up.far = tie((down.first, up.second, up.far), packed_grad)
        packed_grad = from_units(exchange(packed_grad.reshape(tm_size, rows, 3 * PAIR)))
        down.keep(True)
        up.send(True)
        up.hop_first()
        packed_grad = tie(packed_grad, down.kept, up.sent, up.first)
        if ending:
            out.far = tie(out.far, down.first)
            out.hop_second()
            out.hop_first()
            down.hop_kept()
            packed_grad = tie(packed_grad, out.first, out.second, outputs, down.kept)
        if not ending:
            down.kept = tie(down.kept, packed_grad)
        up.sent = tie(up.sent, packed_grad)
        if ending:
            products = functools.partial(projection_products, pairs, range(3))
            group = Gradient(products, 3 * columns, 0, "qkv", *first_in, packed_grad)
            group.start()
            group.hop_second()
            group.hop_first()
            packed_grad = tie(packed_grad, group.far)
        theirs, mine = call(
            functools.partial(unproject_kernel, pairs),
            sums,
            "unproject",
            packed_grad,
            *attention_w,
        )
        total, come = sum_heads(theirs, mine)
        if not ending:
            down.hop_kept()
        up.hop_sent()
        down_grads.append(down.kept)
        if ending:
            out.second = tie(out.second, theirs)
            out.send()
            out.hop_sent()
            come = tie(come, group.second, up.sent, out.sent)
            group.second, up.sent, out.sent = tie((group.second, up.sent, out.sent), come)
            group.send()
            up.keep()
            out.keep()
            come = tie(come, group.sent, up.kept, out.kept)
            group.hop_sent()
            up.hop_kept()
            out.hop_kept()
        else:
            late_attention = Gradient(
                functools.partial(attention_products, pairs),
                4 * columns,
                0,
                "attention",
                *first_in,
                packed_grad,
                *grad_attn,
                mixed,
            )
            late_attention.start()
            late_attention.hop_second()
            come = tie(come, down.kept, up.sent, late_attention.second)
        late_up = up
        upstream, grad_own, vector_sums[layer, 0] = norm_back(
            layer, 0, total, come, normed_one, root_one, upstream
        )
    restored = restore(offsets, shuffle, upstream)
    restored = (restored, swap(restored, 1))
    group.first = tie(group.first, restored, up.kept, out.kept)
    vector_sums = tie(vector_sums, restored)
    group.keep()
    restored, done = tie(
        (restored, (up_grads, down_grads, out_grads, qkv_grads, up.kept, out.kept)), group.kept
    )
    up_grads, down_grads, out_grads, qkv_grads, up.kept, out.kept = done
    group.hop_kept()
    up_grads.append(up.kept)
    out_grads.append(out.kept)
    qkv_grads.append(group.kept.reshape(slices, 3, columns))
    names = [(layer, which) for layer in range(layers) for which in range(2)]
    small = jnp.concatenate(
        [vector_sums[name][kind : kind + 1] for kind in range(2) for name in names], axis=0
    )
    small = small + swap(small, 1)
    for bit in bits[::-1]:
        near, far = jnp.split(small, 2, axis=1)
        small = near + hop(far, bit)
    small = small.reshape(2, layers, 2, slices)
    return (
        outputs,
        all_rows(*restored),
        jnp.stack(qkv_grads[::-1]),
        jnp.stack([grad.T for grad in out_grads[::-1]]),
        jnp.stack(up_grads[::-1]),
        jnp.stack(down_grads[::-1]),
        small[0],
        small[1],
    )


def solution(mesh):
    placed = (
        P("tm", None, None),
        P(None, "tm", None, "head"),
        P(None, "head", "tm"),
        P(None, "tm", "head"),
        P(None, "head", "tm"),
        P(None, None, "tm"),
        P(None, None, "tm"),
        P("tm", None),
        P(None, "tm", None),
        P("tm", None, None),
    )
    return jax.shard_map(
        body,
        mesh=mesh,
        in_specs=placed,
        out_specs=(
            P("tm", None, None),
            P("tm", None, None),
            P(None, "tm", None, "head"),
            P(None, "head", "tm"),
            P(None, "tm", "head"),
            P(None, "head", "tm"),
            P(None, None, "tm"),
            P(None, None, "tm"),
        ),
        check_vma=False,
    )
```

```python
import functools

import jax
import jax.numpy as jnp
from jax import lax
from jax.experimental import pallas as pl
from jax.experimental.pallas import tpu as pltpu
from jax.sharding import PartitionSpec as P

HEAD_DIM = 64
PAIR = 2 * HEAD_DIM
GROUP = HEAD_DIM // 6
NEG_BIG = -1e30
F32 = jnp.float32
BF16 = jnp.bfloat16
NT = (((1,), (1,)), ((), ()))
TN = (((0,), (0,)), ((), ()))
NN = (((1,), (0,)), ((), ()))


def dot(left, right, dims):
    return lax.dot_general(left, right, dims, preferred_element_type=F32)


def rotary_tables(coordinates):
    lane = jnp.arange(PAIR, dtype=jnp.int32) % HEAD_DIM
    group = jnp.minimum(lane // (2 * GROUP), 2)
    place = lane % (2 * GROUP)
    turned = lane < 6 * GROUP
    first = turned & (place < GROUP)
    second = turned & (place >= GROUP)
    inverse = 10000.0 ** (-(place % GROUP).astype(F32) / GROUP)
    spread = jnp.where(
        group == 0,
        coordinates[:, 0:1],
        jnp.where(group == 1, coordinates[:, 1:2], coordinates[:, 2:3]),
    )
    angles = spread * inverse
    cosine = jnp.where(turned, jnp.cos(angles), 1.0)
    sine = jnp.sin(angles)
    return (cosine, jnp.where(first, -sine, 0.0), jnp.where(second, sine, 0.0))


def turn(values, cosine, sine_first, sine_second):
    ahead = pltpu.roll(values, PAIR - GROUP, 1)
    behind = pltpu.roll(values, GROUP, 1)
    return values * cosine + ahead * sine_first + behind * sine_second


def turn_back(values, cosine, sine_first, sine_second):
    ahead = pltpu.roll(values, PAIR - GROUP, 1)
    behind = pltpu.roll(values, GROUP, 1)
    return values * cosine - ahead * sine_first - behind * sine_second


def project_kernel(own, peer, left, right, cosine, sine_first, sine_second, out):
    rows = out.shape[2]
    width = out.shape[1] * PAIR
    middle = left.shape[0]
    for step, acts in enumerate((own, peer)):
        span = pl.ds(step * 2 * rows, 2 * rows)
        raw = dot(acts[:, :middle], left[:, : 3 * width], NN)
        raw += dot(acts[:, middle:], right[:, : 3 * width], NN)
        tables = (cosine[span, :], sine_first[span, :], sine_second[span, :])
        for pair in range(out.shape[1]):
            for part in range(3):
                start = part * width + pair * PAIR
                piece = raw[:, start : start + PAIR]
                if part < 2:
                    piece = turn(piece, *tables)
                piece = piece.astype(BF16)
                for half in range(2):
                    out[2 * step + half, pair, :, part * PAIR : (part + 1) * PAIR] = piece[
                        half * rows : (half + 1) * rows
                    ]


def unit_rows(tiles, micros, pairs, lanes):
    return jnp.concatenate(
        [
            jnp.concatenate([tiles[micro * pairs + pair, :, lanes] for pair in range(pairs)], axis=1)
            for micro in micros
        ],
        axis=0,
    )


def mix_kernel(pairs, mixed, left, right, theirs, mine):
    width = pairs * PAIR
    micro = mixed.shape[0] // pairs
    middle = left.shape[0]
    skip = left.shape[1] - width
    for micros, out in ((range(micro // 2, micro), theirs), (range(micro // 2), mine)):
        rows = unit_rows(mixed, micros, pairs, slice(0, PAIR))
        out[:, :middle] = dot(rows, left[:, skip:], NT).astype(out.dtype)
        out[:, middle:] = dot(rows, right[:, skip:], NT).astype(out.dtype)


def unmix_kernel(own, peer, left, right, out):
    rows = out.shape[2]
    width = out.shape[1] * PAIR
    middle = left.shape[0]
    skip = left.shape[1] - width
    for step, acts in enumerate((own, peer)):
        raw = dot(acts[:, :middle], left[:, skip:], NN) + dot(acts[:, middle:], right[:, skip:], NN)
        raw = raw.astype(BF16)
        for pair in range(out.shape[1]):
            for half in range(2):
                out[2 * step + half, pair] = raw[
                    half * rows : (half + 1) * rows, pair * PAIR : (pair + 1) * PAIR
                ]


def unproject_kernel(pairs, packed, left, right, theirs, mine):
    width = pairs * PAIR
    micro = packed.shape[0] // pairs
    middle = left.shape[0]
    for micros, out in ((range(micro // 2, micro), theirs), (range(micro // 2), mine)):
        for weights, place in ((left, slice(0, middle)), (right, slice(middle, 2 * middle))):
            total = 0.0
            for part in range(3):
                rows = unit_rows(packed, micros, pairs, slice(part * PAIR, (part + 1) * PAIR))
                total += dot(rows, weights[:, part * width : (part + 1) * width], NT)
            out[:, place] = total.astype(out.dtype)


def up_kernel(own, peer, left, right, activated, slope):
    middle = left.shape[0]
    half = own.shape[0]
    for start in range(0, activated.shape[1], 256):
        block = slice(start, start + 256)
        for step, acts in enumerate((own, peer)):
            upward = dot(acts[:, :middle], left[:, block], NN)
            upward += dot(acts[:, middle:], right[:, block], NN)
            bell = 0.5 * (1.0 + lax.erf(upward * 0.7071067811865476))
            span = slice(step * half, (step + 1) * half)
            activated[span, block] = (upward * bell).astype(BF16)
            slope[span, block] = (
                bell + upward * jnp.exp(-0.5 * upward * upward) * 0.3989422804014327
            )


def down_kernel(activated, left, right, theirs, mine):
    half = mine.shape[0]
    middle = left.shape[1]
    for span, out in ((slice(half, 2 * half), theirs), (slice(0, half), mine)):
        out[:, :middle] = dot(activated[span, :], left[...], NN).astype(out.dtype)
        out[:, middle:] = dot(activated[span, :], right[...], NN).astype(out.dtype)


def dense_back_kernel(own, peer, up_left, up_right, down_left, down_right, slope, inner, theirs, mine):
    half = mine.shape[0]
    middle = up_left.shape[0]
    for acts, span, out in (
        (peer, slice(half, 2 * half), theirs),
        (own, slice(0, half), mine),
    ):
        raw = dot(acts[:, :middle], down_left[...], NT)
        raw += dot(acts[:, middle:], down_right[...], NT)
        grad = (raw * slope[span, :]).astype(BF16)
        inner[span, :] = grad
        out[:, :middle] = dot(grad, up_left[...], NT).astype(out.dtype)
        out[:, middle:] = dot(grad, up_right[...], NT).astype(out.dtype)


def pair_kernel(mine, come, total):
    total[...] = (mine[...] + come[...].astype(F32)).astype(BF16)


def normalized(hidden, gain, bias):
    centered = hidden - jnp.mean(hidden, axis=-1, keepdims=True)
    root = lax.rsqrt(jnp.mean(centered * centered, axis=-1, keepdims=True) + 1e-06)
    normed = centered * root
    return normed, root, (normed * gain + bias).astype(BF16)


def first_norm_kernel(gain, bias, hidden, vectors, normed, root, out):
    normed[...], scale, out[...] = normalized(
        hidden[...], vectors[gain : gain + 1, :], vectors[bias : bias + 1, :]
    )
    root[...] = jnp.broadcast_to(scale, root.shape)


def norm_kernel(gain, bias, hidden, total, come, vectors, result, normed, root, out):
    value = hidden[...] + (total[...].astype(F32) + come[...].astype(F32))
    result[...] = value
    normed[...], scale, out[...] = normalized(
        value, vectors[gain : gain + 1, :], vectors[bias : bias + 1, :]
    )
    root[...] = jnp.broadcast_to(scale, root.shape)


def norm_back_kernel(gain, total, come, normed, root, vectors, upstream, result, out, sums):
    grad = total[...].astype(F32) + come[...].astype(F32)
    known = normed[...]
    sums[0:1, :] = jnp.sum(grad * known, axis=0, keepdims=True)
    sums[1:2, :] = jnp.sum(grad, axis=0, keepdims=True)
    scaled = grad * vectors[gain : gain + 1, :]
    value = upstream[...] + root[:, 0:1] * (
        scaled
        - jnp.mean(scaled, axis=-1, keepdims=True)
        - known * jnp.mean(scaled * known, axis=-1, keepdims=True)
    )
    result[...] = value
    out[...] = value.astype(BF16)


def quarter_of(own, peer, quarter):
    size = own.shape[1] // 4
    span = slice(quarter * size, (quarter + 1) * size)
    return jnp.concatenate([own[:, span], peer[:, span]], axis=0)


def up_products(quarter, own, peer, inner):
    rows = quarter_of(own, peer, quarter)
    for start in range(0, inner.shape[1], 256):
        span = slice(start, start + 256)
        yield (slice(None), span), dot(rows, inner[:, span], TN)


def down_products(quarter, own, peer, activated):
    rows = quarter_of(own, peer, quarter)
    for start in range(0, activated.shape[1], 256):
        span = slice(start, start + 256)
        yield (span, slice(None)), dot(activated[:, span], rows, TN)


def projection_products(pairs, parts, quarter, own, peer, packed):
    rows = quarter_of(own, peer, quarter)
    micros = range(packed.shape[0] // pairs)
    for place, part in enumerate(parts):
        other = unit_rows(packed, micros, pairs, slice(part * PAIR, (part + 1) * PAIR))
        span = slice(place * pairs * PAIR, (place + 1) * pairs * PAIR)
        yield (slice(None), span), dot(rows, other, TN)


def mix_products(pairs, start, quarter, own, peer, mixed):
    rows = quarter_of(own, peer, quarter)
    micros = range(mixed.shape[0] // pairs)
    other = unit_rows(mixed, micros, pairs, slice(0, PAIR))
    yield (slice(None), slice(start, start + pairs * PAIR)), dot(rows, other, TN)


def attention_products(pairs, quarter, own, peer, packed, grad_own, grad_peer, mixed):
    yield from projection_products(pairs, range(3), quarter, own, peer, packed)
    yield from mix_products(pairs, 3 * pairs * PAIR, quarter, grad_own, grad_peer, mixed)


def far_kernel(products, *refs):
    for quarter, out in ((2, refs[-2]), (3, refs[-1])):
        for place, value in products(quarter, *refs[:-2]):
            out[place] = value.astype(BF16)


def joined_kernel(products, *refs):
    out = refs[-1]
    size = out.shape[0] // 2
    for side, quarter in enumerate((2, 3)):
        for (rows, columns), value in products(quarter, *refs[:-1]):
            out[side * size : (side + 1) * size, columns] = value.astype(BF16)


def send_kernel(products, *refs):
    arrived, out = refs[-2:]
    if arrived.shape[0] == 2 * out.shape[0]:
        arrived = arrived.at[out.shape[0] :]
    for place, value in products(1, *refs[:-2]):
        out[place] = (value + arrived[place].astype(F32)).astype(BF16)


def keep_kernel(products, axis, *refs):
    arrived, folded, keep, send = refs[-4:]
    half = keep.shape[axis]
    if arrived.shape[0] == 2 * folded.shape[0]:
        arrived = arrived.at[: folded.shape[0]]
    for place, value in products(0, *refs[:-4]):
        value = value + arrived[place].astype(F32) + folded[place].astype(F32)
        if axis:
            keep[place] = value[:, :half]
            send[place] = value[:, half:].astype(BF16)
        else:
            keep[place] = value[:half]
            send[place] = value[half:].astype(BF16)


def lane_mask(shape, head):
    lane = lax.broadcasted_iota(jnp.int32, shape, 1)
    return (lane >= head * HEAD_DIM) & (lane < (head + 1) * HEAD_DIM)


def visible_bias(key_frames, query_frames, block):
    spread = jnp.concatenate([key_frames] * (block // key_frames.shape[1]), axis=1)
    return spread <= query_frames


def attend_kernel(block, start, qkv, key_frames, query_frames, out, out_t, lse):
    key_vecs = qkv[:, PAIR : 2 * PAIR]
    value_t = jnp.transpose(qkv[:, 2 * PAIR :].astype(F32)).astype(BF16)
    query_rows = out.shape[0]

    def one(step, carry):
        place = pl.multiple_of(step * block, block)
        source = pl.multiple_of(start[0] + step * block, block)
        queries = qkv[pl.ds(source, block), :PAIR] * jnp.asarray(HEAD_DIM**-0.5, BF16)
        seen = visible_bias(key_frames[...], query_frames[:, pl.ds(source, block)], block)
        pieces = []
        for head in range(2):
            mine = jnp.where(lane_mask(queries.shape, head), queries, jnp.zeros_like(queries))
            scores = jnp.where(seen, dot(key_vecs, mine, NT), NEG_BIG)
            top = jnp.max(scores, axis=0, keepdims=True)
            raised = jnp.exp(scores - top)
            total = jnp.sum(raised, axis=0, keepdims=True)
            summed = dot(
                value_t[head * HEAD_DIM : (head + 1) * HEAD_DIM], raised.astype(BF16), NN
            )
            pieces.append(summed / total)
            lse[head : head + 1, pl.ds(place, block)] = top + jnp.log(total)
        both = jnp.concatenate(pieces, axis=0)
        out_t[:, pl.ds(place, block)] = both
        out[pl.ds(place, block), :] = jnp.transpose(both).astype(BF16)
        return carry

    lax.fori_loop(0, query_rows // block, one, 0)


def attend_back_kernel(
    block,
    start,
    qkv,
    grad_out,
    out_t,
    lse,
    key_frames,
    query_frames,
    cosine,
    sine_first,
    sine_second,
    result,
    key_sum,
    value_sum,
):
    key_vecs = qkv[:, PAIR : 2 * PAIR]
    value_vecs = qkv[:, 2 * PAIR :]
    key_t = jnp.transpose(key_vecs.astype(F32)).astype(BF16)
    query_rows = grad_out.shape[0]
    key_sum[...] = jnp.zeros_like(key_sum)
    value_sum[...] = jnp.zeros_like(value_sum)
    if query_rows != qkv.shape[0]:
        result[:, :PAIR] = jnp.zeros((qkv.shape[0], PAIR), BF16)

    def one(step, carry):
        place = pl.multiple_of(step * block, block)
        source = pl.multiple_of(start[0] + step * block, block)
        queries = qkv[pl.ds(source, block), :PAIR] * jnp.asarray(HEAD_DIM**-0.5, BF16)
        upstream = grad_out[pl.ds(place, block), :]
        seen = visible_bias(key_frames[...], query_frames[:, pl.ds(source, block)], block)
        both = out_t[:, pl.ds(place, block)] * jnp.transpose(upstream.astype(F32))
        pieces = []
        for head in range(2):
            keep = lane_mask(queries.shape, head)
            mine = jnp.where(keep, queries, jnp.zeros_like(queries))
            above = jnp.where(keep, upstream, jnp.zeros_like(upstream))
            rows = slice(head * HEAD_DIM, (head + 1) * HEAD_DIM)
            delta = jnp.sum(both[rows], axis=0, keepdims=True)
            log_total = lse[head : head + 1, pl.ds(place, block)]
            weights = jnp.where(seen, jnp.exp(dot(key_vecs, mine, NT) - log_total), 0.0)
            slope = (weights * (dot(value_vecs, above, NT) - delta)).astype(BF16)
            value_sum[...] += dot(weights.astype(BF16), above, NN)
            key_sum[...] += dot(slope, mine, NN)
            pieces.append(dot(key_t[rows], slope, NN))
        query_grad = jnp.transpose(jnp.concatenate(pieces, axis=0)) * HEAD_DIM**-0.5
        span = pl.ds(source, block)
        result[span, :PAIR] = turn_back(
            query_grad, cosine[span, :], sine_first[span, :], sine_second[span, :]
        ).astype(BF16)
        return carry

    lax.fori_loop(0, query_rows // block, one, 0)
    result[:, PAIR : 2 * PAIR] = turn_back(
        key_sum[...], cosine[...], sine_first[...], sine_second[...]
    ).astype(BF16)
    result[:, 2 * PAIR :] = value_sum[...].astype(BF16)


def whole():
    return pl.BlockSpec(memory_space=pltpu.VMEM)


def scalars():
    return pl.BlockSpec(memory_space=pltpu.SMEM)


def call(kernel, outs, name, *operands, numbers=(), scratch=(), scale=1, away=False):
    shapes = [(jax.ShapeDtypeStruct if away else pltpu.VMEM)(shape, kind) for shape, kind in outs]
    memory = pltpu.HBM if away else pltpu.VMEM
    operands = [pltpu.with_memory_space_constraint(operand, memory) for operand in operands]
    single = len(shapes) == 1
    return pl.pallas_call(
        kernel,
        out_shape=shapes[0] if single else shapes,
        in_specs=[scalars()] * len(numbers) + [whole()] * len(operands),
        out_specs=whole() if single else [whole()] * len(shapes),
        scratch_shapes=scratch,
        compiler_params=pltpu.CompilerParams(vmem_limit_bytes=scale * 10 * 1024 * 1024),
        name=name,
    )(*numbers, *operands)


def strip_kernel(*refs):
    pieces, (left, right, extras, vectors) = refs[:-4], refs[-4:]
    count = len(pieces)
    size = left.shape[0] // (count // 2)
    for place, piece in enumerate(pieces):
        out = (left, right)[place // (count // 2)]
        first = place % (count // 2) * size
        out[first : first + size, :] = piece[:size, :]
        extras[place] = piece[size:, :]
        extra = piece[size:, :].astype(F32)
        for row in range(vectors.shape[0]):
            start = row * size
            lanes = start % extra.shape[1]
            line = start // extra.shape[1]
            vectors[row : row + 1, place * size : (place + 1) * size] = extra[
                line : line + 1, lanes : lanes + size
            ]


def shard_kernel(qkv, out, result):
    width = qkv.shape[3]
    for part in range(3):
        result[:, part * width : (part + 1) * width] = qkv[0, :, part, :].astype(BF16)
    result[:, 3 * width :] = jnp.transpose(out[0]).astype(BF16)


def shard(layer, qkv_all, out_all):
    rows, width = qkv_all.shape[1], qkv_all.shape[3]
    return pl.pallas_call(
        shard_kernel,
        grid=(1,),
        out_shape=jax.ShapeDtypeStruct((rows, 4 * width), BF16),
        in_specs=[
            pl.BlockSpec((1,) + qkv_all.shape[1:], lambda i: (layer, 0, 0, 0)),
            pl.BlockSpec((1,) + out_all.shape[1:], lambda i: (layer, 0, 0)),
        ],
        out_specs=pl.BlockSpec((rows, 4 * width), lambda i: (0, 0)),
        compiler_params=pltpu.CompilerParams(vmem_limit_bytes=10 * 1024 * 1024),
        name="shard",
    )(qkv_all, out_all)


def call_window(kernel, outs, name, operands, weights, width, index):
    shapes = [jax.ShapeDtypeStruct(shape, kind) for shape, kind in outs]

    def full(shape):
        return pl.BlockSpec(shape, lambda i: (0,) * len(shape))

    single = len(shapes) == 1
    specs = [full(shape) for shape, kind in outs]
    return pl.pallas_call(
        kernel,
        grid=(1,),
        out_shape=shapes[0] if single else shapes,
        in_specs=[full(operand.shape) for operand in operands]
        + [pl.BlockSpec((part.shape[0], width), lambda i: (0, index)) for part in weights],
        out_specs=specs[0] if single else specs,
        compiler_params=pltpu.CompilerParams(vmem_limit_bytes=10 * 1024 * 1024),
        name=name,
    )(*operands, *weights)


def attend(start, qkv, key_frames, query_frames, query_rows):
    return call(
        functools.partial(attend_kernel, 256),
        [((query_rows, PAIR), BF16), ((PAIR, query_rows), F32), ((2, query_rows), F32)],
        "attend",
        qkv,
        key_frames,
        query_frames,
        numbers=(start,),
        scale=max(2, 2 * qkv.shape[0] // 1024),
        away=True,
    )


def attend_back(start, qkv, grad_out, out_t, lse, key_frames, query_frames, tables):
    return call(
        functools.partial(attend_back_kernel, 256),
        [(qkv.shape, BF16)],
        "attend_back",
        qkv,
        grad_out,
        out_t,
        lse,
        key_frames,
        query_frames,
        *tables,
        numbers=(start,),
        scratch=[pltpu.VMEM((qkv.shape[0], PAIR), F32)] * 2,
        scale=max(2, 2 * qkv.shape[0] // 1024),
        away=True,
    )


def restore_kernel(places, values, out):
    size = values.shape[1] // places.shape[0]
    for block in range(places.shape[0]):
        place = pl.multiple_of(places[block], size)
        out[:, pl.ds(place, size)] = values[:, block * size : (block + 1) * size]


def restore(places, shuffle, values):
    if values.shape[1] // places.shape[0] % 128 == 0:
        return call(restore_kernel, [(values.shape, values.dtype)], "restore", values, numbers=(places,))
    exact = lax.Precision.HIGHEST
    return lax.dot_general(
        values.astype(F32), shuffle.astype(F32), NT, precision=exact
    ).astype(values.dtype)


def body(
    inputs,
    qkv_master,
    out_master,
    up_master,
    down_master,
    norm_gain,
    norm_bias,
    frame_ids,
    patch_pos,
    cotangent,
):
    rows, micro, width = inputs.shape
    tm_size = lax.axis_size("tm")
    head_size = lax.axis_size("head")
    here = lax.axis_index("tm")
    layers = qkv_master.shape[0]
    columns = qkv_master.shape[3]
    hidden_units = up_master.shape[2]
    slices = width // tm_size
    half = micro // 2
    half_rows = half * rows
    odd = lax.axis_index("head") % 2
    pairs = columns // PAIR
    units = micro * pairs
    repeats = tm_size // units
    tokens = rows * tm_size
    query_rows = tokens // repeats

    bits = []
    order = [0]
    bit = tm_size // 2
    while bit:
        bits.append(bit)
        order = order + [place | bit for place in order]
        bit //= 2
    last = bits[-1]

    def sync(*values):
        return lax.optimization_barrier(values)

    def tie(value, *others):
        return sync(value, others)[0]

    def hop(values, bit):
        return lax.ppermute(values, "tm", [(i, i ^ bit) for i in range(tm_size)])

    def swap(values, bit):
        return lax.ppermute(values, "head", [(i, i ^ bit) for i in range(head_size)])

    half_shape = (half_rows, width)
    sums = [(half_shape, BF16), (half_shape, F32)]

    def sum_heads(theirs, mine):
        total = call(pair_kernel, [(half_shape, BF16)], "pair", mine, swap(theirs, 1))
        bit = 2
        while 2 * bit < head_size:
            total = sync((total.astype(F32) + swap(total, bit).astype(F32)).astype(BF16))[0]
            bit *= 2
        return total, swap(total, bit)

    def exchange(values):
        return lax.all_to_all(values, "tm", 0, 0, tiled=True)

    def grow(held, axis=0):
        return jnp.concatenate([held, hop(held, bits[0])], axis=axis)

    def reach(held, axis=0):
        pieces = [held]
        for bit in bits[1:-1]:
            so_far = jnp.concatenate(pieces, axis=axis) if len(pieces) > 1 else held
            pieces.append(hop(so_far, bit))
        return pieces

    def stack(pieces, axis=0):
        return jnp.concatenate(pieces, axis=axis)

    def fold(parts, axis=0):
        keep, send = parts
        for bit in bits[-3::-1]:
            total = keep + hop(send, bit).astype(F32)
            if bit == bits[0]:
                return total
            keep, send = jnp.split(total, 2, axis=axis)
            send = send.astype(BF16)

    def own_rows(values, shuffle):
        mine = lax.dynamic_slice_in_dim(values, half * odd, half, 1)
        mine = jnp.transpose(mine, (1, 0, 2)).reshape(half_rows, width)
        return dot(mine, shuffle, NN)

    def to_units(values):
        return jnp.repeat(values, repeats, axis=0) if repeats > 1 else values

    def from_units(values):
        if repeats == 1:
            return values
        grouped = values.reshape((units, repeats) + values.shape[1:]).astype(F32)
        return jnp.sum(grouped, axis=1).astype(BF16)

    def attention_shard(layer, qkv_all, out_all):
        if slices % 128 == 0:
            return shard(layer, qkv_all, out_all)
        return jnp.concatenate(
            [
                qkv_all[layer].astype(BF16).reshape(slices, 3 * columns),
                out_all[layer].astype(BF16).T,
            ],
            axis=1,
        )

    ordered = (jnp.arange(micro) + half * odd) % micro
    whole_numbers = jnp.concatenate([frame_ids[None], patch_pos], axis=0).astype(F32)
    whole_numbers = jnp.take(jnp.transpose(whole_numbers, (2, 0, 1)), ordered, axis=0)
    vectors = jnp.concatenate([norm_gain, norm_bias], axis=0)
    extra = jnp.concatenate([vectors.reshape(-1), whole_numbers.reshape(-1)]).astype(BF16)
    extra = jnp.pad(extra, (0, 8 * 4 * columns - extra.size)).reshape(8, 4 * columns)

    pieces = {
        0: jnp.concatenate([attention_shard(0, qkv_master, out_master), extra], axis=0)
    }
    for bit in bits:
        pieces[bit] = hop(pieces[0], bit)

    early = [pieces.pop(bit) for bit in bits[:-1]]
    masters = (qkv_master, out_master, up_master, down_master)
    early, inputs, whole_numbers, here, masters = sync(
        early, inputs, whole_numbers, here, masters
    )
    qkv_master, out_master, up_master, down_master = masters
    attention_held = [None] + [
        attention_shard(layer, qkv_master, out_master) for layer in range(1, layers)
    ]
    up_held = [up_master[layer].astype(BF16) for layer in range(layers)]
    down_held = [down_master[layer].astype(BF16) for layer in range(layers)]
    up, down = up_held[0], down_held[0]
    pieces.update(zip(bits[:-1], early))
    for bit in bits:
        for place in [place for place in order if place and place & (bit - 1) == 0]:
            if place & bit and place not in pieces:
                pieces[place] = hop(pieces[place ^ bit], bit)
    up = grow(up)
    down = grow(down, 1)
    feature = jnp.arange(width, dtype=jnp.int32)
    origin = (here ^ jnp.asarray(order, jnp.int32)[:, None]) * slices + jnp.arange(
        slices, dtype=jnp.int32
    )
    offsets = origin[:, 0]
    shuffle = (feature[:, None] == origin.reshape(1, width)).astype(BF16)
    row_tables = rotary_tables(jnp.transpose(whole_numbers, (0, 2, 1)).reshape(micro * rows, 3))
    start = ((here % repeats) * query_rows).reshape(1)

    hidden = own_rows(inputs, shuffle)
    root_shape = (half_rows, 128)
    norm_outs = [(half_shape, F32), (root_shape, F32), (half_shape, BF16)]

    def row_of(layer, which):
        return 2 * layer + which, 2 * layers + 2 * layer + which

    def norm(layer, which, hidden, total, come):
        return call(
            functools.partial(norm_kernel, *row_of(layer, which)),
            [(half_shape, F32)] + norm_outs,
            "norm",
            hidden,
            total,
            come,
            vectors,
        )

    hidden, attention_held[1:], row_tables = sync(hidden, attention_held[1:], row_tables)
    hidden, pieces, up, down = sync(hidden, pieces, up, down)
    if slices % 128 == 0:
        left, right, extras, vectors = call(
            strip_kernel,
            [((width // 2, 4 * columns), BF16)] * 2
            + [((tm_size, 8, 4 * columns), BF16), ((4 * layers, width), F32)],
            "strip",
            *[pieces[place] for place in order],
        )
        attention_w = (left, right)
        extras = extras.reshape(tm_size, -1)
    else:
        extras = jnp.stack([pieces[place][slices:].reshape(-1) for place in order])
        vectors = extras[:, : vectors.size].reshape(tm_size, 4 * layers, slices).astype(F32)
        vectors = jnp.transpose(vectors, (1, 0, 2)).reshape(4 * layers, width)
        attention_w = tuple(
            stack([pieces[place][:slices] for place in places_of])
            for places_of in (order[: tm_size // 2], order[tm_size // 2 :])
        )
    numbers = extras[:, 4 * layers * slices : 4 * layers * slices + 3 * rows * micro]
    numbers = lax.dynamic_index_in_dim(
        numbers.reshape(tm_size, micro, 3 * rows), here // (tm_size // micro), 1, keepdims=False
    )
    devices = jnp.arange(tm_size, dtype=jnp.int32)
    origins = (devices[:, None] == (here ^ jnp.asarray(order, jnp.int32))[None, :]).astype(BF16)
    places = dot(origins, numbers, NN).reshape(tm_size, 3, rows)
    places = jnp.transpose(places, (1, 0, 2)).reshape(3, tokens)
    query_frames = places[0:1]
    normed_one, root_one, first_own = call(
        functools.partial(first_norm_kernel, *row_of(0, 0)), norm_outs, "first_norm", hidden, vectors
    )
    stored = []
    weights = []
    for layer in range(layers):
        more = layer + 1 < layers
        first_in = (first_own, swap(first_own, 1))
        first_in, attention_w = sync(first_in, attention_w)
        first_in, down = sync(first_in, down)
        up = tie(up, first_in)
        packed = call(
            project_kernel,
            [((micro, pairs, rows, 3 * PAIR), BF16)],
            "project",
            *first_in,
            *attention_w,
            *row_tables,
        )
        up, down = tie((up, down), packed)
        packed = to_units(packed.reshape(units, rows, 3 * PAIR))
        qkv = exchange(packed).reshape(tokens, 3 * PAIR)
        down_far = []
        if layer == 0:
            up = reach(up)
            sequence_tables = rotary_tables(places.T)
            key_frames = jnp.broadcast_to(places[0][:, None], (tokens, 128))
            qkv, sequence_tables, key_frames = sync(qkv, sequence_tables, key_frames)
        up_far = [hop(up[0], last)]
        qkv, up_far = sync(qkv, up_far)
        if layer == 0:
            down_far = [hop(down, last)]
        down = reach(down, 1)
        if layer:
            up_far = up_far + [hop(piece, last) for piece in tie(up[1:], qkv)]
        if more:
            coming = grow(tie(attention_held[layer + 1], packed))
        mixed, mixed_t, lse = attend(start, qkv, key_frames, query_frames, query_rows)
        if repeats > 1:
            mixed = lax.dynamic_update_slice_in_dim(
                jnp.zeros((tokens, PAIR), BF16), mixed, start[0], 0
            )
        mixed, up_far, up, down_far = sync(mixed, up_far, up, down_far)
        if more:
            mixed, coming = sync(mixed, coming)
        mixed = from_units(exchange(mixed.reshape(tm_size, rows, PAIR)))
        if layer:
            down_far = [hop(down[0], last)]
        else:
            up_far = up_far + [hop(piece, last) for piece in up[1:]]
        mixed, up_far, down_far, down = sync(mixed, up_far, down_far, down)
        theirs, mine = call_window(
            functools.partial(mix_kernel, pairs), sums, "mix", (mixed,), attention_w, columns, 3
        )
        total, come = sum_heads(theirs, mine)
        down_far = down_far + [hop(piece, last) for piece in down[1:]]
        up_w = (stack(up), stack(up_far))
        if more:
            coming, next_up = tie((coming, up_held[layer + 1]), mixed)
            coming_far = [hop(coming, last)]
            coming = reach(coming)
            next_up = grow(next_up)
            come = tie(come, coming, next_up)
        come = tie(come, up_w)
        middle, normed_two, root_two, second_own = norm(layer, 1, hidden, total, come)
        second_in = (second_own, swap(second_own, 1))
        activated, slope = call(
            up_kernel,
            [((micro * rows, hidden_units), BF16), ((micro * rows, hidden_units), F32)],
            "up_project",
            *second_in,
            *up_w,
        )
        down_w = (stack(down, 1), stack(down_far, 1))
        activated = tie(activated, down_w)
        if more:
            theirs, mine = call(down_kernel, sums, "down_project", activated, *down_w)
            total, come = sum_heads(theirs, mine)
            coming_far = coming_far + [hop(piece, last) for piece in coming[1:]]
            next_up, next_down = tie((next_up, down_held[layer + 1]), second_in)
            next_up = reach(next_up)
            next_down = grow(next_down, 1)
            attention_next = (stack(coming), stack(coming_far))
            come = tie(come, next_up, next_down, coming_far[0])
        stored.append(
            (
                normed_one,
                root_one,
                first_in,
                qkv,
                mixed,
                mixed_t,
                lse,
                normed_two,
                root_two,
                second_in,
                activated,
                slope,
            )
        )
        weights.append((attention_w, up_w, down_w))
        if more:
            hidden, normed_one, root_one, first_own = norm(layer + 1, 0, middle, total, come)
            attention_w = attention_next
            up, down = next_up, next_down

    def all_rows(mine, other):
        ours = jnp.concatenate([mine, other], axis=0).reshape(micro, rows, width)
        return jnp.transpose(jnp.roll(ours, half * odd, axis=0), (1, 0, 2))

    def final(middle, activated, down_w):
        total, come = sum_heads(*call(down_kernel, sums, "down_project", activated, *down_w))
        result = middle + (total.astype(F32) + come.astype(F32))
        result = restore(offsets, shuffle, result.astype(BF16))
        return all_rows(result, swap(result, 1))

    class Gradient:
        def __init__(self, products, span, axis, name, *sources):
            self.products, self.axis, self.name, self.sources = products, axis, name, sources
            self.shape = (span, width // 4) if axis else (width // 4, span)
            self.ends = (span, width // 8) if axis else (width // 8, span)
            self.far = None

        def start(self, away=False):
            self.far = call(
                functools.partial(far_kernel, self.products),
                [(self.shape, BF16)] * 2,
                self.name + "_far",
                *self.sources,
                away=away,
            )

        def start_joined(self, away=False):
            span = self.shape[1]
            joined = call(
                functools.partial(joined_kernel, self.products),
                [((2 * self.shape[0], span), BF16)],
                self.name + "_far",
                *self.sources,
                away=away,
            )
            self.far = joined

        def hop_joined(self):
            self.first = self.second = hop(self.far, last)

        def hop_second(self):
            self.second = hop(self.far[1], last)

        def hop_first(self):
            self.first = hop(self.far[0], last)

        def send(self, away=False):
            self.sent = call(
                functools.partial(send_kernel, self.products),
                [(self.shape, BF16)],
                self.name + "_send",
                *self.sources,
                self.second,
                away=away,
            )

        def hop_sent(self):
            self.sent = hop(self.sent, bits[-2])

        def keep(self, away=False):
            self.kept = call(
                functools.partial(keep_kernel, self.products, self.axis),
                [(self.ends, F32), (self.ends, BF16)],
                self.name + "_keep",
                *self.sources,
                self.first,
                self.sent,
                away=away,
            )

        def hop_kept(self):
            self.kept = fold(self.kept, self.axis)

    upstream = own_rows(cotangent, shuffle)
    grad_own = upstream.astype(BF16)
    back_outs = [(half_shape, F32), (half_shape, BF16), ((2, width), F32)]

    def norm_back(layer, which, total, come, normed, root, upstream):
        return call(
            functools.partial(norm_back_kernel, row_of(layer, which)[0]),
            back_outs,
            "norm_back",
            total,
            come,
            normed,
            root,
            vectors,
            upstream,
        )

    vector_sums = {}
    up_grads, down_grads, qkv_grads, out_grads = [], [], [], []
    late_attention = late_up = None
    for layer in reversed(range(layers)):
        attention_w, up_w, down_w = weights[layer]
        (
            normed_one,
            root_one,
            first_in,
            qkv,
            mixed,
            mixed_t,
            lse,
            normed_two,
            root_two,
            second_in,
            activated,
            slope,
        ) = stored[layer]
        ending = layer == 0
        late = late_attention is not None
        grad_mlp = (grad_own, swap(grad_own, 1))
        down = Gradient(down_products, hidden_units, 1, "down", *grad_mlp, activated)
        down.start()
        down.hop_second()
        grad_mlp = tie(grad_mlp, down.far)
        inner, theirs, mine = call(
            dense_back_kernel,
            [((micro * rows, hidden_units), BF16)] + sums,
            "dense_back",
            *grad_mlp,
            *up_w,
            *down_w,
            slope,
        )
        if late:
            theirs = tie(theirs, late_attention.first)
        total, come = sum_heads(theirs, mine)
        up = Gradient(up_products, hidden_units, 0, "up", *second_in, inner)
        up.start()
        come = tie(come, up.far, down.second)
        if late:
            late_attention.send()
            late_attention.hop_sent()
            late_up.keep()
            come = tie(come, late_up.kept)
            come = tie(come, late_attention.sent)
        upstream, grad_own, vector_sums[layer, 1] = norm_back(
            layer, 1, total, come, normed_two, root_two, upstream
        )
        grad_attn = (grad_own, swap(grad_own, 1))
        grad_mixed = call_window(
            unmix_kernel,
            [((micro, pairs, rows, PAIR), BF16)],
            "unmix",
            grad_attn,
            attention_w,
            columns,
            3,
        )
        down.second = tie(down.second, grad_mixed)
        grad_mixed = to_units(grad_mixed.reshape(units, rows, PAIR))
        grad_mixed = exchange(grad_mixed).reshape(tokens, PAIR)
        if repeats > 1:
            grad_mixed = lax.dynamic_slice_in_dim(grad_mixed, start[0], query_rows, 0)
        down.send(True)
        down.far = tie(down.far, down.second)
        down.hop_first()
        grad_mixed = tie(grad_mixed, down.sent, down.first)
        if ending:
            out = Gradient(
                functools.partial(mix_products, pairs, 0), columns, 0, "out", *grad_attn, mixed
            )
            out.start(True)
            grad_mixed = tie(grad_mixed, out.far)
        if late:
            late_attention.keep(True)
            grad_mixed = tie(grad_mixed, late_attention.kept)
            late_up.kept = tie(late_up.kept, down.sent)
            late_up.hop_kept()
            late_attention.kept = tie(late_attention.kept, grad_mixed)
            late_attention.hop_kept()
        down.sent, up.far = tie((down.sent, up.far), grad_mixed)
        down.hop_sent()
        up.hop_second()
        packed_grad = attend_back(
            start, qkv, grad_mixed, mixed_t, lse, key_frames, query_frames, sequence_tables
        )
        packed_grad = tie(packed_grad, down.sent, up.second)
        if late:
            packed_grad = tie(packed_grad, late_attention.kept, late_up.kept)
            up_grads.append(late_up.kept)
            qkv_grads.append(late_attention.kept)
            out_grads.append(late_attention.kept)
        if layer + 1 == layers:
            middle, last_in = tie((middle, activated), packed_grad)
            outputs = final(middle, last_in, down_w)
        down.first, up.second, up.far = tie((down.first, up.second, up.far), packed_grad)
        packed_grad = from_units(exchange(packed_grad.reshape(tm_size, rows, 3 * PAIR)))
        down.keep(True)
        up.send(True)
        up.hop_first()
        packed_grad = tie(packed_grad, down.kept, up.sent, up.first)
        if ending:
            out.far = tie(out.far, down.first)
            out.hop_second()
            out.hop_first()
            down.hop_kept()
            packed_grad = tie(packed_grad, out.first, out.second, outputs, down.kept)
        if not ending:
            down.kept = tie(down.kept, packed_grad)
        up.sent = tie(up.sent, packed_grad)
        if ending:
            products = functools.partial(projection_products, pairs, range(3))
            group = Gradient(products, 3 * columns, 0, "qkv", *first_in, packed_grad)
            group.start()
            group.hop_second()
            group.hop_first()
            packed_grad = tie(packed_grad, group.far)
        theirs, mine = call(
            functools.partial(unproject_kernel, pairs),
            sums,
            "unproject",
            packed_grad,
            *attention_w,
        )
        total, come = sum_heads(theirs, mine)
        if not ending:
            down.hop_kept()
        up.hop_sent()
        down_grads.append(down.kept)
        if ending:
            out.second = tie(out.second, theirs)
            out.send()
            out.hop_sent()
            come = tie(come, group.second, up.sent, out.sent)
            group.second, up.sent, out.sent = tie((group.second, up.sent, out.sent), come)
            group.send()
            up.keep()
            out.keep()
            come = tie(come, group.sent, up.kept, out.kept)
            group.hop_sent()
            up.hop_kept()
            out.hop_kept()
        else:
            late_attention = Gradient(
                functools.partial(attention_products, pairs),
                4 * columns,
                0,
                "attention",
                *first_in,
                packed_grad,
                *grad_attn,
                mixed,
            )
            late_attention.sources = tie(late_attention.sources, total)
            late_attention.start_joined(True)
            late_attention.hop_joined()
            come = tie(come, down.kept, up.sent, late_attention.far)
        late_up = up
        upstream, grad_own, vector_sums[layer, 0] = norm_back(
            layer, 0, total, come, normed_one, root_one, upstream
        )
    restored = restore(offsets, shuffle, upstream)
    restored = (restored, swap(restored, 1))
    group.first = tie(group.first, restored, up.kept, out.kept)
    group.keep()
    vector_sums = tie(vector_sums, group.sent)
    names = [(layer, which) for layer in range(layers) for which in range(2)]
    small = jnp.concatenate(
        [vector_sums[name][kind : kind + 1] for kind in range(2) for name in names], axis=0
    )
    small = small + swap(small, 1)
    for bit in bits[::-1]:
        near, far = jnp.split(small, 2, axis=1)
        small = near + hop(far, bit)
    restored, done = tie(
        (restored, (up_grads, down_grads, out_grads, qkv_grads, up.kept, out.kept)), group.kept
    )
    up_grads, down_grads, out_grads, qkv_grads, up.kept, out.kept = done
    group.hop_kept()
    up_grads.append(up.kept)
    out_grads.append(out.kept)
    qkv_grads.append(group.kept)
    small = small.reshape(2, layers, 2, slices)
    return (
        outputs,
        all_rows(*restored),
        jnp.stack(
            [grad[:, : 3 * columns].reshape(slices, 3, columns) for grad in qkv_grads[::-1]]
        ),
        jnp.stack([grad[:, -columns:].T for grad in out_grads[::-1]]),
        jnp.stack(up_grads[::-1]),
        jnp.stack(down_grads[::-1]),
        small[0],
        small[1],
    )


def solution(mesh):
    placed = (
        P("tm", None, None),
        P(None, "tm", None, "head"),
        P(None, "head", "tm"),
        P(None, "tm", "head"),
        P(None, "head", "tm"),
        P(None, None, "tm"),
        P(None, None, "tm"),
        P("tm", None),
        P(None, "tm", None),
        P("tm", None, None),
    )
    return jax.shard_map(
        body,
        mesh=mesh,
        in_specs=placed,
        out_specs=(
            P("tm", None, None),
            P("tm", None, None),
            P(None, "tm", None, "head"),
            P(None, "head", "tm"),
            P(None, "tm", "head"),
            P(None, "head", "tm"),
            P(None, None, "tm"),
            P(None, None, "tm"),
        ),
        check_vma=False,
    )
```

```python
import functools

import jax
import jax.numpy as jnp
from jax import lax
from jax.experimental import pallas as pl
from jax.experimental.pallas import tpu as pltpu
from jax.sharding import PartitionSpec as P

HEAD_DIM = 64
PAIR = 2 * HEAD_DIM
GROUP = HEAD_DIM // 6
NEG_BIG = -1e30
F32 = jnp.float32
BF16 = jnp.bfloat16
NT = (((1,), (1,)), ((), ()))
TN = (((0,), (0,)), ((), ()))
NN = (((1,), (0,)), ((), ()))


def dot(left, right, dims):
    return lax.dot_general(left, right, dims, preferred_element_type=F32)


def rotary_tables(coordinates):
    lane = jnp.arange(PAIR, dtype=jnp.int32) % HEAD_DIM
    group = jnp.minimum(lane // (2 * GROUP), 2)
    place = lane % (2 * GROUP)
    turned = lane < 6 * GROUP
    first = turned & (place < GROUP)
    second = turned & (place >= GROUP)
    inverse = 10000.0 ** (-(place % GROUP).astype(F32) / GROUP)
    spread = jnp.where(
        group == 0,
        coordinates[:, 0:1],
        jnp.where(group == 1, coordinates[:, 1:2], coordinates[:, 2:3]),
    )
    angles = spread * inverse
    cosine = jnp.where(turned, jnp.cos(angles), 1.0)
    sine = jnp.sin(angles)
    return (cosine, jnp.where(first, -sine, 0.0), jnp.where(second, sine, 0.0))


def turn(values, cosine, sine_first, sine_second):
    ahead = pltpu.roll(values, PAIR - GROUP, 1)
    behind = pltpu.roll(values, GROUP, 1)
    return values * cosine + ahead * sine_first + behind * sine_second


def turn_back(values, cosine, sine_first, sine_second):
    ahead = pltpu.roll(values, PAIR - GROUP, 1)
    behind = pltpu.roll(values, GROUP, 1)
    return values * cosine - ahead * sine_first - behind * sine_second


def project_kernel(own, peer, left, right, cosine, sine_first, sine_second, out):
    rows = out.shape[2]
    width = out.shape[1] * PAIR
    middle = left.shape[0]
    for step, acts in enumerate((own, peer)):
        span = pl.ds(step * 2 * rows, 2 * rows)
        raw = dot(acts[:, :middle], left[:, : 3 * width], NN)
        raw += dot(acts[:, middle:], right[:, : 3 * width], NN)
        tables = (cosine[span, :], sine_first[span, :], sine_second[span, :])
        for pair in range(out.shape[1]):
            for part in range(3):
                start = part * width + pair * PAIR
                piece = raw[:, start : start + PAIR]
                if part < 2:
                    piece = turn(piece, *tables)
                piece = piece.astype(BF16)
                for half in range(2):
                    out[2 * step + half, pair, :, part * PAIR : (part + 1) * PAIR] = piece[
                        half * rows : (half + 1) * rows
                    ]


def unit_rows(tiles, micros, pairs, lanes):
    return jnp.concatenate(
        [
            jnp.concatenate([tiles[micro * pairs + pair, :, lanes] for pair in range(pairs)], axis=1)
            for micro in micros
        ],
        axis=0,
    )


def mix_kernel(pairs, mixed, left, right, theirs, mine):
    width = pairs * PAIR
    micro = mixed.shape[0] // pairs
    middle = left.shape[0]
    skip = left.shape[1] - width
    for micros, out in ((range(micro // 2, micro), theirs), (range(micro // 2), mine)):
        rows = unit_rows(mixed, micros, pairs, slice(0, PAIR))
        out[:, :middle] = dot(rows, left[:, skip:], NT).astype(out.dtype)
        out[:, middle:] = dot(rows, right[:, skip:], NT).astype(out.dtype)


def unmix_kernel(own, peer, left, right, out):
    rows = out.shape[2]
    width = out.shape[1] * PAIR
    middle = left.shape[0]
    skip = left.shape[1] - width
    for step, acts in enumerate((own, peer)):
        raw = dot(acts[:, :middle], left[:, skip:], NN) + dot(acts[:, middle:], right[:, skip:], NN)
        raw = raw.astype(BF16)
        for pair in range(out.shape[1]):
            for half in range(2):
                out[2 * step + half, pair] = raw[
                    half * rows : (half + 1) * rows, pair * PAIR : (pair + 1) * PAIR
                ]


def unproject_kernel(pairs, packed, left, right, theirs, mine):
    width = pairs * PAIR
    micro = packed.shape[0] // pairs
    middle = left.shape[0]
    for micros, out in ((range(micro // 2, micro), theirs), (range(micro // 2), mine)):
        for weights, place in ((left, slice(0, middle)), (right, slice(middle, 2 * middle))):
            total = 0.0
            for part in range(3):
                rows = unit_rows(packed, micros, pairs, slice(part * PAIR, (part + 1) * PAIR))
                total += dot(rows, weights[:, part * width : (part + 1) * width], NT)
            out[:, place] = total.astype(out.dtype)


def up_kernel(own, peer, left, right, activated, slope):
    middle = left.shape[0]
    half = own.shape[0]
    for start in range(0, activated.shape[1], 256):
        block = slice(start, start + 256)
        for step, acts in enumerate((own, peer)):
            upward = dot(acts[:, :middle], left[:, block], NN)
            upward += dot(acts[:, middle:], right[:, block], NN)
            bell = 0.5 * (1.0 + lax.erf(upward * 0.7071067811865476))
            span = slice(step * half, (step + 1) * half)
            activated[span, block] = (upward * bell).astype(BF16)
            slope[span, block] = (
                bell + upward * jnp.exp(-0.5 * upward * upward) * 0.3989422804014327
            )


def down_kernel(activated, left, right, theirs, mine):
    half = mine.shape[0]
    middle = left.shape[1]
    for span, out in ((slice(half, 2 * half), theirs), (slice(0, half), mine)):
        out[:, :middle] = dot(activated[span, :], left[...], NN).astype(out.dtype)
        out[:, middle:] = dot(activated[span, :], right[...], NN).astype(out.dtype)


def dense_back_kernel(own, peer, up_left, up_right, down_left, down_right, slope, inner, theirs, mine):
    half = mine.shape[0]
    middle = up_left.shape[0]
    for acts, span, out in (
        (peer, slice(half, 2 * half), theirs),
        (own, slice(0, half), mine),
    ):
        raw = dot(acts[:, :middle], down_left[...], NT)
        raw += dot(acts[:, middle:], down_right[...], NT)
        grad = (raw * slope[span, :]).astype(BF16)
        inner[span, :] = grad
        out[:, :middle] = dot(grad, up_left[...], NT).astype(out.dtype)
        out[:, middle:] = dot(grad, up_right[...], NT).astype(out.dtype)


def pair_kernel(mine, come, total):
    total[...] = (mine[...] + come[...].astype(F32)).astype(BF16)


def normalized(hidden, gain, bias):
    centered = hidden - jnp.mean(hidden, axis=-1, keepdims=True)
    root = lax.rsqrt(jnp.mean(centered * centered, axis=-1, keepdims=True) + 1e-06)
    normed = centered * root
    return normed, root, (normed * gain + bias).astype(BF16)


def first_norm_kernel(gain, bias, hidden, vectors, normed, root, out):
    normed[...], scale, out[...] = normalized(
        hidden[...], vectors[gain : gain + 1, :], vectors[bias : bias + 1, :]
    )
    root[...] = jnp.broadcast_to(scale, root.shape)


def norm_kernel(gain, bias, hidden, total, come, vectors, result, normed, root, out):
    value = hidden[...] + (total[...].astype(F32) + come[...].astype(F32))
    result[...] = value
    normed[...], scale, out[...] = normalized(
        value, vectors[gain : gain + 1, :], vectors[bias : bias + 1, :]
    )
    root[...] = jnp.broadcast_to(scale, root.shape)


def norm_back_kernel(gain, total, come, normed, root, vectors, upstream, result, out, sums):
    grad = total[...].astype(F32) + come[...].astype(F32)
    known = normed[...]
    sums[0:1, :] = jnp.sum(grad * known, axis=0, keepdims=True)
    sums[1:2, :] = jnp.sum(grad, axis=0, keepdims=True)
    scaled = grad * vectors[gain : gain + 1, :]
    value = upstream[...] + root[:, 0:1] * (
        scaled
        - jnp.mean(scaled, axis=-1, keepdims=True)
        - known * jnp.mean(scaled * known, axis=-1, keepdims=True)
    )
    result[...] = value
    out[...] = value.astype(BF16)


def quarter_of(own, peer, quarter):
    size = own.shape[1] // 4
    span = slice(quarter * size, (quarter + 1) * size)
    return jnp.concatenate([own[:, span], peer[:, span]], axis=0)


def up_products(quarter, own, peer, inner):
    rows = quarter_of(own, peer, quarter)
    for start in range(0, inner.shape[1], 256):
        span = slice(start, start + 256)
        yield (slice(None), span), dot(rows, inner[:, span], TN)


def down_products(quarter, own, peer, activated):
    rows = quarter_of(own, peer, quarter)
    for start in range(0, activated.shape[1], 256):
        span = slice(start, start + 256)
        yield (span, slice(None)), dot(activated[:, span], rows, TN)


def projection_products(pairs, parts, quarter, own, peer, packed):
    rows = quarter_of(own, peer, quarter)
    micros = range(packed.shape[0] // pairs)
    for place, part in enumerate(parts):
        other = unit_rows(packed, micros, pairs, slice(part * PAIR, (part + 1) * PAIR))
        span = slice(place * pairs * PAIR, (place + 1) * pairs * PAIR)
        yield (slice(None), span), dot(rows, other, TN)


def mix_products(pairs, start, quarter, own, peer, mixed):
    rows = quarter_of(own, peer, quarter)
    micros = range(mixed.shape[0] // pairs)
    other = unit_rows(mixed, micros, pairs, slice(0, PAIR))
    yield (slice(None), slice(start, start + pairs * PAIR)), dot(rows, other, TN)


def attention_products(pairs, quarter, own, peer, packed, grad_own, grad_peer, mixed):
    yield from projection_products(pairs, range(3), quarter, own, peer, packed)
    yield from mix_products(pairs, 3 * pairs * PAIR, quarter, grad_own, grad_peer, mixed)


def far_kernel(products, *refs):
    for quarter, out in ((2, refs[-2]), (3, refs[-1])):
        for place, value in products(quarter, *refs[:-2]):
            out[place] = value.astype(BF16)


def joined_kernel(products, *refs):
    out = refs[-1]
    size = out.shape[0] // 2
    for side, quarter in enumerate((2, 3)):
        for (rows, columns), value in products(quarter, *refs[:-1]):
            out[side * size : (side + 1) * size, columns] = value.astype(BF16)


def send_kernel(products, *refs):
    arrived, out = refs[-2:]
    if arrived.shape[0] == 2 * out.shape[0]:
        arrived = arrived.at[out.shape[0] :]
    for place, value in products(1, *refs[:-2]):
        out[place] = (value + arrived[place].astype(F32)).astype(BF16)


def keep_kernel(products, axis, *refs):
    arrived, folded, keep, send = refs[-4:]
    half = keep.shape[axis]
    if arrived.shape[0] == 2 * folded.shape[0]:
        arrived = arrived.at[: folded.shape[0]]
    for place, value in products(0, *refs[:-4]):
        value = value + arrived[place].astype(F32) + folded[place].astype(F32)
        if axis:
            keep[place] = value[:, :half]
            send[place] = value[:, half:].astype(BF16)
        else:
            keep[place] = value[:half]
            send[place] = value[half:].astype(BF16)


def lane_mask(shape, head):
    lane = lax.broadcasted_iota(jnp.int32, shape, 1)
    return (lane >= head * HEAD_DIM) & (lane < (head + 1) * HEAD_DIM)


def tagged(vectors, frames, head, value):
    lane = lax.broadcasted_iota(jnp.int32, vectors.shape, 1)
    first = (1 - head) * HEAD_DIM
    tags = value((lane - first).astype(F32), frames)
    return jnp.where(lane_mask(vectors.shape, head), vectors.astype(F32), tags).astype(BF16)


def key_tags(vectors, frames, head):
    return tagged(vectors, frames, head, lambda lane, frame: jnp.where(lane == frame, 1.0, 0.0))


def query_tags(vectors, frames, head):
    return tagged(vectors, frames, head, lambda lane, frame: jnp.where(lane > frame, NEG_BIG, 0.0))


def attend_kernel(block, start, qkv, key_frames, out, out_t, lse):
    frames = key_frames[...]
    keys = [key_tags(qkv[:, PAIR : 2 * PAIR], frames, head) for head in range(2)]
    value_t = jnp.transpose(qkv[:, 2 * PAIR :].astype(F32))
    ones = jnp.ones((16, value_t.shape[1]), F32)
    values = [
        jnp.concatenate([value_t[head * HEAD_DIM : (head + 1) * HEAD_DIM], ones], axis=0).astype(
            BF16
        )
        for head in range(2)
    ]
    query_rows = out.shape[0]

    def one(step, carry):
        place = pl.multiple_of(step * block, block)
        source = pl.multiple_of(start[0] + step * block, block)
        queries = qkv[pl.ds(source, block), :PAIR] * jnp.asarray(HEAD_DIM**-0.5, BF16)
        own_frames = key_frames[pl.ds(source, block), :]
        pieces = []
        for head in range(2):
            scores = dot(keys[head], query_tags(queries, own_frames, head), NT)
            top = jnp.max(scores, axis=0, keepdims=True)
            summed = dot(values[head], jnp.exp(scores - top).astype(BF16), NN)
            total = summed[HEAD_DIM : HEAD_DIM + 1]
            pieces.append(summed[:HEAD_DIM] / total)
            lse[head : head + 1, pl.ds(place, block)] = top + jnp.log(total)
        both = jnp.concatenate(pieces, axis=0)
        out_t[:, pl.ds(place, block)] = both
        out[pl.ds(place, block), :] = jnp.transpose(both).astype(BF16)
        return carry

    lax.fori_loop(0, query_rows // block, one, 0)


def attend_back_kernel(
    block,
    start,
    qkv,
    grad_out,
    out_t,
    lse,
    key_frames,
    cosine,
    sine_first,
    sine_second,
    result,
    key_sum,
    value_sum,
):
    key_vecs = qkv[:, PAIR : 2 * PAIR]
    frames = key_frames[...]
    keys = [key_tags(key_vecs, frames, head) for head in range(2)]
    value_vecs = qkv[:, 2 * PAIR :]
    key_t = jnp.transpose(key_vecs.astype(F32)).astype(BF16)
    query_rows = grad_out.shape[0]
    key_sum[...] = jnp.zeros_like(key_sum)
    value_sum[...] = jnp.zeros_like(value_sum)
    if query_rows != qkv.shape[0]:
        result[:, :PAIR] = jnp.zeros((qkv.shape[0], PAIR), BF16)

    def one(step, carry):
        place = pl.multiple_of(step * block, block)
        source = pl.multiple_of(start[0] + step * block, block)
        queries = qkv[pl.ds(source, block), :PAIR] * jnp.asarray(HEAD_DIM**-0.5, BF16)
        upstream = grad_out[pl.ds(place, block), :]
        own_frames = key_frames[pl.ds(source, block), :]
        both = out_t[:, pl.ds(place, block)] * jnp.transpose(upstream.astype(F32))
        pieces = []
        for head in range(2):
            keep = lane_mask(queries.shape, head)
            mine = jnp.where(keep, queries, jnp.zeros_like(queries))
            above = jnp.where(keep, upstream, jnp.zeros_like(upstream))
            rows = slice(head * HEAD_DIM, (head + 1) * HEAD_DIM)
            delta = jnp.sum(both[rows], axis=0, keepdims=True)
            log_total = lse[head : head + 1, pl.ds(place, block)]
            scores = dot(keys[head], query_tags(queries, own_frames, head), NT)
            weights = jnp.exp(scores - log_total)
            slope = (weights * (dot(value_vecs, above, NT) - delta)).astype(BF16)
            value_sum[...] += dot(weights.astype(BF16), above, NN)
            key_sum[...] += dot(slope, mine, NN)
            pieces.append(dot(key_t[rows], slope, NN))
        query_grad = jnp.transpose(jnp.concatenate(pieces, axis=0)) * HEAD_DIM**-0.5
        span = pl.ds(source, block)
        result[span, :PAIR] = turn_back(
            query_grad, cosine[span, :], sine_first[span, :], sine_second[span, :]
        ).astype(BF16)
        return carry

    lax.fori_loop(0, query_rows // block, one, 0)
    result[:, PAIR : 2 * PAIR] = turn_back(
        key_sum[...], cosine[...], sine_first[...], sine_second[...]
    ).astype(BF16)
    result[:, 2 * PAIR :] = value_sum[...].astype(BF16)


def whole():
    return pl.BlockSpec(memory_space=pltpu.VMEM)


def scalars():
    return pl.BlockSpec(memory_space=pltpu.SMEM)


def call(kernel, outs, name, *operands, numbers=(), scratch=(), scale=1, away=False):
    shapes = [(jax.ShapeDtypeStruct if away else pltpu.VMEM)(shape, kind) for shape, kind in outs]
    memory = pltpu.HBM if away else pltpu.VMEM
    operands = [pltpu.with_memory_space_constraint(operand, memory) for operand in operands]
    single = len(shapes) == 1
    return pl.pallas_call(
        kernel,
        out_shape=shapes[0] if single else shapes,
        in_specs=[scalars()] * len(numbers) + [whole()] * len(operands),
        out_specs=whole() if single else [whole()] * len(shapes),
        scratch_shapes=scratch,
        compiler_params=pltpu.CompilerParams(vmem_limit_bytes=scale * 10 * 1024 * 1024),
        name=name,
    )(*numbers, *operands)


def strip_kernel(*refs):
    pieces, (left, right, extras, vectors) = refs[:-4], refs[-4:]
    count = len(pieces)
    size = left.shape[0] // (count // 2)
    for place, piece in enumerate(pieces):
        out = (left, right)[place // (count // 2)]
        first = place % (count // 2) * size
        out[first : first + size, :] = piece[:size, :]
        extras[place] = piece[size:, :]
        extra = piece[size:, :].astype(F32)
        for row in range(vectors.shape[0]):
            start = row * size
            lanes = start % extra.shape[1]
            line = start // extra.shape[1]
            vectors[row : row + 1, place * size : (place + 1) * size] = extra[
                line : line + 1, lanes : lanes + size
            ]


def shard_kernel(qkv, out, result):
    width = qkv.shape[3]
    for part in range(3):
        result[:, part * width : (part + 1) * width] = qkv[0, :, part, :].astype(BF16)
    result[:, 3 * width :] = jnp.transpose(out[0]).astype(BF16)


def shard(layer, qkv_all, out_all):
    rows, width = qkv_all.shape[1], qkv_all.shape[3]
    return pl.pallas_call(
        shard_kernel,
        grid=(1,),
        out_shape=jax.ShapeDtypeStruct((rows, 4 * width), BF16),
        in_specs=[
            pl.BlockSpec((1,) + qkv_all.shape[1:], lambda i: (layer, 0, 0, 0)),
            pl.BlockSpec((1,) + out_all.shape[1:], lambda i: (layer, 0, 0)),
        ],
        out_specs=pl.BlockSpec((rows, 4 * width), lambda i: (0, 0)),
        compiler_params=pltpu.CompilerParams(vmem_limit_bytes=10 * 1024 * 1024),
        name="shard",
    )(qkv_all, out_all)


def call_window(kernel, outs, name, operands, weights, width, index):
    shapes = [jax.ShapeDtypeStruct(shape, kind) for shape, kind in outs]

    def full(shape):
        return pl.BlockSpec(shape, lambda i: (0,) * len(shape))

    single = len(shapes) == 1
    specs = [full(shape) for shape, kind in outs]
    return pl.pallas_call(
        kernel,
        grid=(1,),
        out_shape=shapes[0] if single else shapes,
        in_specs=[full(operand.shape) for operand in operands]
        + [pl.BlockSpec((part.shape[0], width), lambda i: (0, index)) for part in weights],
        out_specs=specs[0] if single else specs,
        compiler_params=pltpu.CompilerParams(vmem_limit_bytes=10 * 1024 * 1024),
        name=name,
    )(*operands, *weights)


def attend(start, qkv, key_frames, query_rows):
    return call(
        functools.partial(attend_kernel, 512),
        [((query_rows, PAIR), BF16), ((PAIR, query_rows), F32), ((2, query_rows), F32)],
        "attend",
        qkv,
        key_frames,
        numbers=(start,),
        scale=max(2, 2 * qkv.shape[0] // 1024),
        away=True,
    )


def attend_back(start, qkv, grad_out, out_t, lse, key_frames, tables):
    return call(
        functools.partial(attend_back_kernel, 512),
        [(qkv.shape, BF16)],
        "attend_back",
        qkv,
        grad_out,
        out_t,
        lse,
        key_frames,
        *tables,
        numbers=(start,),
        scratch=[pltpu.VMEM((qkv.shape[0], PAIR), F32)] * 2,
        scale=max(2, 2 * qkv.shape[0] // 1024),
        away=True,
    )


def restore_kernel(places, values, out):
    size = values.shape[1] // places.shape[0]
    for block in range(places.shape[0]):
        place = pl.multiple_of(places[block], size)
        out[:, pl.ds(place, size)] = values[:, block * size : (block + 1) * size]


def restore(places, shuffle, values):
    if values.shape[1] // places.shape[0] % 128 == 0:
        return call(restore_kernel, [(values.shape, values.dtype)], "restore", values, numbers=(places,))
    exact = lax.Precision.HIGHEST
    return lax.dot_general(
        values.astype(F32), shuffle.astype(F32), NT, precision=exact
    ).astype(values.dtype)


def body(
    inputs,
    qkv_master,
    out_master,
    up_master,
    down_master,
    norm_gain,
    norm_bias,
    frame_ids,
    patch_pos,
    cotangent,
):
    rows, micro, width = inputs.shape
    tm_size = lax.axis_size("tm")
    head_size = lax.axis_size("head")
    here = lax.axis_index("tm")
    layers = qkv_master.shape[0]
    columns = qkv_master.shape[3]
    hidden_units = up_master.shape[2]
    slices = width // tm_size
    half = micro // 2
    half_rows = half * rows
    odd = lax.axis_index("head") % 2
    pairs = columns // PAIR
    units = micro * pairs
    repeats = tm_size // units
    tokens = rows * tm_size
    query_rows = tokens // repeats

    bits = []
    order = [0]
    bit = tm_size // 2
    while bit:
        bits.append(bit)
        order = order + [place | bit for place in order]
        bit //= 2
    last = bits[-1]

    def sync(*values):
        return lax.optimization_barrier(values)

    def tie(value, *others):
        return sync(value, others)[0]

    def hop(values, bit):
        return lax.ppermute(values, "tm", [(i, i ^ bit) for i in range(tm_size)])

    def swap(values, bit):
        return lax.ppermute(values, "head", [(i, i ^ bit) for i in range(head_size)])

    half_shape = (half_rows, width)
    sums = [(half_shape, BF16), (half_shape, F32)]

    def sum_heads(theirs, mine):
        total = call(pair_kernel, [(half_shape, BF16)], "pair", mine, swap(theirs, 1))
        bit = 2
        while 2 * bit < head_size:
            total = sync((total.astype(F32) + swap(total, bit).astype(F32)).astype(BF16))[0]
            bit *= 2
        return total, swap(total, bit)

    def exchange(values):
        return lax.all_to_all(values, "tm", 0, 0, tiled=True)

    def grow(held, axis=0):
        return jnp.concatenate([held, hop(held, bits[0])], axis=axis)

    def reach(held, axis=0):
        pieces = [held]
        for bit in bits[1:-1]:
            so_far = jnp.concatenate(pieces, axis=axis) if len(pieces) > 1 else held
            pieces.append(hop(so_far, bit))
        return pieces

    def stack(pieces, axis=0):
        return jnp.concatenate(pieces, axis=axis)

    def fold(parts, axis=0):
        keep, send = parts
        for bit in bits[-3::-1]:
            total = keep + hop(send, bit).astype(F32)
            if bit == bits[0]:
                return total
            keep, send = jnp.split(total, 2, axis=axis)
            send = send.astype(BF16)

    def own_rows(values, shuffle):
        mine = lax.dynamic_slice_in_dim(values, half * odd, half, 1)
        mine = jnp.transpose(mine, (1, 0, 2)).reshape(half_rows, width)
        return dot(mine, shuffle, NN)

    def to_units(values):
        return jnp.repeat(values, repeats, axis=0) if repeats > 1 else values

    def from_units(values):
        if repeats == 1:
            return values
        grouped = values.reshape((units, repeats) + values.shape[1:]).astype(F32)
        return jnp.sum(grouped, axis=1).astype(BF16)

    def attention_shard(layer, qkv_all, out_all):
        if slices % 128 == 0:
            return shard(layer, qkv_all, out_all)
        return jnp.concatenate(
            [
                qkv_all[layer].astype(BF16).reshape(slices, 3 * columns),
                out_all[layer].astype(BF16).T,
            ],
            axis=1,
        )

    ordered = (jnp.arange(micro) + half * odd) % micro
    whole_numbers = jnp.concatenate([frame_ids[None], patch_pos], axis=0).astype(F32)
    whole_numbers = jnp.take(jnp.transpose(whole_numbers, (2, 0, 1)), ordered, axis=0)
    vectors = jnp.concatenate([norm_gain, norm_bias], axis=0)
    extra = jnp.concatenate([vectors.reshape(-1), whole_numbers.reshape(-1)]).astype(BF16)
    extra = jnp.pad(extra, (0, 8 * 4 * columns - extra.size)).reshape(8, 4 * columns)

    pieces = {
        0: jnp.concatenate([attention_shard(0, qkv_master, out_master), extra], axis=0)
    }
    for bit in bits:
        pieces[bit] = hop(pieces[0], bit)

    early = [pieces.pop(bit) for bit in bits[:-1]]
    masters = (qkv_master, out_master, up_master, down_master)
    early, inputs, whole_numbers, here, masters = sync(
        early, inputs, whole_numbers, here, masters
    )
    qkv_master, out_master, up_master, down_master = masters
    attention_held = [None] + [
        attention_shard(layer, qkv_master, out_master) for layer in range(1, layers)
    ]
    up_held = [up_master[layer].astype(BF16) for layer in range(layers)]
    down_held = [down_master[layer].astype(BF16) for layer in range(layers)]
    up, down = up_held[0], down_held[0]
    pieces.update(zip(bits[:-1], early))
    for bit in bits:
        for place in [place for place in order if place and place & (bit - 1) == 0]:
            if place & bit and place not in pieces:
                pieces[place] = hop(pieces[place ^ bit], bit)
    up = grow(up)
    down = grow(down, 1)
    feature = jnp.arange(width, dtype=jnp.int32)
    origin = (here ^ jnp.asarray(order, jnp.int32)[:, None]) * slices + jnp.arange(
        slices, dtype=jnp.int32
    )
    offsets = origin[:, 0]
    shuffle = (feature[:, None] == origin.reshape(1, width)).astype(BF16)
    row_tables = rotary_tables(jnp.transpose(whole_numbers, (0, 2, 1)).reshape(micro * rows, 3))
    start = ((here % repeats) * query_rows).reshape(1)

    hidden = own_rows(inputs, shuffle)
    root_shape = (half_rows, 128)
    norm_outs = [(half_shape, F32), (root_shape, F32), (half_shape, BF16)]

    def row_of(layer, which):
        return 2 * layer + which, 2 * layers + 2 * layer + which

    def norm(layer, which, hidden, total, come):
        return call(
            functools.partial(norm_kernel, *row_of(layer, which)),
            [(half_shape, F32)] + norm_outs,
            "norm",
            hidden,
            total,
            come,
            vectors,
        )

    hidden, attention_held[1:], row_tables = sync(hidden, attention_held[1:], row_tables)
    hidden, pieces, up, down = sync(hidden, pieces, up, down)
    if slices % 128 == 0:
        left, right, extras, vectors = call(
            strip_kernel,
            [((width // 2, 4 * columns), BF16)] * 2
            + [((tm_size, 8, 4 * columns), BF16), ((4 * layers, width), F32)],
            "strip",
            *[pieces[place] for place in order],
        )
        attention_w = (left, right)
        extras = extras.reshape(tm_size, -1)
    else:
        extras = jnp.stack([pieces[place][slices:].reshape(-1) for place in order])
        vectors = extras[:, : vectors.size].reshape(tm_size, 4 * layers, slices).astype(F32)
        vectors = jnp.transpose(vectors, (1, 0, 2)).reshape(4 * layers, width)
        attention_w = tuple(
            stack([pieces[place][:slices] for place in places_of])
            for places_of in (order[: tm_size // 2], order[tm_size // 2 :])
        )
    numbers = extras[:, 4 * layers * slices : 4 * layers * slices + 3 * rows * micro]
    numbers = lax.dynamic_index_in_dim(
        numbers.reshape(tm_size, micro, 3 * rows), here // (tm_size // micro), 1, keepdims=False
    )
    devices = jnp.arange(tm_size, dtype=jnp.int32)
    origins = (devices[:, None] == (here ^ jnp.asarray(order, jnp.int32))[None, :]).astype(BF16)
    places = dot(origins, numbers, NN).reshape(tm_size, 3, rows)
    places = jnp.transpose(places, (1, 0, 2)).reshape(3, tokens)
    normed_one, root_one, first_own = call(
        functools.partial(first_norm_kernel, *row_of(0, 0)), norm_outs, "first_norm", hidden, vectors
    )
    stored = []
    weights = []
    for layer in range(layers):
        more = layer + 1 < layers
        first_in = (first_own, swap(first_own, 1))
        first_in, attention_w = sync(first_in, attention_w)
        first_in, down = sync(first_in, down)
        up = tie(up, first_in)
        packed = call(
            project_kernel,
            [((micro, pairs, rows, 3 * PAIR), BF16)],
            "project",
            *first_in,
            *attention_w,
            *row_tables,
        )
        up, down = tie((up, down), packed)
        packed = to_units(packed.reshape(units, rows, 3 * PAIR))
        qkv = exchange(packed).reshape(tokens, 3 * PAIR)
        down_far = []
        if layer == 0:
            up = reach(up)
            sequence_tables = rotary_tables(places.T)
            key_frames = jnp.broadcast_to(places[0][:, None], (tokens, 128))
            qkv, sequence_tables, key_frames = sync(qkv, sequence_tables, key_frames)
        up_far = [hop(up[0], last)]
        qkv, up_far = sync(qkv, up_far)
        if layer == 0:
            down_far = [hop(down, last)]
        down = reach(down, 1)
        if layer:
            up_far = up_far + [hop(piece, last) for piece in tie(up[1:], qkv)]
        if more:
            coming = tie(attention_held[layer + 1], packed)
            coming = (coming, hop(coming, bits[0]))
        mixed, mixed_t, lse = attend(start, qkv, key_frames, query_rows)
        if repeats > 1:
            mixed = lax.dynamic_update_slice_in_dim(
                jnp.zeros((tokens, PAIR), BF16), mixed, start[0], 0
            )
        mixed, up_far, up, down_far = sync(mixed, up_far, up, down_far)
        if more:
            mixed, coming = sync(mixed, coming)
        mixed = from_units(exchange(mixed.reshape(tm_size, rows, PAIR)))
        if layer:
            down_far = [hop(down[0], last)]
        else:
            up_far = up_far + [hop(piece, last) for piece in up[1:]]
        mixed, up_far, down_far, down = sync(mixed, up_far, down_far, down)
        theirs, mine = call_window(
            functools.partial(mix_kernel, pairs), sums, "mix", (mixed,), attention_w, columns, 3
        )
        total, come = sum_heads(theirs, mine)
        down_far = down_far + [hop(piece, last) for piece in down[1:]]
        up_w = (stack(up), stack(up_far))
        if more:
            coming, next_up = tie((coming, up_held[layer + 1]), mixed)
            coming = stack(coming)
            coming_far = [hop(coming, last)]
            coming = reach(coming)
            next_up = grow(next_up)
            come = tie(come, coming, next_up)
        come = tie(come, up_w)
        middle, normed_two, root_two, second_own = norm(layer, 1, hidden, total, come)
        second_in = (second_own, swap(second_own, 1))
        activated, slope = call(
            up_kernel,
            [((micro * rows, hidden_units), BF16), ((micro * rows, hidden_units), F32)],
            "up_project",
            *second_in,
            *up_w,
        )
        down_w = (stack(down, 1), stack(down_far, 1))
        activated = tie(activated, down_w)
        if more:
            theirs, mine = call(down_kernel, sums, "down_project", activated, *down_w)
            total, come = sum_heads(theirs, mine)
            coming_far = coming_far + [hop(piece, last) for piece in coming[1:]]
            next_up, next_down = tie((next_up, down_held[layer + 1]), second_in)
            next_up = reach(next_up)
            next_down = grow(next_down, 1)
            attention_next = (stack(coming), stack(coming_far))
            come = tie(come, next_up, next_down, coming_far[0])
        stored.append(
            (
                normed_one,
                root_one,
                first_in,
                qkv,
                mixed,
                mixed_t,
                lse,
                normed_two,
                root_two,
                second_in,
                activated,
                slope,
            )
        )
        weights.append((attention_w, up_w, down_w))
        if more:
            hidden, normed_one, root_one, first_own = norm(layer + 1, 0, middle, total, come)
            attention_w = attention_next
            up, down = next_up, next_down

    def all_rows(mine, other):
        ours = jnp.concatenate([mine, other], axis=0).reshape(micro, rows, width)
        return jnp.transpose(jnp.roll(ours, half * odd, axis=0), (1, 0, 2))

    def final(middle, activated, down_w):
        total, come = sum_heads(*call(down_kernel, sums, "down_project", activated, *down_w))
        result = middle + (total.astype(F32) + come.astype(F32))
        result = restore(offsets, shuffle, result.astype(BF16))
        return all_rows(result, swap(result, 1))

    class Gradient:
        def __init__(self, products, span, axis, name, *sources):
            self.products, self.axis, self.name, self.sources = products, axis, name, sources
            self.shape = (span, width // 4) if axis else (width // 4, span)
            self.ends = (span, width // 8) if axis else (width // 8, span)
            self.far = None

        def start(self, away=False):
            self.far = call(
                functools.partial(far_kernel, self.products),
                [(self.shape, BF16)] * 2,
                self.name + "_far",
                *self.sources,
                away=away,
            )

        def start_joined(self, away=False):
            span = self.shape[1]
            joined = call(
                functools.partial(joined_kernel, self.products),
                [((2 * self.shape[0], span), BF16)],
                self.name + "_far",
                *self.sources,
                away=away,
            )
            self.far = joined

        def hop_joined(self):
            self.first = self.second = hop(self.far, last)

        def hop_second(self):
            self.second = hop(self.far[1], last)

        def hop_first(self):
            self.first = hop(self.far[0], last)

        def send(self, away=False):
            self.sent = call(
                functools.partial(send_kernel, self.products),
                [(self.shape, BF16)],
                self.name + "_send",
                *self.sources,
                self.second,
                away=away,
            )

        def hop_sent(self):
            self.sent = hop(self.sent, bits[-2])

        def keep(self, away=False):
            self.kept = call(
                functools.partial(keep_kernel, self.products, self.axis),
                [(self.ends, F32), (self.ends, BF16)],
                self.name + "_keep",
                *self.sources,
                self.first,
                self.sent,
                away=away,
            )

        def hop_kept(self):
            self.kept = fold(self.kept, self.axis)

    upstream = own_rows(cotangent, shuffle)
    grad_own = upstream.astype(BF16)
    back_outs = [(half_shape, F32), (half_shape, BF16), ((2, width), F32)]

    def norm_back(layer, which, total, come, normed, root, upstream):
        return call(
            functools.partial(norm_back_kernel, row_of(layer, which)[0]),
            back_outs,
            "norm_back",
            total,
            come,
            normed,
            root,
            vectors,
            upstream,
        )

    vector_sums = {}
    up_grads, down_grads, qkv_grads, out_grads = [], [], [], []
    late_attention = late_up = None
    for layer in reversed(range(layers)):
        attention_w, up_w, down_w = weights[layer]
        (
            normed_one,
            root_one,
            first_in,
            qkv,
            mixed,
            mixed_t,
            lse,
            normed_two,
            root_two,
            second_in,
            activated,
            slope,
        ) = stored[layer]
        ending = layer == 0
        late = late_attention is not None
        grad_mlp = (grad_own, swap(grad_own, 1))
        down = Gradient(down_products, hidden_units, 1, "down", *grad_mlp, activated)
        down.start()
        down.hop_second()
        grad_mlp = tie(grad_mlp, down.far)
        inner, theirs, mine = call(
            dense_back_kernel,
            [((micro * rows, hidden_units), BF16)] + sums,
            "dense_back",
            *grad_mlp,
            *up_w,
            *down_w,
            slope,
        )
        if late:
            theirs = tie(theirs, late_attention.first)
        total, come = sum_heads(theirs, mine)
        up = Gradient(up_products, hidden_units, 0, "up", *second_in, inner)
        up.start()
        come = tie(come, up.far, down.second)
        if late:
            late_attention.send()
            late_attention.hop_sent()
            late_up.keep()
            come = tie(come, late_up.kept)
            come = tie(come, late_attention.sent)
        upstream, grad_own, vector_sums[layer, 1] = norm_back(
            layer, 1, total, come, normed_two, root_two, upstream
        )
        grad_attn = (grad_own, swap(grad_own, 1))
        grad_mixed = call_window(
            unmix_kernel,
            [((micro, pairs, rows, PAIR), BF16)],
            "unmix",
            grad_attn,
            attention_w,
            columns,
            3,
        )
        down.second = tie(down.second, grad_mixed)
        grad_mixed = to_units(grad_mixed.reshape(units, rows, PAIR))
        grad_mixed = exchange(grad_mixed).reshape(tokens, PAIR)
        if repeats > 1:
            grad_mixed = lax.dynamic_slice_in_dim(grad_mixed, start[0], query_rows, 0)
        down.send(True)
        down.far = tie(down.far, down.second)
        down.hop_first()
        grad_mixed = tie(grad_mixed, down.sent, down.first)
        if ending:
            out = Gradient(
                functools.partial(mix_products, pairs, 0), columns, 0, "out", *grad_attn, mixed
            )
            out.start(True)
            grad_mixed = tie(grad_mixed, out.far)
        if late:
            late_attention.keep(True)
            grad_mixed = tie(grad_mixed, late_attention.kept)
            late_up.kept = tie(late_up.kept, down.sent)
            late_up.hop_kept()
            late_attention.kept = tie(late_attention.kept, grad_mixed)
            late_attention.hop_kept()
        down.sent, up.far = tie((down.sent, up.far), grad_mixed)
        down.hop_sent()
        up.hop_second()
        packed_grad = attend_back(
            start, qkv, grad_mixed, mixed_t, lse, key_frames, sequence_tables
        )
        packed_grad = tie(packed_grad, down.sent, up.second)
        if late:
            packed_grad = tie(packed_grad, late_attention.kept, late_up.kept)
            up_grads.append(late_up.kept)
            qkv_grads.append(late_attention.kept)
            out_grads.append(late_attention.kept)
        if layer + 1 == layers:
            last_parts = (middle, activated, down_w)
        if ending:
            outputs = final(*tie(last_parts, packed_grad))
        down.first, up.second, up.far = tie((down.first, up.second, up.far), packed_grad)
        packed_grad = from_units(exchange(packed_grad.reshape(tm_size, rows, 3 * PAIR)))
        down.keep(True)
        up.send(True)
        up.hop_first()
        packed_grad = tie(packed_grad, down.kept, up.sent, up.first)
        if ending:
            out.far = tie(out.far, down.first)
            out.hop_second()
            out.hop_first()
            down.hop_kept()
            packed_grad = tie(packed_grad, out.first, out.second, down.kept)
        if not ending:
            down.kept = tie(down.kept, packed_grad)
        up.sent = tie(up.sent, packed_grad)
        if ending:
            products = functools.partial(projection_products, pairs, range(3))
            group = Gradient(products, 3 * columns, 0, "qkv", *first_in, packed_grad)
            group.start()
            group.hop_second()
            group.hop_first()
            packed_grad = tie(packed_grad, group.far)
        theirs, mine = call(
            functools.partial(unproject_kernel, pairs),
            sums,
            "unproject",
            packed_grad,
            *attention_w,
        )
        total, come = sum_heads(theirs, mine)
        if not ending:
            down.hop_kept()
        up.hop_sent()
        down_grads.append(down.kept)
        if ending:
            out.second = tie(out.second, theirs)
            out.send()
            out.hop_sent()
            come = tie(come, group.second, up.sent, out.sent, outputs)
            group.second, up.sent, out.sent = tie((group.second, up.sent, out.sent), come)
            group.send()
            up.keep()
            out.keep()
            come = tie(come, group.sent, up.kept, out.kept)
            group.hop_sent()
            up.hop_kept()
            out.hop_kept()
        else:
            late_attention = Gradient(
                functools.partial(attention_products, pairs),
                4 * columns,
                0,
                "attention",
                *first_in,
                packed_grad,
                *grad_attn,
                mixed,
            )
            late_attention.sources = tie(late_attention.sources, total)
            late_attention.start_joined(True)
            late_attention.hop_joined()
            come = tie(come, down.kept, up.sent, late_attention.far)
        late_up = up
        upstream, grad_own, vector_sums[layer, 0] = norm_back(
            layer, 0, total, come, normed_one, root_one, upstream
        )
    restored = restore(offsets, shuffle, upstream)
    restored = (restored, swap(restored, 1))
    group.first = tie(group.first, restored, up.kept, out.kept)
    group.keep()
    vector_sums = tie(vector_sums, group.sent)
    names = [(layer, which) for layer in range(layers) for which in range(2)]
    small = jnp.concatenate(
        [vector_sums[name][kind : kind + 1] for kind in range(2) for name in names], axis=0
    )
    small = small + swap(small, 1)
    for bit in bits[::-1]:
        near, far = jnp.split(small, 2, axis=1)
        small = near + hop(far, bit)
    restored, done = tie(
        (restored, (up_grads, down_grads, out_grads, qkv_grads, up.kept, out.kept)), group.kept
    )
    up_grads, down_grads, out_grads, qkv_grads, up.kept, out.kept = done
    group.hop_kept()
    up_grads.append(up.kept)
    out_grads.append(out.kept)
    qkv_grads.append(group.kept)
    small = small.reshape(2, layers, 2, slices)
    return (
        outputs,
        all_rows(*restored),
        jnp.stack(
            [grad[:, : 3 * columns].reshape(slices, 3, columns) for grad in qkv_grads[::-1]]
        ),
        jnp.stack([grad[:, -columns:].T for grad in out_grads[::-1]]),
        jnp.stack(up_grads[::-1]),
        jnp.stack(down_grads[::-1]),
        small[0],
        small[1],
    )


def solution(mesh):
    placed = (
        P("tm", None, None),
        P(None, "tm", None, "head"),
        P(None, "head", "tm"),
        P(None, "tm", "head"),
        P(None, "head", "tm"),
        P(None, None, "tm"),
        P(None, None, "tm"),
        P("tm", None),
        P(None, "tm", None),
        P("tm", None, None),
    )
    return jax.shard_map(
        body,
        mesh=mesh,
        in_specs=placed,
        out_specs=(
            P("tm", None, None),
            P("tm", None, None),
            P(None, "tm", None, "head"),
            P(None, "head", "tm"),
            P(None, "tm", "head"),
            P(None, "head", "tm"),
            P(None, None, "tm"),
            P(None, None, "tm"),
        ),
        check_vma=False,
    )
```

```python
import functools

import jax
import jax.numpy as jnp
from jax import lax
from jax.experimental import pallas as pl
from jax.experimental.pallas import tpu as pltpu
from jax.sharding import PartitionSpec as P

HEAD_DIM = 64
PAIR = 2 * HEAD_DIM
GROUP = HEAD_DIM // 6
NEG_BIG = -1e30
F32 = jnp.float32
BF16 = jnp.bfloat16
NT = (((1,), (1,)), ((), ()))
TN = (((0,), (0,)), ((), ()))
NN = (((1,), (0,)), ((), ()))


def dot(left, right, dims):
    return lax.dot_general(left, right, dims, preferred_element_type=F32)


def rotary_tables(coordinates):
    lane = jnp.arange(PAIR, dtype=jnp.int32) % HEAD_DIM
    group = jnp.minimum(lane // (2 * GROUP), 2)
    place = lane % (2 * GROUP)
    turned = lane < 6 * GROUP
    first = turned & (place < GROUP)
    second = turned & (place >= GROUP)
    inverse = 10000.0 ** (-(place % GROUP).astype(F32) / GROUP)
    spread = jnp.where(
        group == 0,
        coordinates[:, 0:1],
        jnp.where(group == 1, coordinates[:, 1:2], coordinates[:, 2:3]),
    )
    angles = spread * inverse
    cosine = jnp.where(turned, jnp.cos(angles), 1.0)
    sine = jnp.sin(angles)
    return (cosine, jnp.where(first, -sine, 0.0), jnp.where(second, sine, 0.0))


def turn(values, cosine, sine_first, sine_second):
    ahead = pltpu.roll(values, PAIR - GROUP, 1)
    behind = pltpu.roll(values, GROUP, 1)
    return values * cosine + ahead * sine_first + behind * sine_second


def turn_back(values, cosine, sine_first, sine_second):
    ahead = pltpu.roll(values, PAIR - GROUP, 1)
    behind = pltpu.roll(values, GROUP, 1)
    return values * cosine - ahead * sine_first - behind * sine_second


def project_kernel(own, peer, left, right, cosine, sine_first, sine_second, out):
    rows = out.shape[2]
    width = out.shape[1] * PAIR
    middle = left.shape[0]
    for step, acts in enumerate((own, peer)):
        span = pl.ds(step * 2 * rows, 2 * rows)
        raw = dot(acts[:, :middle], left[:, : 3 * width], NN)
        raw += dot(acts[:, middle:], right[:, : 3 * width], NN)
        tables = (cosine[span, :], sine_first[span, :], sine_second[span, :])
        for pair in range(out.shape[1]):
            for part in range(3):
                start = part * width + pair * PAIR
                piece = raw[:, start : start + PAIR]
                if part < 2:
                    piece = turn(piece, *tables)
                piece = piece.astype(BF16)
                for half in range(2):
                    out[2 * step + half, pair, :, part * PAIR : (part + 1) * PAIR] = piece[
                        half * rows : (half + 1) * rows
                    ]


def unit_rows(tiles, micros, pairs, lanes):
    return jnp.concatenate(
        [
            jnp.concatenate([tiles[micro * pairs + pair, :, lanes] for pair in range(pairs)], axis=1)
            for micro in micros
        ],
        axis=0,
    )


def mix_kernel(pairs, mixed, left, right, theirs, mine):
    width = pairs * PAIR
    micro = mixed.shape[0] // pairs
    middle = left.shape[0]
    skip = left.shape[1] - width
    for micros, out in ((range(micro // 2, micro), theirs), (range(micro // 2), mine)):
        rows = unit_rows(mixed, micros, pairs, slice(0, PAIR))
        out[:, :middle] = dot(rows, left[:, skip:], NT).astype(out.dtype)
        out[:, middle:] = dot(rows, right[:, skip:], NT).astype(out.dtype)


def unmix_kernel(own, peer, left, right, out):
    rows = out.shape[2]
    width = out.shape[1] * PAIR
    middle = left.shape[0]
    skip = left.shape[1] - width
    for step, acts in enumerate((own, peer)):
        raw = dot(acts[:, :middle], left[:, skip:], NN) + dot(acts[:, middle:], right[:, skip:], NN)
        raw = raw.astype(BF16)
        for pair in range(out.shape[1]):
            for half in range(2):
                out[2 * step + half, pair] = raw[
                    half * rows : (half + 1) * rows, pair * PAIR : (pair + 1) * PAIR
                ]


def unproject_kernel(pairs, packed, left, right, theirs, mine):
    width = pairs * PAIR
    micro = packed.shape[0] // pairs
    middle = left.shape[0]
    for micros, out in ((range(micro // 2, micro), theirs), (range(micro // 2), mine)):
        for weights, place in ((left, slice(0, middle)), (right, slice(middle, 2 * middle))):
            total = 0.0
            for part in range(3):
                rows = unit_rows(packed, micros, pairs, slice(part * PAIR, (part + 1) * PAIR))
                total += dot(rows, weights[:, part * width : (part + 1) * width], NT)
            out[:, place] = total.astype(out.dtype)


def up_kernel(own, peer, left, right, activated, slope):
    middle = left.shape[0]
    half = own.shape[0]
    for start in range(0, activated.shape[1], 256):
        block = slice(start, start + 256)
        for step, acts in enumerate((own, peer)):
            upward = dot(acts[:, :middle], left[:, block], NN)
            upward += dot(acts[:, middle:], right[:, block], NN)
            bell = 0.5 * (1.0 + lax.erf(upward * 0.7071067811865476))
            span = slice(step * half, (step + 1) * half)
            activated[span, block] = (upward * bell).astype(BF16)
            slope[span, block] = (
                bell + upward * jnp.exp(-0.5 * upward * upward) * 0.3989422804014327
            )


def down_kernel(activated, left, right, theirs, mine):
    half = mine.shape[0]
    middle = left.shape[1]
    for span, out in ((slice(half, 2 * half), theirs), (slice(0, half), mine)):
        out[:, :middle] = dot(activated[span, :], left[...], NN).astype(out.dtype)
        out[:, middle:] = dot(activated[span, :], right[...], NN).astype(out.dtype)


def dense_back_kernel(own, peer, up_left, up_right, down_left, down_right, slope, inner, theirs, mine):
    half = mine.shape[0]
    middle = up_left.shape[0]
    for acts, span, out in (
        (peer, slice(half, 2 * half), theirs),
        (own, slice(0, half), mine),
    ):
        raw = dot(acts[:, :middle], down_left[...], NT)
        raw += dot(acts[:, middle:], down_right[...], NT)
        grad = (raw * slope[span, :]).astype(BF16)
        inner[span, :] = grad
        out[:, :middle] = dot(grad, up_left[...], NT).astype(out.dtype)
        out[:, middle:] = dot(grad, up_right[...], NT).astype(out.dtype)


def pair_kernel(mine, come, total):
    total[...] = (mine[...] + come[...].astype(F32)).astype(BF16)


def normalized(hidden, gain, bias):
    centered = hidden - jnp.mean(hidden, axis=-1, keepdims=True)
    root = lax.rsqrt(jnp.mean(centered * centered, axis=-1, keepdims=True) + 1e-06)
    normed = centered * root
    return normed, root, (normed * gain + bias).astype(BF16)


def first_norm_kernel(gain, bias, hidden, vectors, normed, root, out):
    normed[...], scale, out[...] = normalized(
        hidden[...], vectors[gain : gain + 1, :], vectors[bias : bias + 1, :]
    )
    root[...] = jnp.broadcast_to(scale, root.shape)


def norm_kernel(gain, bias, hidden, total, come, vectors, result, normed, root, out):
    value = hidden[...] + (total[...].astype(F32) + come[...].astype(F32))
    result[...] = value
    normed[...], scale, out[...] = normalized(
        value, vectors[gain : gain + 1, :], vectors[bias : bias + 1, :]
    )
    root[...] = jnp.broadcast_to(scale, root.shape)


def norm_back_kernel(gain, total, come, normed, root, vectors, upstream, result, out, sums):
    grad = total[...].astype(F32) + come[...].astype(F32)
    known = normed[...]
    sums[0:1, :] = jnp.sum(grad * known, axis=0, keepdims=True)
    sums[1:2, :] = jnp.sum(grad, axis=0, keepdims=True)
    scaled = grad * vectors[gain : gain + 1, :]
    value = upstream[...] + root[:, 0:1] * (
        scaled
        - jnp.mean(scaled, axis=-1, keepdims=True)
        - known * jnp.mean(scaled * known, axis=-1, keepdims=True)
    )
    result[...] = value
    out[...] = value.astype(BF16)


def quarter_of(own, peer, quarter):
    size = own.shape[1] // 4
    span = slice(quarter * size, (quarter + 1) * size)
    return jnp.concatenate([own[:, span], peer[:, span]], axis=0)


def up_products(quarter, own, peer, inner):
    rows = quarter_of(own, peer, quarter)
    for start in range(0, inner.shape[1], 256):
        span = slice(start, start + 256)
        yield (slice(None), span), dot(rows, inner[:, span], TN)


def down_products(quarter, own, peer, activated):
    rows = quarter_of(own, peer, quarter)
    for start in range(0, activated.shape[1], 256):
        span = slice(start, start + 256)
        yield (span, slice(None)), dot(activated[:, span], rows, TN)


def projection_products(pairs, parts, quarter, own, peer, packed):
    rows = quarter_of(own, peer, quarter)
    micros = range(packed.shape[0] // pairs)
    for place, part in enumerate(parts):
        other = unit_rows(packed, micros, pairs, slice(part * PAIR, (part + 1) * PAIR))
        span = slice(place * pairs * PAIR, (place + 1) * pairs * PAIR)
        yield (slice(None), span), dot(rows, other, TN)


def mix_products(pairs, start, quarter, own, peer, mixed):
    rows = quarter_of(own, peer, quarter)
    micros = range(mixed.shape[0] // pairs)
    other = unit_rows(mixed, micros, pairs, slice(0, PAIR))
    yield (slice(None), slice(start, start + pairs * PAIR)), dot(rows, other, TN)


def attention_products(pairs, quarter, own, peer, packed, grad_own, grad_peer, mixed):
    yield from projection_products(pairs, range(3), quarter, own, peer, packed)
    yield from mix_products(pairs, 3 * pairs * PAIR, quarter, grad_own, grad_peer, mixed)


def far_kernel(products, *refs):
    for quarter, out in ((2, refs[-2]), (3, refs[-1])):
        for place, value in products(quarter, *refs[:-2]):
            out[place] = value.astype(BF16)


def joined_kernel(products, *refs):
    out = refs[-1]
    size = out.shape[0] // 2
    for side, quarter in enumerate((2, 3)):
        for (rows, columns), value in products(quarter, *refs[:-1]):
            out[side * size : (side + 1) * size, columns] = value.astype(BF16)


def send_kernel(products, *refs):
    arrived, out = refs[-2:]
    if arrived.shape[0] == 2 * out.shape[0]:
        arrived = arrived.at[out.shape[0] :]
    for place, value in products(1, *refs[:-2]):
        out[place] = (value + arrived[place].astype(F32)).astype(BF16)


def keep_kernel(products, axis, *refs):
    arrived, folded, keep, send = refs[-4:]
    half = keep.shape[axis]
    if arrived.shape[0] == 2 * folded.shape[0]:
        arrived = arrived.at[: folded.shape[0]]
    for place, value in products(0, *refs[:-4]):
        value = value + arrived[place].astype(F32) + folded[place].astype(F32)
        if axis:
            keep[place] = value[:, :half]
            send[place] = value[:, half:].astype(BF16)
        else:
            keep[place] = value[:half]
            send[place] = value[half:].astype(BF16)


def lane_mask(shape, head):
    lane = lax.broadcasted_iota(jnp.int32, shape, 1)
    return (lane >= head * HEAD_DIM) & (lane < (head + 1) * HEAD_DIM)


def tagged(vectors, frames, head, value):
    lane = lax.broadcasted_iota(jnp.int32, vectors.shape, 1)
    first = (1 - head) * HEAD_DIM
    tags = value((lane - first).astype(F32), frames)
    return jnp.where(lane_mask(vectors.shape, head), vectors.astype(F32), tags).astype(BF16)


def key_tags(vectors, frames, head):
    return tagged(vectors, frames, head, lambda lane, frame: jnp.where(lane == frame, 1.0, 0.0))


def query_tags(vectors, frames, head):
    return tagged(vectors, frames, head, lambda lane, frame: jnp.where(lane > frame, NEG_BIG, 0.0))


def attend_kernel(block, start, qkv, key_frames, out, out_t, lse):
    frames = key_frames[...]
    keys = [key_tags(qkv[:, PAIR : 2 * PAIR], frames, head) for head in range(2)]
    value_t = jnp.transpose(qkv[:, 2 * PAIR :].astype(F32))
    ones = jnp.ones((16, value_t.shape[1]), F32)
    values = [
        jnp.concatenate([value_t[head * HEAD_DIM : (head + 1) * HEAD_DIM], ones], axis=0).astype(
            BF16
        )
        for head in range(2)
    ]
    query_rows = out.shape[0]

    def one(step, carry):
        place = pl.multiple_of(step * block, block)
        source = pl.multiple_of(start[0] + step * block, block)
        queries = qkv[pl.ds(source, block), :PAIR] * jnp.asarray(HEAD_DIM**-0.5, BF16)
        own_frames = key_frames[pl.ds(source, block), :]
        pieces = []
        for head in range(2):
            scores = dot(keys[head], query_tags(queries, own_frames, head), NT)
            top = jnp.max(scores, axis=0, keepdims=True)
            summed = dot(values[head], jnp.exp(scores - top).astype(BF16), NN)
            total = summed[HEAD_DIM : HEAD_DIM + 1]
            pieces.append(summed[:HEAD_DIM] / total)
            lse[head : head + 1, pl.ds(place, block)] = top + jnp.log(total)
        both = jnp.concatenate(pieces, axis=0)
        out_t[:, pl.ds(place, block)] = both
        out[pl.ds(place, block), :] = jnp.transpose(both).astype(BF16)
        return carry

    lax.fori_loop(0, query_rows // block, one, 0)


def attend_back_kernel(
    block,
    start,
    qkv,
    grad_out,
    out_t,
    lse,
    key_frames,
    cosine,
    sine_first,
    sine_second,
    result,
    key_sum,
    value_sum,
):
    key_vecs = qkv[:, PAIR : 2 * PAIR]
    frames = key_frames[...]
    keys = [key_tags(key_vecs, frames, head) for head in range(2)]
    value_vecs = qkv[:, 2 * PAIR :]
    key_t = jnp.transpose(key_vecs.astype(F32)).astype(BF16)
    query_rows = grad_out.shape[0]
    key_sum[...] = jnp.zeros_like(key_sum)
    value_sum[...] = jnp.zeros_like(value_sum)
    if query_rows != qkv.shape[0]:
        result[:, :PAIR] = jnp.zeros((qkv.shape[0], PAIR), BF16)

    def one(step, carry):
        place = pl.multiple_of(step * block, block)
        source = pl.multiple_of(start[0] + step * block, block)
        queries = qkv[pl.ds(source, block), :PAIR] * jnp.asarray(HEAD_DIM**-0.5, BF16)
        upstream = grad_out[pl.ds(place, block), :]
        own_frames = key_frames[pl.ds(source, block), :]
        both = out_t[:, pl.ds(place, block)] * jnp.transpose(upstream.astype(F32))
        pieces = []
        for head in range(2):
            keep = lane_mask(queries.shape, head)
            mine = jnp.where(keep, queries, jnp.zeros_like(queries))
            above = jnp.where(keep, upstream, jnp.zeros_like(upstream))
            rows = slice(head * HEAD_DIM, (head + 1) * HEAD_DIM)
            delta = jnp.sum(both[rows], axis=0, keepdims=True)
            log_total = lse[head : head + 1, pl.ds(place, block)]
            scores = dot(keys[head], query_tags(queries, own_frames, head), NT)
            weights = jnp.exp(scores - log_total)
            slope = (weights * (dot(value_vecs, above, NT) - delta)).astype(BF16)
            value_sum[...] += dot(weights.astype(BF16), above, NN)
            key_sum[...] += dot(slope, mine, NN)
            pieces.append(dot(key_t[rows], slope, NN))
        query_grad = jnp.transpose(jnp.concatenate(pieces, axis=0)) * HEAD_DIM**-0.5
        span = pl.ds(source, block)
        result[span, :PAIR] = turn_back(
            query_grad, cosine[span, :], sine_first[span, :], sine_second[span, :]
        ).astype(BF16)
        return carry

    lax.fori_loop(0, query_rows // block, one, 0)
    result[:, PAIR : 2 * PAIR] = turn_back(
        key_sum[...], cosine[...], sine_first[...], sine_second[...]
    ).astype(BF16)
    result[:, 2 * PAIR :] = value_sum[...].astype(BF16)


def whole():
    return pl.BlockSpec(memory_space=pltpu.VMEM)


def scalars():
    return pl.BlockSpec(memory_space=pltpu.SMEM)


def call(kernel, outs, name, *operands, numbers=(), scratch=(), scale=1, away=False):
    shapes = [(jax.ShapeDtypeStruct if away else pltpu.VMEM)(shape, kind) for shape, kind in outs]
    memory = pltpu.HBM if away else pltpu.VMEM
    operands = [pltpu.with_memory_space_constraint(operand, memory) for operand in operands]
    single = len(shapes) == 1
    return pl.pallas_call(
        kernel,
        out_shape=shapes[0] if single else shapes,
        in_specs=[scalars()] * len(numbers) + [whole()] * len(operands),
        out_specs=whole() if single else [whole()] * len(shapes),
        scratch_shapes=scratch,
        compiler_params=pltpu.CompilerParams(vmem_limit_bytes=scale * 10 * 1024 * 1024),
        name=name,
    )(*numbers, *operands)


def strip_kernel(*refs):
    pieces, (left, right, extras, vectors) = refs[:-4], refs[-4:]
    count = len(pieces)
    size = left.shape[0] // (count // 2)
    for place, piece in enumerate(pieces):
        out = (left, right)[place // (count // 2)]
        first = place % (count // 2) * size
        out[first : first + size, :] = piece[:size, :]
        extras[place] = piece[size:, :]
        extra = piece[size:, :].astype(F32)
        for row in range(vectors.shape[0]):
            start = row * size
            lanes = start % extra.shape[1]
            line = start // extra.shape[1]
            vectors[row : row + 1, place * size : (place + 1) * size] = extra[
                line : line + 1, lanes : lanes + size
            ]


def shard_kernel(qkv, out, result):
    width = qkv.shape[3]
    for part in range(3):
        result[:, part * width : (part + 1) * width] = qkv[0, :, part, :].astype(BF16)
    result[:, 3 * width :] = jnp.transpose(out[0]).astype(BF16)


def shard(layer, qkv_all, out_all):
    rows, width = qkv_all.shape[1], qkv_all.shape[3]
    return pl.pallas_call(
        shard_kernel,
        grid=(1,),
        out_shape=jax.ShapeDtypeStruct((rows, 4 * width), BF16),
        in_specs=[
            pl.BlockSpec((1,) + qkv_all.shape[1:], lambda i: (layer, 0, 0, 0)),
            pl.BlockSpec((1,) + out_all.shape[1:], lambda i: (layer, 0, 0)),
        ],
        out_specs=pl.BlockSpec((rows, 4 * width), lambda i: (0, 0)),
        compiler_params=pltpu.CompilerParams(vmem_limit_bytes=10 * 1024 * 1024),
        name="shard",
    )(qkv_all, out_all)


def call_window(kernel, outs, name, operands, weights, width, index):
    shapes = [jax.ShapeDtypeStruct(shape, kind) for shape, kind in outs]

    def full(shape):
        return pl.BlockSpec(shape, lambda i: (0,) * len(shape))

    single = len(shapes) == 1
    specs = [full(shape) for shape, kind in outs]
    return pl.pallas_call(
        kernel,
        grid=(1,),
        out_shape=shapes[0] if single else shapes,
        in_specs=[full(operand.shape) for operand in operands]
        + [pl.BlockSpec((part.shape[0], width), lambda i: (0, index)) for part in weights],
        out_specs=specs[0] if single else specs,
        compiler_params=pltpu.CompilerParams(vmem_limit_bytes=10 * 1024 * 1024),
        name=name,
    )(*operands, *weights)


def attend(start, qkv, key_frames, query_rows):
    return call(
        functools.partial(attend_kernel, 256),
        [((query_rows, PAIR), BF16), ((PAIR, query_rows), F32), ((2, query_rows), F32)],
        "attend",
        qkv,
        key_frames,
        numbers=(start,),
        scale=max(2, 2 * qkv.shape[0] // 1024),
        away=True,
    )


def attend_back(start, qkv, grad_out, out_t, lse, key_frames, tables):
    return call(
        functools.partial(attend_back_kernel, 256),
        [(qkv.shape, BF16)],
        "attend_back",
        qkv,
        grad_out,
        out_t,
        lse,
        key_frames,
        *tables,
        numbers=(start,),
        scratch=[pltpu.VMEM((qkv.shape[0], PAIR), F32)] * 2,
        scale=max(2, 2 * qkv.shape[0] // 1024),
        away=True,
    )


def restore_kernel(places, values, out):
    size = values.shape[1] // places.shape[0]
    for block in range(places.shape[0]):
        place = pl.multiple_of(places[block], size)
        out[:, pl.ds(place, size)] = values[:, block * size : (block + 1) * size]


def restore(places, shuffle, values):
    if values.shape[1] // places.shape[0] % 128 == 0:
        return call(restore_kernel, [(values.shape, values.dtype)], "restore", values, numbers=(places,))
    exact = lax.Precision.HIGHEST
    return lax.dot_general(
        values.astype(F32), shuffle.astype(F32), NT, precision=exact
    ).astype(values.dtype)


def body(
    inputs,
    qkv_master,
    out_master,
    up_master,
    down_master,
    norm_gain,
    norm_bias,
    frame_ids,
    patch_pos,
    cotangent,
):
    rows, micro, width = inputs.shape
    tm_size = lax.axis_size("tm")
    head_size = lax.axis_size("head")
    here = lax.axis_index("tm")
    layers = qkv_master.shape[0]
    columns = qkv_master.shape[3]
    hidden_units = up_master.shape[2]
    slices = width // tm_size
    half = micro // 2
    half_rows = half * rows
    odd = lax.axis_index("head") % 2
    pairs = columns // PAIR
    units = micro * pairs
    repeats = tm_size // units
    tokens = rows * tm_size
    query_rows = tokens // repeats

    bits = []
    order = [0]
    bit = tm_size // 2
    while bit:
        bits.append(bit)
        order = order + [place | bit for place in order]
        bit //= 2
    last = bits[-1]

    def sync(*values):
        return lax.optimization_barrier(values)

    def tie(value, *others):
        return sync(value, others)[0]

    def hop(values, bit):
        return lax.ppermute(values, "tm", [(i, i ^ bit) for i in range(tm_size)])

    def swap(values, bit):
        return lax.ppermute(values, "head", [(i, i ^ bit) for i in range(head_size)])

    half_shape = (half_rows, width)
    sums = [(half_shape, BF16), (half_shape, F32)]

    def sum_heads(theirs, mine):
        total = call(pair_kernel, [(half_shape, BF16)], "pair", mine, swap(theirs, 1))
        bit = 2
        while 2 * bit < head_size:
            total = sync((total.astype(F32) + swap(total, bit).astype(F32)).astype(BF16))[0]
            bit *= 2
        return total, swap(total, bit)

    def exchange(values):
        return lax.all_to_all(values, "tm", 0, 0, tiled=True)

    def grow(held, axis=0):
        return jnp.concatenate([held, hop(held, bits[0])], axis=axis)

    def reach(held, axis=0):
        pieces = [held]
        for bit in bits[1:-1]:
            so_far = jnp.concatenate(pieces, axis=axis) if len(pieces) > 1 else held
            pieces.append(hop(so_far, bit))
        return pieces

    def stack(pieces, axis=0):
        return jnp.concatenate(pieces, axis=axis)

    def fold(parts, axis=0):
        keep, send = parts
        for bit in bits[-3::-1]:
            total = keep + hop(send, bit).astype(F32)
            if bit == bits[0]:
                return total
            keep, send = jnp.split(total, 2, axis=axis)
            send = send.astype(BF16)

    def own_rows(values, shuffle):
        mine = lax.dynamic_slice_in_dim(values, half * odd, half, 1)
        mine = jnp.transpose(mine, (1, 0, 2)).reshape(half_rows, width)
        return dot(mine, shuffle, NN)

    def to_units(values):
        return jnp.repeat(values, repeats, axis=0) if repeats > 1 else values

    def from_units(values):
        if repeats == 1:
            return values
        grouped = values.reshape((units, repeats) + values.shape[1:]).astype(F32)
        return jnp.sum(grouped, axis=1).astype(BF16)

    def attention_shard(layer, qkv_all, out_all):
        if slices % 128 == 0:
            return shard(layer, qkv_all, out_all)
        return jnp.concatenate(
            [
                qkv_all[layer].astype(BF16).reshape(slices, 3 * columns),
                out_all[layer].astype(BF16).T,
            ],
            axis=1,
        )

    ordered = (jnp.arange(micro) + half * odd) % micro
    whole_numbers = jnp.concatenate([frame_ids[None], patch_pos], axis=0).astype(F32)
    whole_numbers = jnp.take(jnp.transpose(whole_numbers, (2, 0, 1)), ordered, axis=0)
    vectors = jnp.concatenate([norm_gain, norm_bias], axis=0)
    extra = jnp.concatenate([vectors.reshape(-1), whole_numbers.reshape(-1)]).astype(BF16)
    extra = jnp.pad(extra, (0, 8 * 4 * columns - extra.size)).reshape(8, 4 * columns)

    pieces = {
        0: jnp.concatenate([attention_shard(0, qkv_master, out_master), extra], axis=0)
    }
    for bit in bits:
        pieces[bit] = hop(pieces[0], bit)

    early = [pieces.pop(bit) for bit in bits[:-1]]
    masters = (qkv_master, out_master, up_master, down_master)
    early, inputs, whole_numbers, here, masters = sync(
        early, inputs, whole_numbers, here, masters
    )
    qkv_master, out_master, up_master, down_master = masters
    attention_held = [None] + [
        attention_shard(layer, qkv_master, out_master) for layer in range(1, layers)
    ]
    up_held = [up_master[layer].astype(BF16) for layer in range(layers)]
    down_held = [down_master[layer].astype(BF16) for layer in range(layers)]
    up, down = up_held[0], down_held[0]
    pieces.update(zip(bits[:-1], early))
    for bit in bits:
        for place in [place for place in order if place and place & (bit - 1) == 0]:
            if place & bit and place not in pieces:
                pieces[place] = hop(pieces[place ^ bit], bit)
    up = grow(up)
    down = grow(down, 1)
    feature = jnp.arange(width, dtype=jnp.int32)
    origin = (here ^ jnp.asarray(order, jnp.int32)[:, None]) * slices + jnp.arange(
        slices, dtype=jnp.int32
    )
    offsets = origin[:, 0]
    shuffle = (feature[:, None] == origin.reshape(1, width)).astype(BF16)
    row_tables = rotary_tables(jnp.transpose(whole_numbers, (0, 2, 1)).reshape(micro * rows, 3))
    start = ((here % repeats) * query_rows).reshape(1)

    hidden = own_rows(inputs, shuffle)
    root_shape = (half_rows, 128)
    norm_outs = [(half_shape, F32), (root_shape, F32), (half_shape, BF16)]

    def row_of(layer, which):
        return 2 * layer + which, 2 * layers + 2 * layer + which

    def norm(layer, which, hidden, total, come):
        return call(
            functools.partial(norm_kernel, *row_of(layer, which)),
            [(half_shape, F32)] + norm_outs,
            "norm",
            hidden,
            total,
            come,
            vectors,
        )

    hidden, attention_held[1:], row_tables = sync(hidden, attention_held[1:], row_tables)
    hidden, pieces, up, down = sync(hidden, pieces, up, down)
    if slices % 128 == 0:
        left, right, extras, vectors = call(
            strip_kernel,
            [((width // 2, 4 * columns), BF16)] * 2
            + [((tm_size, 8, 4 * columns), BF16), ((4 * layers, width), F32)],
            "strip",
            *[pieces[place] for place in order],
        )
        attention_w = (left, right)
        extras = extras.reshape(tm_size, -1)
    else:
        extras = jnp.stack([pieces[place][slices:].reshape(-1) for place in order])
        vectors = extras[:, : vectors.size].reshape(tm_size, 4 * layers, slices).astype(F32)
        vectors = jnp.transpose(vectors, (1, 0, 2)).reshape(4 * layers, width)
        attention_w = tuple(
            stack([pieces[place][:slices] for place in places_of])
            for places_of in (order[: tm_size // 2], order[tm_size // 2 :])
        )
    numbers = extras[:, 4 * layers * slices : 4 * layers * slices + 3 * rows * micro]
    numbers = lax.dynamic_index_in_dim(
        numbers.reshape(tm_size, micro, 3 * rows), here // (tm_size // micro), 1, keepdims=False
    )
    devices = jnp.arange(tm_size, dtype=jnp.int32)
    origins = (devices[:, None] == (here ^ jnp.asarray(order, jnp.int32))[None, :]).astype(BF16)
    places = dot(origins, numbers, NN).reshape(tm_size, 3, rows)
    places = jnp.transpose(places, (1, 0, 2)).reshape(3, tokens)
    normed_one, root_one, first_own = call(
        functools.partial(first_norm_kernel, *row_of(0, 0)), norm_outs, "first_norm", hidden, vectors
    )
    stored = []
    weights = []
    for layer in range(layers):
        more = layer + 1 < layers
        first_in = (first_own, swap(first_own, 1))
        first_in, attention_w = sync(first_in, attention_w)
        first_in, down = sync(first_in, down)
        up = tie(up, first_in)
        packed = call(
            project_kernel,
            [((micro, pairs, rows, 3 * PAIR), BF16)],
            "project",
            *first_in,
            *attention_w,
            *row_tables,
        )
        up, down = tie((up, down), packed)
        packed = to_units(packed.reshape(units, rows, 3 * PAIR))
        qkv = exchange(packed).reshape(tokens, 3 * PAIR)
        down_far = []
        if layer == 0:
            up = reach(up)
            sequence_tables = rotary_tables(places.T)
            key_frames = jnp.broadcast_to(places[0][:, None], (tokens, 128))
            qkv, sequence_tables, key_frames = sync(qkv, sequence_tables, key_frames)
        up_far = [hop(up[0], last)]
        qkv, up_far = sync(qkv, up_far)
        if layer == 0:
            down_far = [hop(down, last)]
        down = reach(down, 1)
        if layer:
            up_far = up_far + [hop(piece, last) for piece in tie(up[1:], qkv)]
        if more:
            coming = grow(tie(attention_held[layer + 1], packed))
        mixed, mixed_t, lse = attend(start, qkv, key_frames, query_rows)
        if repeats > 1:
            mixed = lax.dynamic_update_slice_in_dim(
                jnp.zeros((tokens, PAIR), BF16), mixed, start[0], 0
            )
        mixed, up_far, up, down_far = sync(mixed, up_far, up, down_far)
        if more:
            mixed, coming = sync(mixed, coming)
        mixed = from_units(exchange(mixed.reshape(tm_size, rows, PAIR)))
        if layer:
            down_far = [hop(down[0], last)]
        else:
            up_far = up_far + [hop(piece, last) for piece in up[1:]]
        mixed, up_far, down_far, down = sync(mixed, up_far, down_far, down)
        theirs, mine = call_window(
            functools.partial(mix_kernel, pairs), sums, "mix", (mixed,), attention_w, columns, 3
        )
        total, come = sum_heads(theirs, mine)
        down_far = down_far + [hop(piece, last) for piece in down[1:]]
        up_w = (stack(up), stack(up_far))
        if more:
            coming, next_up = tie((coming, up_held[layer + 1]), mixed)
            coming_far = [hop(coming, last)]
            coming = reach(coming)
            next_up = grow(next_up)
            come = tie(come, coming, next_up)
        come = tie(come, up_w)
        middle, normed_two, root_two, second_own = norm(layer, 1, hidden, total, come)
        second_in = (second_own, swap(second_own, 1))
        activated, slope = call(
            up_kernel,
            [((micro * rows, hidden_units), BF16), ((micro * rows, hidden_units), F32)],
            "up_project",
            *second_in,
            *up_w,
        )
        down_w = (stack(down, 1), stack(down_far, 1))
        activated = tie(activated, down_w)
        if more:
            theirs, mine = call(down_kernel, sums, "down_project", activated, *down_w)
            total, come = sum_heads(theirs, mine)
            coming_far = coming_far + [hop(piece, last) for piece in coming[1:]]
            next_up, next_down = tie((next_up, down_held[layer + 1]), second_in)
            next_up = reach(next_up)
            next_down = grow(next_down, 1)
            attention_next = (stack(coming), stack(coming_far))
            come = tie(come, next_up, next_down, coming_far[0])
        stored.append(
            (
                normed_one,
                root_one,
                first_in,
                qkv,
                mixed,
                mixed_t,
                lse,
                normed_two,
                root_two,
                second_in,
                activated,
                slope,
            )
        )
        weights.append((attention_w, up_w, down_w))
        if more:
            hidden, normed_one, root_one, first_own = norm(layer + 1, 0, middle, total, come)
            attention_w = attention_next
            up, down = next_up, next_down

    def all_rows(mine, other):
        ours = jnp.concatenate([mine, other], axis=0).reshape(micro, rows, width)
        return jnp.transpose(jnp.roll(ours, half * odd, axis=0), (1, 0, 2))

    def final(middle, activated, down_w):
        total, come = sum_heads(*call(down_kernel, sums, "down_project", activated, *down_w))
        result = middle + (total.astype(F32) + come.astype(F32))
        result = restore(offsets, shuffle, result.astype(BF16))
        return all_rows(result, swap(result, 1))

    class Gradient:
        def __init__(self, products, span, axis, name, *sources):
            self.products, self.axis, self.name, self.sources = products, axis, name, sources
            self.shape = (span, width // 4) if axis else (width // 4, span)
            self.ends = (span, width // 8) if axis else (width // 8, span)
            self.far = None

        def start(self, away=False):
            self.far = call(
                functools.partial(far_kernel, self.products),
                [(self.shape, BF16)] * 2,
                self.name + "_far",
                *self.sources,
                away=away,
            )

        def start_joined(self, away=False):
            span = self.shape[1]
            joined = call(
                functools.partial(joined_kernel, self.products),
                [((2 * self.shape[0], span), BF16)],
                self.name + "_far",
                *self.sources,
                away=away,
            )
            self.far = joined

        def hop_joined(self):
            self.first = self.second = hop(self.far, last)

        def hop_second(self):
            self.second = hop(self.far[1], last)

        def hop_first(self):
            self.first = hop(self.far[0], last)

        def send(self, away=False):
            self.sent = call(
                functools.partial(send_kernel, self.products),
                [(self.shape, BF16)],
                self.name + "_send",
                *self.sources,
                self.second,
                away=away,
            )

        def hop_sent(self):
            self.sent = hop(self.sent, bits[-2])

        def keep(self, away=False):
            self.kept = call(
                functools.partial(keep_kernel, self.products, self.axis),
                [(self.ends, F32), (self.ends, BF16)],
                self.name + "_keep",
                *self.sources,
                self.first,
                self.sent,
                away=away,
            )

        def hop_kept(self):
            self.kept = fold(self.kept, self.axis)

    upstream = own_rows(cotangent, shuffle)
    grad_own = upstream.astype(BF16)
    back_outs = [(half_shape, F32), (half_shape, BF16), ((2, width), F32)]

    def norm_back(layer, which, total, come, normed, root, upstream):
        return call(
            functools.partial(norm_back_kernel, row_of(layer, which)[0]),
            back_outs,
            "norm_back",
            total,
            come,
            normed,
            root,
            vectors,
            upstream,
        )

    vector_sums = {}
    up_grads, down_grads, qkv_grads, out_grads = [], [], [], []
    late_attention = late_up = None
    for layer in reversed(range(layers)):
        attention_w, up_w, down_w = weights[layer]
        (
            normed_one,
            root_one,
            first_in,
            qkv,
            mixed,
            mixed_t,
            lse,
            normed_two,
            root_two,
            second_in,
            activated,
            slope,
        ) = stored[layer]
        ending = layer == 0
        late = late_attention is not None
        grad_mlp = (grad_own, swap(grad_own, 1))
        down = Gradient(down_products, hidden_units, 1, "down", *grad_mlp, activated)
        down.start()
        down.hop_second()
        grad_mlp = tie(grad_mlp, down.far)
        inner, theirs, mine = call(
            dense_back_kernel,
            [((micro * rows, hidden_units), BF16)] + sums,
            "dense_back",
            *grad_mlp,
            *up_w,
            *down_w,
            slope,
        )
        if late:
            theirs = tie(theirs, late_attention.first)
        total, come = sum_heads(theirs, mine)
        up = Gradient(up_products, hidden_units, 0, "up", *second_in, inner)
        up.start()
        come = tie(come, up.far, down.second)
        if late:
            late_attention.send()
            late_attention.hop_sent()
            late_up.keep()
            come = tie(come, late_up.kept)
            come = tie(come, late_attention.sent)
        upstream, grad_own, vector_sums[layer, 1] = norm_back(
            layer, 1, total, come, normed_two, root_two, upstream
        )
        grad_attn = (grad_own, swap(grad_own, 1))
        grad_mixed = call_window(
            unmix_kernel,
            [((micro, pairs, rows, PAIR), BF16)],
            "unmix",
            grad_attn,
            attention_w,
            columns,
            3,
        )
        down.second = tie(down.second, grad_mixed)
        grad_mixed = to_units(grad_mixed.reshape(units, rows, PAIR))
        grad_mixed = exchange(grad_mixed).reshape(tokens, PAIR)
        if repeats > 1:
            grad_mixed = lax.dynamic_slice_in_dim(grad_mixed, start[0], query_rows, 0)
        down.send(True)
        down.far = tie(down.far, down.second)
        down.hop_first()
        grad_mixed = tie(grad_mixed, down.sent, down.first)
        if ending:
            out = Gradient(
                functools.partial(mix_products, pairs, 0), columns, 0, "out", *grad_attn, mixed
            )
            out.start(True)
            grad_mixed = tie(grad_mixed, out.far)
        if late:
            late_attention.keep(True)
            grad_mixed = tie(grad_mixed, late_attention.kept)
            late_up.kept = tie(late_up.kept, down.sent)
            late_up.hop_kept()
            late_attention.kept = tie(late_attention.kept, grad_mixed)
            late_attention.hop_kept()
        down.sent, up.far = tie((down.sent, up.far), grad_mixed)
        down.hop_sent()
        up.hop_second()
        packed_grad = attend_back(
            start, qkv, grad_mixed, mixed_t, lse, key_frames, sequence_tables
        )
        packed_grad = tie(packed_grad, down.sent, up.second)
        if late:
            packed_grad = tie(packed_grad, late_attention.kept, late_up.kept)
            up_grads.append(late_up.kept)
            qkv_grads.append(late_attention.kept)
            out_grads.append(late_attention.kept)
        if layer + 1 == layers:
            middle, last_in = tie((middle, activated), packed_grad)
            outputs = final(middle, last_in, down_w)
        down.first, up.second, up.far = tie((down.first, up.second, up.far), packed_grad)
        packed_grad = from_units(exchange(packed_grad.reshape(tm_size, rows, 3 * PAIR)))
        down.keep(True)
        up.send(True)
        up.hop_first()
        packed_grad = tie(packed_grad, down.kept, up.sent, up.first)
        if ending:
            out.far = tie(out.far, down.first)
            out.hop_second()
            out.hop_first()
            down.hop_kept()
            packed_grad = tie(packed_grad, out.first, out.second, outputs, down.kept)
        if not ending:
            down.kept = tie(down.kept, packed_grad)
        up.sent = tie(up.sent, packed_grad)
        if ending:
            products = functools.partial(projection_products, pairs, range(3))
            group = Gradient(products, 3 * columns, 0, "qkv", *first_in, packed_grad)
            group.start()
            group.hop_second()
            group.hop_first()
            packed_grad = tie(packed_grad, group.far)
        theirs, mine = call(
            functools.partial(unproject_kernel, pairs),
            sums,
            "unproject",
            packed_grad,
            *attention_w,
        )
        total, come = sum_heads(theirs, mine)
        if not ending:
            down.hop_kept()
        up.hop_sent()
        down_grads.append(down.kept)
        if ending:
            out.second = tie(out.second, theirs)
            out.send()
            out.hop_sent()
            come = tie(come, group.second, up.sent, out.sent)
            group.second, up.sent, out.sent = tie((group.second, up.sent, out.sent), come)
            group.send()
            up.keep()
            out.keep()
            come = tie(come, group.sent, up.kept, out.kept)
            group.hop_sent()
            up.hop_kept()
            out.hop_kept()
        else:
            late_attention = Gradient(
                functools.partial(attention_products, pairs),
                4 * columns,
                0,
                "attention",
                *first_in,
                packed_grad,
                *grad_attn,
                mixed,
            )
            late_attention.sources = tie(late_attention.sources, total)
            late_attention.start_joined(True)
            late_attention.hop_joined()
            come = tie(come, down.kept, up.sent, late_attention.far)
        late_up = up
        upstream, grad_own, vector_sums[layer, 0] = norm_back(
            layer, 0, total, come, normed_one, root_one, upstream
        )
    restored = restore(offsets, shuffle, upstream)
    restored = (restored, swap(restored, 1))
    group.first = tie(group.first, restored, up.kept, out.kept)
    group.keep()
    vector_sums = tie(vector_sums, group.sent)
    names = [(layer, which) for layer in range(layers) for which in range(2)]
    small = jnp.concatenate(
        [vector_sums[name][kind : kind + 1] for kind in range(2) for name in names], axis=0
    )
    small = small + swap(small, 1)
    for bit in bits[::-1]:
        near, far = jnp.split(small, 2, axis=1)
        small = near + hop(far, bit)
    restored, done = tie(
        (restored, (up_grads, down_grads, out_grads, qkv_grads, up.kept, out.kept)), group.kept
    )
    up_grads, down_grads, out_grads, qkv_grads, up.kept, out.kept = done
    group.hop_kept()
    up_grads.append(up.kept)
    out_grads.append(out.kept)
    qkv_grads.append(group.kept)
    small = small.reshape(2, layers, 2, slices)
    return (
        outputs,
        all_rows(*restored),
        jnp.stack(
            [grad[:, : 3 * columns].reshape(slices, 3, columns) for grad in qkv_grads[::-1]]
        ),
        jnp.stack([grad[:, -columns:].T for grad in out_grads[::-1]]),
        jnp.stack(up_grads[::-1]),
        jnp.stack(down_grads[::-1]),
        small[0],
        small[1],
    )


def solution(mesh):
    placed = (
        P("tm", None, None),
        P(None, "tm", None, "head"),
        P(None, "head", "tm"),
        P(None, "tm", "head"),
        P(None, "head", "tm"),
        P(None, None, "tm"),
        P(None, None, "tm"),
        P("tm", None),
        P(None, "tm", None),
        P("tm", None, None),
    )
    return jax.shard_map(
        body,
        mesh=mesh,
        in_specs=placed,
        out_specs=(
            P("tm", None, None),
            P("tm", None, None),
            P(None, "tm", None, "head"),
            P(None, "head", "tm"),
            P(None, "tm", "head"),
            P(None, "head", "tm"),
            P(None, None, "tm"),
            P(None, None, "tm"),
        ),
        check_vma=False,
    )
```
